32 devices in a mesh: gx: 4 (over y, x), gy: 4 (over z), gz: 2 (over core).
Axes of the slice: x: 2, y: 2, z: 4, core: 2. Of those that a mesh axis runs over, the one named last changes fastest.
Arguments:
- state: float32 [3, 32, 160, 512], P(None, 'gz', 'gy', 'gx'), may hold values from -6 to 6
- right_side: float32 [3, 32, 160, 512], P(None, 'gz', 'gy', 'gx'), may hold values from -6 to 6
- permeability: bfloat16 [32, 160, 512], P('gz', 'gy', 'gx'), may hold values from 0.099609375 to 10
- pore_volume: bfloat16 [32, 160, 512], P('gz', 'gy', 'gx'), may hold values from 0.019897461 to 0.19921875
- facies: int32 [32], P('gz'), may hold values from 0 to 3
- storage_table: float32 [4, 3, 3], replicated, may hold values from -0.3 to 2, as said below
- coupling_table: float32 [4, 3, 3], replicated, may hold values from -0.3 to 2, as said below
Outputs:
- new_state: float32 [3, 32, 160, 512], P(None, 'gz', 'gy', 'gx')
- correction: float32 [160, 512], P('gy', 'gx')
The draws below stay inside these ranges and needn't reach their ends.
Inputs may be any that keep to these rules, and one draw needn't show every extreme that they name: `storage_table`: each facies block has a diagonal of 1 to 2 and off-diagonal entries of magnitude at most 0.3. `coupling_table`: each facies block has a diagonal of 1 to 2 and off-diagonal entries of magnitude at most 0.3.
All inputs are finite; a program needn't handle non-finite values.
Results may differ from the reference program's by a relative error of at most 0.0003.
Values sent between devices are 32-bit elements; how exact they have to be, the bound alone decides.
A program may use at most 64 MiB of HBM per device.

```python
import math
import jax
import jax.numpy as jnp
from jax import lax

FACIES = 4
SWEEPS = 8
NX = 512
NY = 160
NZ = 32


def draw_table(key):
    first_key, second_key = jax.random.split(key)
    diagonal = jax.random.uniform(first_key, (FACIES, 3), jnp.float32, 1.0, 2.0)
    spread = jax.random.uniform(second_key, (FACIES, 3, 3), jnp.float32, -0.3, 0.3)
    identity = jnp.eye(3, dtype=jnp.float32)
    return spread * (1.0 - identity) + diagonal[:, :, None] * identity


def draw_storage_table(key, part):
    return draw_table(jax.random.fold_in(key, 11))


def draw_coupling_table(key, part):
    return draw_table(jax.random.fold_in(key, 12))


def plant(result, rng, least, top_value):
    longest = result.shape.index(max(result.shape))
    spots = []
    for shift in (0, 1):
        where = [jax.random.randint(jax.random.fold_in(rng, axis), (), 0, length) for axis, length in enumerate(result.shape)]
        where[longest] = (where[longest] + shift) % result.shape[longest]
        spots.append(tuple(where))
    return result.at[spots[0]].set(least).at[spots[1]].set(top_value)


def steps_of(rng, dims, cuts, low, largest):
    factor_of, own = 1.0, jax.random.fold_in(rng, 6)
    for dim, parts in cuts:
        heights = jnp.exp(jax.random.uniform(jax.random.fold_in(own, dim), (parts,), jnp.float32, low / len(cuts), largest / len(cuts)))
        factor_of = factor_of * jnp.repeat(heights, dims[dim] // parts).reshape([-1 if axis == dim else 1 for axis in range(len(dims))])
    return factor_of


def gaussian(rng, extent, width, limit, shards=(), held_as=jnp.bfloat16):
    gain = steps_of(rng, extent, shards, -0.22, 0.18) if shards else 1.0
    result = jax.random.normal(rng, extent, jnp.float32) * width * gain
    return jnp.minimum(jnp.maximum(result, -limit), limit).astype(held_as)


def setup_inputs(seed: int = 0) -> dict:
    arg_keys = jax.random.split(jax.random.key(seed), 8)
    state = gaussian(arg_keys[0], (3, NZ, NY, NX), 1.0, 6.0, ((1, 2), (2, 4), (3, 4)), jnp.float32)
    right_side = gaussian(arg_keys[1], (3, NZ, NY, NX), 1.0, 6.0, ((1, 2), (2, 4), (3, 4)), jnp.float32)
    permeability = jnp.clip(jnp.exp(math.log(10.0) - 4.609084 * jax.random.uniform(arg_keys[2], (NZ, NY, NX), jnp.float32) ** steps_of(arg_keys[2], (NZ, NY, NX), ((0, 2), (1, 4), (2, 4)), -0.2, 0.2)), 0.099609375, 10.0).astype(jnp.bfloat16)
    pore_volume = jnp.clip(jnp.exp(math.log(0.19921875) - 2.3038113 * jax.random.uniform(arg_keys[3], (NZ, NY, NX), jnp.float32) ** steps_of(arg_keys[3], (NZ, NY, NX), ((0, 2), (1, 4), (2, 4)), -0.2, 0.2)), 0.019897461, 0.19921875).astype(jnp.bfloat16)
    facies = plant(jax.random.randint(arg_keys[4], (NZ,), 0, FACIES), jax.random.fold_in(arg_keys[4], 1), 0, FACIES - 1).astype(jnp.int32)
    storage_table = draw_storage_table(jax.random.fold_in(arg_keys[7], 71), 0)
    coupling_table = draw_coupling_table(jax.random.fold_in(arg_keys[7], 71), 0)
    return dict(state=state, right_side=right_side, permeability=permeability, pore_volume=pore_volume, facies=facies, storage_table=storage_table, coupling_table=coupling_table)


relax = 0.8


def layer_tables(facies, table):
    onehot = (facies[:, None] == jnp.arange(table.shape[0])[None, :]).astype(jnp.float32)
    return jnp.dot(onehot, table.reshape(table.shape[0], 9), precision=lax.Precision.HIGHEST)


def layer_coefficient(rows, row_index, column_index):
    return rows[:, 3 * row_index + column_index][:, None, None]


def neighbours(padded):
    return [padded[..., 2:, 1:-1, 1:-1], padded[..., :-2, 1:-1, 1:-1],
            padded[..., 1:-1, 2:, 1:-1], padded[..., 1:-1, :-2, 1:-1],
            padded[..., 1:-1, 1:-1, 2:], padded[..., 1:-1, 1:-1, :-2]]


def face_weights(padded_perm):
    center = padded_perm[1:-1, 1:-1, 1:-1]
    return [2.0 * center * nearby / (center + nearby) for nearby in neighbours(padded_perm)]


def apply_operator(padded_state, weights, storage, storage_rows, coupling_rows):
    center = padded_state[:, 1:-1, 1:-1, 1:-1]
    fluxes = jnp.zeros_like(center)
    for weight, nearby in zip(weights, neighbours(padded_state)):
        fluxes = fluxes + weight[None] * (center - nearby)
    outputs = []
    for row_index in range(3):
        local = sum(layer_coefficient(storage_rows, row_index, k) * center[k] for k in range(3))
        moved = sum(layer_coefficient(coupling_rows, row_index, k) * fluxes[k] for k in range(3))
        outputs.append(storage * local + moved)
    return jnp.stack(outputs)


def coarse_planes(residual, weights, storage, storage_rows, coupling_rows):
    first_coupling = layer_coefficient(coupling_rows, 0, 0)
    first_storage = layer_coefficient(storage_rows, 0, 0)
    items = [residual[0], storage * first_storage] + [weights[k] * first_coupling for k in range(2, 6)]
    return jnp.stack([jnp.sum(item, axis=0) for item in items])


def jacobi(field, bordered, planes):
    diagonal = planes[1] + planes[2] + planes[3] + planes[4] + planes[5]
    nearby = (planes[2] * bordered[2:, 1:-1] + planes[3] * bordered[:-2, 1:-1]
              + planes[4] * bordered[1:-1, 2:] + planes[5] * bordered[1:-1, :-2])
    return field + relax * (planes[0] - diagonal * field + nearby) / diagonal


def block_solve(weights, storage, storage_rows, coupling_rows, residual):
    face_total = weights[0] + weights[1] + weights[2] + weights[3] + weights[4] + weights[5]
    entries = [[storage * layer_coefficient(storage_rows, r, c) + face_total * layer_coefficient(coupling_rows, r, c)
                for c in range(3)] for r in range(3)]

    def cofactor(r, c):
        return (entries[(r + 1) % 3][(c + 1) % 3] * entries[(r + 2) % 3][(c + 2) % 3]
                - entries[(r + 1) % 3][(c + 2) % 3] * entries[(r + 2) % 3][(c + 1) % 3])

    factors = [[cofactor(r, c) for c in range(3)] for r in range(3)]
    determinant = entries[0][0] * factors[0][0] + entries[0][1] * factors[0][1] + entries[0][2] * factors[0][2]
    return jnp.stack([(factors[0][r] * residual[0] + factors[1][r] * residual[1] + factors[2][r] * residual[2]) / determinant
                      for r in range(3)])


def reference(state, right_side, permeability, pore_volume, facies, storage_table, coupling_table):
    perm_wide = permeability.astype(jnp.float32)
    storage = pore_volume.astype(jnp.float32)
    storage_rows = layer_tables(facies, storage_table)
    coupling_rows = layer_tables(facies, coupling_table)
    weights = face_weights(jnp.pad(perm_wide, 1))
    widths = ((0, 0), (1, 1), (1, 1), (1, 1))
    residual = right_side - apply_operator(jnp.pad(state, widths), weights, storage, storage_rows, coupling_rows)
    planes = coarse_planes(residual, weights, storage, storage_rows, coupling_rows)
    correction = jnp.zeros(planes.shape[1:], jnp.float32)
    for repeat_index in range(SWEEPS):
        correction = jacobi(correction, jnp.pad(correction, 1), planes)
    state_one = state.at[0].add(correction[None])
    later_residual = right_side - apply_operator(jnp.pad(state_one, widths), weights, storage, storage_rows, coupling_rows)
    new_state = state_one + block_solve(weights, storage, storage_rows, coupling_rows, later_residual)
    return new_state, correction
```

```python
import functools
import jax
import jax.numpy as jnp
from jax import lax
from jax.experimental import pallas as pl
from jax.experimental.pallas import tpu as pltpu
from jax.sharding import PartitionSpec as P

SWEEPS = 8
RELAX = 0.8
MESH = pl.DeviceIdType.MESH
HALO = 8
VMEM_BYTES = 67043328

PLANES = 4
SIDES = [(-1, 0), (1, 0), (0, -1), (0, 1), (-1, -1), (-1, 1), (1, -1), (1, 1)]

KINV, NMAT, NADJ, NDIA, NTR, NC2, NDET, NCOEF = 0, 9, 18, 27, 30, 31, 32, 33


def cofactor(e, r, c):
    return (e[(r + 1) % 3][(c + 1) % 3] * e[(r + 2) % 3][(c + 2) % 3]
            - e[(r + 1) % 3][(c + 2) % 3] * e[(r + 2) % 3][(c + 1) % 3])


def block_scalars(m, k):
    kf = [[cofactor(k, r, c) for c in range(3)] for r in range(3)]
    inv = 1.0 / (k[0][0] * kf[0][0] + k[0][1] * kf[0][1] + k[0][2] * kf[0][2])
    kinv = [[kf[c][r] * inv for c in range(3)] for r in range(3)]
    n = [[kinv[r][0] * m[0][c] + kinv[r][1] * m[1][c] + kinv[r][2] * m[2][c] for c in range(3)] for r in range(3)]
    nf = [[cofactor(n, r, c) for c in range(3)] for r in range(3)]
    trace = n[0][0] + n[1][1] + n[2][2]
    return ([kinv[r][c] for r in range(3) for c in range(3)] + [n[r][c] for r in range(3) for c in range(3)]
            + [nf[c][r] for r in range(3) for c in range(3)] + [trace - n[i][i] for i in range(3)]
            + [trace, nf[0][0] + nf[1][1] + nf[2][2], n[0][0] * nf[0][0] + n[0][1] * nf[0][1] + n[0][2] * nf[0][2]])


def column_plan(nz, ny, nx):
    groups = ny // HALO
    per = nx // (2 * nz)
    return groups, per, -(-groups // per)


def strip_plan(ny, nx):
    groups = ny // HALO
    per = nx // (2 * HALO * PLANES)
    heads = [0] if groups == 1 else [0, groups - 1]
    others = list(range(1, groups - 1))
    packed = [[head] + [others.pop(0) for _ in range(per - 1) if others] for head in heads]
    while others:
        packed.append([others.pop(0) for _ in range(per) if others])
    return packed


def kernel(sizes, facies_hbm, mtab_hbm, ktab_hbm, state_hbm, rhs_hbm, perm_hbm, pore_hbm,
           w, qv, tzs, ty, txp, txm, final,
           u, pcb, rhs, permb, poreb, ysend, yrecv, xsend, xrecv, edge, rowk, tzf, shifted,
           zplanes, strips, cyrecv, cxrecv, cdrecv, field,
           facies, mtab, ktab, ctab, near_sem, far_sem, in_sem, h_send, h_recv, c_send, c_recv):
    ngx, ngy, ngz, nz, ny, nx = sizes
    ix, iy, iz = lax.axis_index("gx"), lax.axis_index("gy"), lax.axis_index("gz")
    own = slice(HALO, HALO + ny)
    groups, per, xtiles = column_plan(nz, ny, nx)
    packing = strip_plan(ny, nx)
    f32 = jnp.float32

    def exists(dy, dx):
        ok = None
        for d, i, n in ((dy, iy, ngy), (dx, ix, ngx)):
            if d:
                here = (i > 0) if d < 0 else (i < n - 1)
                ok = here if ok is None else jnp.logical_and(ok, here)
        return ok

    def at(dy, dx):
        return {"gx": ix + dx, "gy": iy + dy, "gz": iz}

    barrier = pltpu.get_barrier_semaphore()
    for side in SIDES[:4]:
        @pl.when(exists(*side))
        def _(side=side):
            pl.semaphore_signal(barrier, inc=1, device_id=at(*side), device_id_type=MESH)

    def signal_peers(sem):
        for d in range(1, ngz):
            pl.semaphore_signal(sem, inc=1, device_id={"gx": ix, "gy": iy, "gz": lax.rem(iz + d, ngz)},
                                device_id_type=MESH)

    signal_peers(barrier)

    loads = [
        pltpu.make_async_copy(perm_hbm, permb, in_sem.at[0]),
        pltpu.make_async_copy(state_hbm, u.at[0:3, 1:nz + 1, own], in_sem.at[1]),
        pltpu.make_async_copy(pore_hbm, poreb, in_sem.at[2]),
        pltpu.make_async_copy(rhs_hbm, rhs, in_sem.at[3]),
        pltpu.make_async_copy(facies_hbm, facies, in_sem.at[4]),
        pltpu.make_async_copy(mtab_hbm, mtab, in_sem.at[5]),
        pltpu.make_async_copy(ktab_hbm, ktab, in_sem.at[6]),
    ]
    for i in (4, 6, 5, 0, 1, 2, 3):
        loads[i].start()

    def zero(ref):
        ref[...] = jnp.zeros(ref.shape, ref.dtype)

    for cond, refs in (
        (iz == 0, [u.at[:, 0, own]]),
        (iz == ngz - 1, [u.at[:, nz + 1, own]]),
        (iy == 0, [yrecv.at[:, 0], cyrecv.at[0]]),
        (iy == ngy - 1, [yrecv.at[:, 1], cyrecv.at[1]]),
        (ix == 0, [xrecv.at[:, 0], cxrecv.at[0]]),
        (ix == ngx - 1, [xrecv.at[:, 1], cxrecv.at[1]]),
        (jnp.logical_or(iy == 0, ix == 0), [cdrecv.at[0]]),
        (jnp.logical_or(iy == 0, ix == ngx - 1), [cdrecv.at[1]]),
        (jnp.logical_or(iy == ngy - 1, ix == 0), [cdrecv.at[2]]),
        (jnp.logical_or(iy == ngy - 1, ix == ngx - 1), [cdrecv.at[3]]),
    ):
        @pl.when(cond)
        def _(refs=refs):
            for ref in refs:
                zero(ref)
    zero(field)
    for z in range(nz):
        zero(pcb.at[z, HALO + ny:])
    zero(shifted.at[:, 0:HALO])

    for i in (4, 6, 5):
        loads[i].wait()

    def coefficient(table, z, r, c):
        return table[r, facies[z], c]

    lane8 = lax.broadcasted_iota(jnp.int32, (HALO, nx), 1)
    row8 = lax.broadcasted_iota(jnp.int32, (HALO, nx), 0)
    pair8 = lax.shift_right_logical(lane8, 1)
    even8 = lax.rem(lane8, 2) == 0
    first8, last8 = lane8 == 0, lane8 == nx - 1
    nil8 = jnp.zeros((HALO, nx), f32)

    for f in range(ktab.shape[1]):
        values = block_scalars([[mtab[r, f, c] for c in range(3)] for r in range(3)],
                               [[ktab[r, f, c] for c in range(3)] for r in range(3)])
        for i, value in enumerate(values):
            ctab[i, f] = value
    layer_of_lane = lax.rem(lane8[0:1], 2 * nz) // 2
    lanek = [jnp.zeros((1, nx), f32) for _ in range(3)]
    for z in range(nz):
        for k in range(3):
            value = coefficient(ktab, z, 0, k)
            rowk[k, z:z + 1, :] = jnp.full((1, nx), value, f32)
            lanek[k] = jnp.where(layer_of_lane == z, value, lanek[k])

    def packed_columns(values):
        out = [nil8] * xtiles
        for z, g, x in values:
            place = (g % per) * nz + z
            out[g // per] = jnp.where(pair8 == place, pltpu.roll(x, 2 * place + 1, 1), out[g // per])
        return out

    def swapped(x):
        return jnp.where(even8, pltpu.roll(x, nx - 1, 1), pltpu.roll(x, 1, 1))

    loads[0].wait()
    values = []
    for z in range(nz):
        r = 0.5 / permb[z].astype(f32)
        u[3, z + 1, own, :] = r
        for side, at_row in ((0, 0), (1, ny - 1)):
            ysend[0, side, nz + z:nz + z + 1, :] = r[at_row:at_row + 1]
        values += [(z, g, r[g * HALO:(g + 1) * HALO]) for g in range(groups)]
    packed = packed_columns(values)
    for t in range(xtiles):
        xsend[0, 1, t] = packed[t]

    loads[1].wait()
    values = []
    for z in range(nz):
        k0 = [coefficient(ktab, z, 0, k) for k in range(3)]
        pc = k0[0] * u[0, z + 1, own, :] + k0[1] * u[1, z + 1, own, :] + k0[2] * u[2, z + 1, own, :]
        pcb[z, own, :] = pc
        for side, at_row in ((0, 0), (1, ny - 1)):
            ysend[0, side, z:z + 1, :] = pc[at_row:at_row + 1]
        values += [(z, g, pc[g * HALO:(g + 1) * HALO]) for g in range(groups)]
    packed = packed_columns(values)
    for t in range(xtiles):
        xsend[0, 0, t] = packed[t]

    beside_y = exists(-1, 0).astype(jnp.int32) + exists(1, 0).astype(jnp.int32)
    beside_x = exists(0, -1).astype(jnp.int32) + exists(0, 1).astype(jnp.int32)
    pl.semaphore_wait(barrier, beside_y + beside_x + (ngz - 1))

    def remote(src, dst, send, recv, device):
        return pltpu.make_async_remote_copy(src_ref=src, dst_ref=dst, send_sem=send, recv_sem=recv,
                                            device_id=device, device_id_type=MESH)

    def start(copies):
        for sends, copy in copies:
            @pl.when(sends)
            def _(copy=copy):
                copy.start()

    def y_copies(batch):
        s = h_send.at[2 + batch], h_recv.at[2 + batch]
        return [(exists(1, 0), remote(ysend.at[batch, 1], yrecv.at[batch, 0], *s, at(1, 0))),
                (exists(-1, 0), remote(ysend.at[batch, 0], yrecv.at[batch, 1], *s, at(-1, 0)))]

    def x_copies(batch):
        s = h_send.at[4 + batch], h_recv.at[4 + batch]
        return [(exists(0, 1), remote(xsend.at[batch], xrecv.at[batch, 0], *s, at(0, 1))),
                (exists(0, -1), remote(xsend.at[batch], xrecv.at[batch, 1], *s, at(0, -1)))]

    def z_device(d):
        return {"gx": ix, "gy": iy, "gz": iz + d}

    z_up = remote(u.at[:, nz, own], u.at[:, 0, own], h_send.at[0], h_recv.at[0], z_device(1))
    z_down = remote(u.at[:, 1, own], u.at[:, nz + 1, own], h_send.at[1], h_recv.at[1], z_device(-1))
    has_below, has_above = iz > 0, iz < ngz - 1

    start(x_copies(0))
    start(y_copies(0))
    start([(has_above, z_up), (has_below, z_down)])
    for side in SIDES[:4]:
        @pl.when(exists(*side))
        def _(side=side):
            pl.semaphore_signal(near_sem, inc=1, device_id=at(*side), device_id_type=MESH)
    signal_peers(near_sem)

    def counted(count, cases, descriptor, done):
        for n, ref in cases:
            @pl.when(count == n)
            def _(ref=ref):
                done(descriptor(ref))

    def wait_many(count, cases, send, recv, sent):
        counted(count, cases, lambda ref: remote(ref, ref, send, recv, z_device(0)),
                (lambda c: c.wait_send()) if sent else (lambda c: c.wait_recv()))

    def wait_y(batch, sent):
        wait_many(beside_y, ((1, yrecv.at[batch, 0]), (2, yrecv.at[batch])), h_send.at[2 + batch], h_recv.at[2 + batch], sent)

    def wait_x(batch, sent):
        wait_many(beside_x, ((1, xrecv.at[batch, 0]), (2, xrecv.at[batch])), h_send.at[4 + batch], h_recv.at[4 + batch], sent)

    for i in range(2):
        values = []
        for z in range(nz):
            c = u[1 + i, z + 1, own, :]
            for side, at_row in ((0, 0), (1, ny - 1)):
                ysend[1, side, i * nz + z:i * nz + z + 1, :] = c[at_row:at_row + 1]
            values += [(z, g, c[g * HALO:(g + 1) * HALO]) for g in range(groups)]
        packed = packed_columns(values)
        for t in range(xtiles):
            xsend[1, i, t] = packed[t]
    start(x_copies(1))
    start(y_copies(1))

    loads[2].wait()
    loads[3].wait()

    def tile_of(g):
        return slice(g * HALO, (g + 1) * HALO)

    def padded(g, shift):
        return slice(HALO + g * HALO + shift, HALO + (g + 1) * HALO + shift)

    def assemble(z, carry, upper=True):
        s_res, s_dia, s_ty, s_tx, s_hx, s_hy, s_z = (list(c) for c in carry)
        volume = poreb[z].astype(f32)
        k00 = coefficient(ktab, z, 0, 0)
        m0 = [coefficient(mtab, z, 0, k) for k in range(3)]
        if upper:
            dk = [coefficient(ktab, z, 0, k) - coefficient(ktab, z + 1, 0, k) for k in range(3)]
        for g in range(groups):
            rows = padded(g, 0)
            r = u[3, z + 1, rows, :]
            typ = 1.0 / (r + u[3, z + 1, padded(g, 1), :])
            if g == groups - 1:
                typ = jnp.where(row8 < HALO - 1, typ, 0.0)
            xp = jnp.where(last8, 0.0, 1.0 / (r + pltpu.roll(r, nx - 1, 1)))
            ty[z, rows, :] = typ
            txp[z, tile_of(g), :] = xp
            pc = pcb[z, rows, :]
            s_hx[g] = s_hx[g] + xp * (pc - pltpu.roll(pc, nx - 1, 1))
            s_hy[g] = s_hy[g] + typ * (pc - pcb[z, padded(g, 1), :])
            v = volume[tile_of(g)]
            c = [u[k, z + 1, rows, :] for k in range(3)]
            s_res[g] = s_res[g] + (rhs[0, z, tile_of(g), :] - v * (m0[0] * c[0] + m0[1] * c[1] + m0[2] * c[2]))
            s_dia[g] = s_dia[g] + v * m0[0]
            s_ty[g] = s_ty[g] + k00 * typ
            s_tx[g] = s_tx[g] + k00 * xp
            if upper:
                t = 1.0 / (r + u[3, z + 2, rows, :])
                tzf[z + 1, tile_of(g), :] = t
                d = [c[k] - u[k, z + 2, rows, :] for k in range(3)]
                s_z[g] = s_z[g] + t * (dk[0] * d[0] + dk[1] * d[1] + dk[2] * d[2])
        return tuple(tuple(s) for s in (s_res, s_dia, s_ty, s_tx, s_hx, s_hy, s_z))

    carry = ((nil8,) * groups,) * 7
    trips = (nz - 1) // 2

    def two(i, carry):
        return assemble(2 * i + 1, assemble(2 * i, carry))

    carry = lax.fori_loop(0, trips, two, carry)
    for z in range(2 * trips, nz):
        carry = assemble(z, carry, upper=z < nz - 1)
    s_res, s_dia, s_ty, s_tx, s_hx, s_hy, s_z = (list(c) for c in carry)

    for g in range(groups):
        shifted[0, padded(g, 0), :] = s_hy[g]
        shifted[1, padded(g, 0), :] = s_ty[g]
    p_rhs, p_dia = [], []
    for g in range(groups):
        p_rhs.append(s_res[g] - s_z[g] - (s_hx[g] - pltpu.roll(s_hx[g], 1, 1)) - (s_hy[g] - shifted[0, padded(g, -1), :]))
        p_dia.append(s_dia[g] + s_ty[g] + shifted[1, padded(g, -1), :] + s_tx[g] + pltpu.roll(s_tx[g], 1, 1))

    @pl.when(has_below)
    def _():
        z_up.wait_recv()

    @pl.when(has_above)
    def _():
        z_down.wait_recv()
    for slot, z, inside in ((0, 0, 1), (nz + 1, nz - 1, nz)):
        k0 = [coefficient(ktab, z, 0, k) for k in range(3)]
        for g in range(groups):
            rows = padded(g, 0)
            there = u[3, slot, rows, :]
            t = jnp.where(there > 0.0, 1.0 / (u[3, inside, rows, :] + there), 0.0)
            tzf[0 if slot == 0 else nz, tile_of(g), :] = t
            d = [u[k, inside, rows, :] - u[k, slot, rows, :] for k in range(3)]
            p_rhs[g] = p_rhs[g] - t * (k0[0] * d[0] + k0[1] * d[1] + k0[2] * d[2])
    mine = [[swapped(xsend[0, i, t]) for t in range(xtiles)] for i in range(2)]
    pl.semaphore_wait(near_sem, beside_y + beside_x + (ngz - 1))
    signal_peers(far_sem)

    wait_y(0, False)
    for side, at_row, g in ((0, 0, 0), (1, HALO - 1, groups - 1)):
        there = yrecv[0, side, nz:, :]
        t = jnp.where(there > 0.0, 1.0 / (ysend[0, side, nz:, :] + there), 0.0)
        for z in range(nz):
            edge_row = HALO - 1 + side * ny
            ty[z, edge_row:edge_row + 1, :] = t[z:z + 1]
        moved = jnp.sum(t * (ysend[0, side, :nz, :] - yrecv[0, side, :nz, :]), axis=0, keepdims=True)
        weight = jnp.sum(rowk[0] * t, axis=0, keepdims=True)
        here = row8 == at_row
        p_rhs[g] = p_rhs[g] - jnp.where(here, moved, 0.0)
        p_dia[g] = p_dia[g] + jnp.where(here, weight, 0.0)
        if side:
            s_ty[g] = s_ty[g] + jnp.where(here, weight, 0.0)
    planes = [p_rhs, p_dia, s_ty, s_tx]
    group8 = lax.shift_right_logical(lane8, 4)
    packed = []
    for tiles in packing:
        strip = nil8
        for i, g in enumerate(tiles):
            for p in range(PLANES):
                slot = i * PLANES + p
                strip = jnp.where(group8 == slot, pltpu.roll(planes[p][g], (2 * HALO * slot + HALO) % nx, 1), strip)
        packed.append(strip)

    wait_x(0, False)
    flux, weights, faces, outside = [], [], [], []
    for t in range(xtiles):
        there = [jnp.where(even8, xrecv[0, 0, i, t], xrecv[0, 1, i, t]) for i in range(2)]
        face = jnp.where(there[1] > 0.0, 1.0 / (mine[1][t] + there[1]), 0.0)
        flux.append(face * (mine[0][t] - there[0]))
        weights.append(face * lanek[0])
        faces.append(face)
        outside.append(there[0])
    in16 = lax.rem(lane8, 2 * HALO)
    for i, tiles in enumerate(packing):
        for j, g in enumerate(tiles):
            low = (g % per) * 2 * nz
            block = jnp.logical_and(lane8 >= low, lane8 < low + 2 * nz)
            sums = []
            for values in (flux, weights):
                for parity in (even8, jnp.logical_not(even8)):
                    chosen = jnp.where(jnp.logical_and(block, parity), values[g // per], 0.0)
                    sums.append(jnp.sum(chosen, axis=1, keepdims=True))
            for p, left, right, sign in ((0, sums[0], sums[1], -1.0), (1, sums[2], sums[3], 1.0), (3, None, sums[3], 1.0)):
                slot = (j * PLANES + p) * 2 * HALO
                at_left, at_right = lane8 == slot + HALO, lane8 == slot + HALO - 1
                change = jnp.where(last8, sign * right, 0.0)
                moved = jnp.where(at_right, sign * right, 0.0)
                if left is not None:
                    change = jnp.where(first8, sign * left, change)
                    moved = jnp.where(at_left, sign * left, moved)
                planes[p][g] = planes[p][g] + change
                packed[i] = packed[i] + moved
    for i in range(len(packing)):
        strips[i] = packed[i]
    for p in range(PLANES):
        for g in range(groups):
            zplanes[iz, p, tile_of(g), :] = planes[p][g]

    pl.semaphore_wait(far_sem, ngz - 1)
    copies = []
    for n, (dy, dx) in enumerate(SIDES[4:]):
        into = (1 - dy) + (1 - dx) // 2
        src = strips.at[0 if dy < 0 or len(packing) == 1 else 1]
        for d in range(ngz):
            device = {"gx": ix + dx, "gy": iy + dy, "gz": lax.rem(iz + d, ngz)}
            copies.append((exists(dy, dx), remote(src, cdrecv.at[into, iz], c_send.at[3], c_recv.at[3], device)))
    for dx in (-1, 1):
        for d in range(ngz):
            device = {"gx": ix + dx, "gy": iy, "gz": lax.rem(iz + d, ngz)}
            copies.append((exists(0, dx), remote(strips, cxrecv.at[(1 - dx) // 2, iz], c_send.at[2], c_recv.at[2], device)))
    for dy in (-1, 1):
        src = zplanes.at[iz, :, 0:HALO] if dy < 0 else zplanes.at[iz, :, ny - HALO:ny]
        for d in range(ngz):
            device = {"gx": ix, "gy": iy + dy, "gz": lax.rem(iz + d, ngz)}
            copies.append((exists(dy, 0), remote(src, cyrecv.at[(1 - dy) // 2, iz], c_send.at[1], c_recv.at[1], device)))
    start(copies)
    for d in range(1, ngz):
        remote(zplanes.at[iz], zplanes.at[iz], c_send.at[0], c_recv.at[0],
               {"gx": ix, "gy": iy, "gz": lax.rem(iz + d, ngz)}).start()

    wait_y(1, False)
    wait_x(1, False)
    invrow = 1.0 / rowk[0]
    for side, at_row in ((0, HALO - 1), (1, HALO + ny)):
        one, two_ = yrecv[1, side, :nz, :], yrecv[1, side, nz:, :]
        zero_ = (yrecv[0, side, :nz, :] - rowk[1] * one - rowk[2] * two_) * invrow
        for z in range(nz):
            for k, x in enumerate((zero_, one, two_)):
                u[k, z + 1, at_row:at_row + 1, :] = x[z:z + 1]
    invlane = 1.0 / lanek[0]
    for t in range(xtiles):
        one, two_ = (jnp.where(even8, xrecv[1, 0, i, t], xrecv[1, 1, i, t]) for i in range(2))
        zero_ = (outside[t] - lanek[1] * one - lanek[2] * two_) * invlane
        for k, x in enumerate((zero_, one, two_)):
            edge[k, t] = swapped(faces[t] * x)
        edge[3, t] = swapped(faces[t])

    outer8 = jnp.logical_or(first8, last8)

    def solve(z, _):
        volume = poreb[z].astype(f32)
        f = facies[z]
        kinv = [[ctab[KINV + 3 * r + c, f] for c in range(3)] for r in range(3)]
        n = [[ctab[NMAT + 3 * r + c, f] for c in range(3)] for r in range(3)]
        adj = [[ctab[NADJ + 3 * r + c, f] for c in range(3)] for r in range(3)]
        dia = [ctab[NDIA + i, f] for i in range(3)]
        trace, minors, det_n = ctab[NTR, f], ctab[NC2, f], ctab[NDET, f]
        for g in range(groups):
            rows = padded(g, 0)
            tile = tile_of(g)
            shift = lax.rem(2 * nx - (2 * nz * (g % per) + 1) - 2 * z, nx)
            lateral = [jnp.where(outer8, pltpu.roll(edge[k, g // per], shift, 1), 0.0) for k in range(4)]
            tzm, tzp = tzf[z, tile, :], tzf[z + 1, tile, :]
            typ, tym = ty[z, rows, :], ty[z, padded(g, -1), :]
            xp = txp[z, tile, :]
            xm = pltpu.roll(xp, 1, 1)
            tz = tzm + tzp
            tzs[z, tile, :] = tz
            total = tz + (typ + tym) + (xp + xm) + lateral[3]
            txp[z, tile, :] = xp + jnp.where(last8, lateral[3], 0.0)
            txm[z, tile, :] = xm + jnp.where(first8, lateral[3], 0.0)
            near = []
            for k in range(3):
                c = u[k, z + 1, rows, :]
                near.append(tzp * u[k, z + 2, rows, :] + tzm * u[k, z, rows, :]
                            + typ * u[k, z + 1, padded(g, 1), :] + tym * u[k, z + 1, padded(g, -1), :]
                            + xp * pltpu.roll(c, nx - 1, 1) + xm * pltpu.roll(c, 1, 1) + lateral[k])
            given = [rhs[k, z, tile, :] for k in range(3)]
            b = [near[r] + kinv[r][0] * given[0] + kinv[r][1] * given[1] + kinv[r][2] * given[2] for r in range(3)]
            v = volume[tile]
            s = total * (1.0 / v)
            e = [[s * (s + dia[r]) + adj[r][r] if r == c else adj[r][c] - s * n[r][c] for c in range(3)] for r in range(3)]
            det = ((s + trace) * s + minors) * s + det_n
            inv = 1.0 / (v * det)
            for r in range(3):
                w[r, z, tile, :] = (e[r][0] * b[0] + e[r][1] * b[1] + e[r][2] * b[2]) * inv
                qv[r, z, tile, :] = e[r][0] * inv
        return 0

    def solve_two(i, carry):
        return solve(2 * i + 1, solve(2 * i, carry))

    lax.fori_loop(0, nz // 2, solve_two, 0)
    if nz % 2:
        solve(nz - 1, 0)

    corners = beside_y * beside_x
    if ngz > 1:
        others = zplanes.at[0:ngz - 1]
        remote(others, others, c_send.at[0], c_recv.at[0], z_device(0)).wait_recv()
    y_cases = ((1, cyrecv.at[0]), (2, cyrecv))
    x_cases = ((1, cxrecv.at[0]), (2, cxrecv))
    d_cases = ((1, cdrecv.at[0]), (2, cdrecv.at[0:2]), (4, cdrecv))
    wait_many(beside_y, y_cases, c_send.at[1], c_recv.at[1], False)
    wait_many(beside_x, x_cases, c_send.at[2], c_recv.at[2], False)
    wait_many(corners, d_cases, c_send.at[3], c_recv.at[3], False)

    def gathered(ref, *index):
        total = ref[index[0], 0] if not index[1:] else ref[(index[0], 0) + index[1:]]
        for i in range(1, ngz):
            total = total + (ref[index[0], i] if not index[1:] else ref[(index[0], i) + index[1:]])
        return total

    rows = ny + 2 * HALO
    elane = lax.broadcasted_iota(jnp.int32, (rows, nx), 1)
    efirst, elast = elane == 0, elane == nx - 1
    left_part = in16 < HALO
    side_tiles = [jnp.where(left_part, gathered(cxrecv, 0, i), gathered(cxrecv, 1, i)) for i in range(len(packing))]
    corner_tiles = [jnp.where(left_part, gathered(cdrecv, 2 * v), gathered(cdrecv, 2 * v + 1)) for v in range(2)]
    where_is = {g: (i, j) for i, tiles in enumerate(packing) for j, g in enumerate(tiles)}
    strip8 = jnp.logical_or(lane8 < HALO, lane8 >= nx - HALO)

    def border_of(p, g):
        if 0 <= g < groups:
            i, j = where_is[g]
            tile, slot = side_tiles[i], j * PLANES + p
        else:
            tile, slot = corner_tiles[0 if g < 0 else 1], p
        return jnp.where(strip8, pltpu.roll(tile, (2 * nx - 2 * HALO * slot - HALO) % nx, 1), 0.0)

    b = [jnp.concatenate([border_of(p, g) for g in range(-1, groups + 1)], axis=0) for p in range(PLANES)]
    a = []
    for p in range(PLANES):
        plane = zplanes[0, p]
        for i in range(1, ngz):
            plane = plane + zplanes[i, p]
        a.append(jnp.concatenate([gathered(cyrecv, 0, p), plane, gathered(cyrecv, 1, p)], axis=0))

    def east(a, b):
        ra, rb = pltpu.roll(a, nx - 1, 1), pltpu.roll(b, nx - 1, 1)
        return jnp.where(elast, rb, ra), jnp.where(elast, ra, rb)

    def west(a, b):
        ra, rb = pltpu.roll(a, 1, 1), pltpu.roll(b, 1, 1)
        return jnp.where(efirst, rb, ra), jnp.where(efirst, ra, rb)

    mid = slice(HALO, HALO + rows)
    wests = west(a[3], b[3])
    terms = []
    for s, planes_ in enumerate((a, b)):
        there = planes_[1] > 0.0
        inv = jnp.where(there, RELAX / jnp.where(there, planes_[1], 1.0), 0.0)
        field[s, mid, :] = planes_[2]
        south = field[s, HALO - 1:HALO - 1 + rows, :]
        terms.append((planes_[0] * inv, planes_[2] * inv, south * inv, planes_[3] * inv, wests[s] * inv))

    c = [terms[0][0], terms[1][0]]
    for sweep in range(1, SWEEPS):
        e, ws = east(*c), west(*c)
        for s in range(2):
            field[s, mid, :] = c[s]
        nxt = []
        for s in range(2):
            r, tyn, tys, txe, txw = terms[s]
            nxt.append((1.0 - RELAX) * c[s] + r
                       + tyn * field[s, HALO + 1:HALO + 1 + rows, :] + tys * field[s, HALO - 1:HALO - 1 + rows, :]
                       + txe * e[s] + txw * ws[s])
        c = nxt
    e, ws = east(*c), west(*c)
    final[0] = c[0]
    final[1] = e[0]
    final[2] = ws[0]
    @pl.when(has_above)
    def _():
        z_up.wait_send()

    @pl.when(has_below)
    def _():
        z_down.wait_send()
    for batch in range(2):
        wait_y(batch, True)
        wait_x(batch, True)
    if ngz > 1:
        remote(others, others, c_send.at[0], c_recv.at[0], z_device(0)).wait_send()
    wait_many(beside_y, y_cases, c_send.at[1], c_recv.at[1], True)
    wait_many(beside_x, x_cases, c_send.at[2], c_recv.at[2], True)
    wait_many(corners, d_cases, c_send.at[3], c_recv.at[3], True)


def finish_kernel(parts, w, qv, tzs, ty, txp, txm, final, new_hbm, corr_hbm, out, out_sem):
    nz, ny, nx = tzs.shape
    own = slice(HALO, HALO + ny)
    corr = pltpu.make_async_copy(final.at[0, own], corr_hbm, out_sem.at[parts])
    corr.start()
    cc, ce, cw = (final[k, own, :] for k in range(3))
    cn, cs = final[0, HALO + 1:HALO + 1 + ny, :], final[0, HALO - 1:HALO - 1 + ny, :]

    def finish(z, _):
        g = (tzs[z] * cc + ty[z, own, :] * cn + ty[z, HALO - 1:HALO + ny - 1, :] * cs
             + txp[z] * ce + txm[z] * cw)
        for r in range(3):
            out[r, z] = w[r, z] + qv[r, z] * g
        return 0

    step = nz // parts
    outs = [corr]
    for part in range(parts):
        lax.fori_loop(part * step, (part + 1) * step, finish, 0)
        chunk = slice(part * step, (part + 1) * step)
        outs.append(pltpu.make_async_copy(out.at[:, chunk], new_hbm.at[:, chunk], out_sem.at[part]))
        outs[-1].start()
    for copy in outs:
        copy.wait()


def per_device(sizes, state, right_side, permeability, pore_volume, facies, storage_table, coupling_table):
    _, nz, ny, nx = state.shape
    sizes = sizes + (nz, ny, nx)
    f32 = jnp.float32
    ngz = sizes[2]
    cells = (nz, ny, nx)
    vmem = lambda *shape: pltpu.VMEM(shape, f32)
    hbm = pl.BlockSpec(memory_space=pltpu.HBM)
    dma = lambda n: pltpu.SemaphoreType.DMA((n,))
    ey = ny + 2 * HALO
    groups, per, xtiles = column_plan(nz, ny, nx)
    strips = len(strip_plan(ny, nx))
    facets = storage_table.shape[0]
    in_vmem = pl.BlockSpec(memory_space=pltpu.VMEM)
    handed = 4 * nx * (9 * nz * ny + nz * ey + 3 * ey)
    limit = 16384 * ((VMEM_BYTES - handed) // 16384)
    middle = pl.pallas_call(
        functools.partial(kernel, sizes),
        out_shape=(vmem(3, *cells), vmem(3, *cells), vmem(*cells), vmem(nz, ey, nx), vmem(*cells), vmem(*cells),
                   vmem(3, ey, nx)),
        in_specs=[hbm, hbm, hbm, hbm, hbm, hbm, hbm],
        out_specs=(in_vmem,) * 7,
        scratch_shapes=[
            vmem(4, nz + 2, ey, nx), vmem(nz, ey, nx), vmem(3, *cells),
            pltpu.VMEM(cells, permeability.dtype), pltpu.VMEM(cells, pore_volume.dtype),
            vmem(2, 2, 2 * nz, nx), vmem(2, 2, 2 * nz, nx),
            vmem(2, 2, xtiles, HALO, nx), vmem(2, 2, 2, xtiles, HALO, nx), vmem(4, xtiles, HALO, nx),
            vmem(3, nz, nx), vmem(nz + 1, ny, nx), vmem(2, ey, nx),
            vmem(ngz, PLANES, ny, nx), vmem(strips, HALO, nx),
            vmem(2, ngz, PLANES, HALO, nx), vmem(2, ngz, strips, HALO, nx), vmem(4, ngz, HALO, nx),
            vmem(2, ey + 2 * HALO, nx),
            pltpu.SMEM((nz,), facies.dtype), pltpu.SMEM((3, facets, 3), f32), pltpu.SMEM((3, facets, 3), f32),
            pltpu.SMEM((NCOEF, facets), f32),
            pltpu.SemaphoreType.REGULAR, pltpu.SemaphoreType.REGULAR, dma(7), dma(6), dma(6), dma(4), dma(4),
        ],
        compiler_params=pltpu.CompilerParams(collective_id=0, has_side_effects=True, vmem_limit_bytes=limit),
        name="cpr_apply",
    )(facies, storage_table.transpose(1, 0, 2), coupling_table.transpose(1, 0, 2),
      state, right_side, permeability, pore_volume)
    parts = 8 if nz % 8 == 0 else 1
    return tuple(pl.pallas_call(
        functools.partial(finish_kernel, parts),
        out_shape=(jax.ShapeDtypeStruct(state.shape, f32), jax.ShapeDtypeStruct((ny, nx), f32)),
        in_specs=[in_vmem] * 7,
        out_specs=(hbm, hbm),
        scratch_shapes=[vmem(3, *cells), dma(parts + 1)],
        compiler_params=pltpu.CompilerParams(vmem_limit_bytes=16 * 2**20),
        name="cpr_finish",
    )(*middle))


def solution(mesh):
    sizes = (mesh.shape["gx"], mesh.shape["gy"], mesh.shape["gz"])
    return jax.shard_map(
        functools.partial(per_device, sizes),
        mesh=mesh,
        in_specs=(
            P(None, "gz", "gy", "gx"),
            P(None, "gz", "gy", "gx"),
            P("gz", "gy", "gx"),
            P("gz", "gy", "gx"),
            P("gz"),
            P(),
            P(),
        ),
        out_specs=(P(None, "gz", "gy", "gx"), P("gy", "gx")),
        check_vma=False,
    )
```

```python
import functools
import jax
import jax.numpy as jnp
from jax import lax
from jax.experimental import pallas as pl
from jax.experimental.pallas import tpu as pltpu
from jax.sharding import PartitionSpec as P

SWEEPS = 8
RELAX = 0.8
MESH = pl.DeviceIdType.MESH
HALO = 8
VMEM_BYTES = 67043328

PLANES = 4
SIDES = [(-1, 0), (1, 0), (0, -1), (0, 1), (-1, -1), (-1, 1), (1, -1), (1, 1)]

KINV, NMAT, NADJ, NDIA, NTR, NC2, NDET, NCOEF = 0, 9, 18, 27, 30, 31, 32, 33


def cofactor(e, r, c):
    return (e[(r + 1) % 3][(c + 1) % 3] * e[(r + 2) % 3][(c + 2) % 3]
            - e[(r + 1) % 3][(c + 2) % 3] * e[(r + 2) % 3][(c + 1) % 3])


def block_scalars(m, k):
    kf = [[cofactor(k, r, c) for c in range(3)] for r in range(3)]
    inv = 1.0 / (k[0][0] * kf[0][0] + k[0][1] * kf[0][1] + k[0][2] * kf[0][2])
    kinv = [[kf[c][r] * inv for c in range(3)] for r in range(3)]
    n = [[kinv[r][0] * m[0][c] + kinv[r][1] * m[1][c] + kinv[r][2] * m[2][c] for c in range(3)] for r in range(3)]
    nf = [[cofactor(n, r, c) for c in range(3)] for r in range(3)]
    trace = n[0][0] + n[1][1] + n[2][2]
    return ([kinv[r][c] for r in range(3) for c in range(3)] + [n[r][c] for r in range(3) for c in range(3)]
            + [nf[c][r] for r in range(3) for c in range(3)] + [trace - n[i][i] for i in range(3)]
            + [trace, nf[0][0] + nf[1][1] + nf[2][2], n[0][0] * nf[0][0] + n[0][1] * nf[0][1] + n[0][2] * nf[0][2]])


def column_plan(nz, ny, nx):
    groups = ny // HALO
    per = nx // (2 * nz)
    return groups, per, -(-groups // per)


def strip_plan(ny, nx):
    groups = ny // HALO
    per = nx // (2 * HALO * PLANES)
    heads = [0] if groups == 1 else [0, groups - 1]
    others = list(range(1, groups - 1))
    packed = [[head] + [others.pop(0) for _ in range(per - 1) if others] for head in heads]
    while others:
        packed.append([others.pop(0) for _ in range(per) if others])
    return packed


def kernel(sizes, facies_hbm, mtab_hbm, ktab_hbm, state_hbm, rhs_hbm, perm_hbm, pore_hbm,
           w, qv, tzs, ty, txp, txm, final,
           u, pcb, rhs, permb, poreb, ysend, yrecv, xsend, xrecv, edge, rowk, tzf, shifted,
           zplanes, ystrips, strips, cyrecv, cxrecv, cdrecv, vsend, vrecv, lsend, lrecv, field,
           facies, mtab, ktab, ctab, near_sem, far_sem, in_sem, h_send, h_recv, c_send, c_recv):
    ngx, ngy, ngz, nz, ny, nx = sizes
    ix, iy, iz = lax.axis_index("gx"), lax.axis_index("gy"), lax.axis_index("gz")
    own = slice(HALO, HALO + ny)
    groups, per, xtiles = column_plan(nz, ny, nx)
    packing = strip_plan(ny, nx)
    f32 = jnp.float32

    def exists(dy, dx):
        ok = None
        for d, i, n in ((dy, iy, ngy), (dx, ix, ngx)):
            if d:
                here = (i > 0) if d < 0 else (i < n - 1)
                ok = here if ok is None else jnp.logical_and(ok, here)
        return ok

    def at(dy, dx):
        return {"gx": ix + dx, "gy": iy + dy, "gz": iz}

    barrier = pltpu.get_barrier_semaphore()
    for side in (SIDES[2], SIDES[3], SIDES[0], SIDES[1]):
        @pl.when(exists(*side))
        def _(side=side):
            pl.semaphore_signal(barrier, inc=1, device_id=at(*side), device_id_type=MESH)

    def signal_peers(sem):
        for d in range(1, ngz):
            pl.semaphore_signal(sem, inc=1, device_id={"gx": ix, "gy": iy, "gz": lax.rem(iz + d, ngz)},
                                device_id_type=MESH)

    signal_peers(barrier)

    loads = [
        pltpu.make_async_copy(perm_hbm, permb, in_sem.at[0]),
        pltpu.make_async_copy(state_hbm, u.at[0:3, 1:nz + 1, own], in_sem.at[1]),
        pltpu.make_async_copy(pore_hbm, poreb, in_sem.at[2]),
        pltpu.make_async_copy(rhs_hbm, rhs, in_sem.at[3]),
        pltpu.make_async_copy(facies_hbm, facies, in_sem.at[4]),
        pltpu.make_async_copy(mtab_hbm, mtab, in_sem.at[5]),
        pltpu.make_async_copy(ktab_hbm, ktab, in_sem.at[6]),
    ]
    for i in (4, 6, 5, 0, 1, 2, 3):
        loads[i].start()

    def zero(ref):
        ref[...] = jnp.zeros(ref.shape, ref.dtype)

    for cond, refs in (
        (iz == 0, [u.at[:, 0, own]]),
        (iz == ngz - 1, [u.at[:, nz + 1, own]]),
        (iy == 0, [yrecv.at[:, 0], cyrecv.at[0], lrecv.at[0]]),
        (iy == ngy - 1, [yrecv.at[:, 1], cyrecv.at[1], lrecv.at[1]]),
        (ix == 0, [xrecv.at[:, 0], cxrecv.at[0], vrecv.at[0]]),
        (ix == ngx - 1, [xrecv.at[:, 1], cxrecv.at[1], vrecv.at[1]]),
        (jnp.logical_or(iy == 0, ix == 0), [cdrecv.at[0]]),
        (jnp.logical_or(iy == 0, ix == ngx - 1), [cdrecv.at[1]]),
        (jnp.logical_or(iy == ngy - 1, ix == 0), [cdrecv.at[2]]),
        (jnp.logical_or(iy == ngy - 1, ix == ngx - 1), [cdrecv.at[3]]),
    ):
        @pl.when(cond)
        def _(refs=refs):
            for ref in refs:
                zero(ref)
    zero(field)
    for z in range(nz):
        zero(pcb.at[z, HALO + ny:])
    zero(shifted.at[:, 0:HALO])

    for i in (4, 6, 5):
        loads[i].wait()

    def coefficient(table, z, r, c):
        return table[r, facies[z], c]

    lane8 = lax.broadcasted_iota(jnp.int32, (HALO, nx), 1)
    row8 = lax.broadcasted_iota(jnp.int32, (HALO, nx), 0)
    pair8 = lax.shift_right_logical(lane8, 1)
    even8 = lax.rem(lane8, 2) == 0
    first8, last8 = lane8 == 0, lane8 == nx - 1
    nil8 = jnp.zeros((HALO, nx), f32)

    def packed_columns(values):
        out = [nil8] * xtiles
        for z, g, x in values:
            place = (g % per) * nz + z
            out[g // per] = jnp.where(pair8 == place, pltpu.roll(x, 2 * place + 1, 1), out[g // per])
        return out

    def swapped(x):
        return jnp.where(even8, pltpu.roll(x, nx - 1, 1), pltpu.roll(x, 1, 1))

    loads[0].wait()
    values = []
    for z in range(nz):
        r = 0.5 / permb[z].astype(f32)
        u[3, z + 1, own, :] = r
        for side, at_row in ((0, 0), (1, ny - 1)):
            ysend[0, side, nz + z:nz + z + 1, :] = r[at_row:at_row + 1]
        values += [(z, g, r[g * HALO:(g + 1) * HALO]) for g in range(groups)]
    packed = packed_columns(values)
    for t in range(xtiles):
        xsend[0, 1, t] = packed[t]

    loads[1].wait()
    values = []
    for z in range(nz):
        k0 = [coefficient(ktab, z, 0, k) for k in range(3)]
        pc = k0[0] * u[0, z + 1, own, :] + k0[1] * u[1, z + 1, own, :] + k0[2] * u[2, z + 1, own, :]
        pcb[z, own, :] = pc
        for side, at_row in ((0, 0), (1, ny - 1)):
            ysend[0, side, z:z + 1, :] = pc[at_row:at_row + 1]
        values += [(z, g, pc[g * HALO:(g + 1) * HALO]) for g in range(groups)]
    packed = packed_columns(values)
    for t in range(xtiles):
        xsend[0, 0, t] = packed[t]

    beside_y = exists(-1, 0).astype(jnp.int32) + exists(1, 0).astype(jnp.int32)
    beside_x = exists(0, -1).astype(jnp.int32) + exists(0, 1).astype(jnp.int32)
    pl.semaphore_wait(barrier, beside_y + beside_x + (ngz - 1))

    def remote(src, dst, send, recv, device):
        return pltpu.make_async_remote_copy(src_ref=src, dst_ref=dst, send_sem=send, recv_sem=recv,
                                            device_id=device, device_id_type=MESH)

    def start(copies):
        for sends, copy in copies:
            @pl.when(sends)
            def _(copy=copy):
                copy.start()

    def y_copies(batch):
        s = h_send.at[2 + batch], h_recv.at[2 + batch]
        return [(exists(1, 0), remote(ysend.at[batch, 1], yrecv.at[batch, 0], *s, at(1, 0))),
                (exists(-1, 0), remote(ysend.at[batch, 0], yrecv.at[batch, 1], *s, at(-1, 0)))]

    def x_copies(batch):
        s = h_send.at[4 + batch], h_recv.at[4 + batch]
        return [(exists(0, 1), remote(xsend.at[batch], xrecv.at[batch, 0], *s, at(0, 1))),
                (exists(0, -1), remote(xsend.at[batch], xrecv.at[batch, 1], *s, at(0, -1)))]

    def z_device(d):
        return {"gx": ix, "gy": iy, "gz": iz + d}

    z_up = remote(u.at[:, nz, own], u.at[:, 0, own], h_send.at[0], h_recv.at[0], z_device(1))
    z_down = remote(u.at[:, 1, own], u.at[:, nz + 1, own], h_send.at[1], h_recv.at[1], z_device(-1))
    has_below, has_above = iz > 0, iz < ngz - 1

    start(y_copies(0))
    start(x_copies(0))
    start([(has_above, z_up), (has_below, z_down)])
    for side in SIDES[:4]:
        @pl.when(exists(*side))
        def _(side=side):
            pl.semaphore_signal(near_sem, inc=1, device_id=at(*side), device_id_type=MESH)
    signal_peers(near_sem)

    def counted(count, cases, descriptor, done):
        for n, ref in cases:
            @pl.when(count == n)
            def _(ref=ref):
                done(descriptor(ref))

    def wait_many(count, cases, send, recv, sent):
        counted(count, cases, lambda ref: remote(ref, ref, send, recv, z_device(0)),
                (lambda c: c.wait_send()) if sent else (lambda c: c.wait_recv()))

    def wait_y(batch, sent):
        wait_many(beside_y, ((1, yrecv.at[batch, 0]), (2, yrecv.at[batch])), h_send.at[2 + batch], h_recv.at[2 + batch], sent)

    def wait_x(batch, sent):
        wait_many(beside_x, ((1, xrecv.at[batch, 0]), (2, xrecv.at[batch])), h_send.at[4 + batch], h_recv.at[4 + batch], sent)

    for i in range(2):
        values = []
        for z in range(nz):
            c = u[1 + i, z + 1, own, :]
            for side, at_row in ((0, 0), (1, ny - 1)):
                ysend[1, side, i * nz + z:i * nz + z + 1, :] = c[at_row:at_row + 1]
            values += [(z, g, c[g * HALO:(g + 1) * HALO]) for g in range(groups)]
        packed = packed_columns(values)
        for t in range(xtiles):
            xsend[1, i, t] = packed[t]
    start(x_copies(1))
    start(y_copies(1))

    for f in range(ktab.shape[1]):
        values = block_scalars([[mtab[r, f, c] for c in range(3)] for r in range(3)],
                               [[ktab[r, f, c] for c in range(3)] for r in range(3)])
        for i, value in enumerate(values):
            ctab[i, f] = value
    layer_of_lane = lax.rem(lane8[0:1], 2 * nz) // 2
    lanek = [jnp.zeros((1, nx), f32) for _ in range(3)]
    for z in range(nz):
        for k in range(3):
            value = coefficient(ktab, z, 0, k)
            rowk[k, z:z + 1, :] = jnp.full((1, nx), value, f32)
            lanek[k] = jnp.where(layer_of_lane == z, value, lanek[k])

    loads[2].wait()
    loads[3].wait()

    def tile_of(g):
        return slice(g * HALO, (g + 1) * HALO)

    def padded(g, shift):
        return slice(HALO + g * HALO + shift, HALO + (g + 1) * HALO + shift)

    def assemble(z, carry, upper=True):
        s_res, s_dia, s_ty, s_tx, s_hx, s_hy, s_z = (list(c) for c in carry)
        volume = poreb[z].astype(f32)
        k00 = coefficient(ktab, z, 0, 0)
        m0 = [coefficient(mtab, z, 0, k) for k in range(3)]
        if upper:
            dk = [coefficient(ktab, z, 0, k) - coefficient(ktab, z + 1, 0, k) for k in range(3)]
        for g in range(groups):
            rows = padded(g, 0)
            r = u[3, z + 1, rows, :]
            typ = 1.0 / (r + u[3, z + 1, padded(g, 1), :])
            if g == groups - 1:
                typ = jnp.where(row8 < HALO - 1, typ, 0.0)
            xp = jnp.where(last8, 0.0, 1.0 / (r + pltpu.roll(r, nx - 1, 1)))
            ty[z, rows, :] = typ
            txp[z, tile_of(g), :] = xp
            pc = pcb[z, rows, :]
            s_hx[g] = s_hx[g] + xp * (pc - pltpu.roll(pc, nx - 1, 1))
            s_hy[g] = s_hy[g] + typ * (pc - pcb[z, padded(g, 1), :])
            v = volume[tile_of(g)]
            c = [u[k, z + 1, rows, :] for k in range(3)]
            s_res[g] = s_res[g] + (rhs[0, z, tile_of(g), :] - v * (m0[0] * c[0] + m0[1] * c[1] + m0[2] * c[2]))
            s_dia[g] = s_dia[g] + v * m0[0]
            s_ty[g] = s_ty[g] + k00 * typ
            s_tx[g] = s_tx[g] + k00 * xp
            if upper:
                t = 1.0 / (r + u[3, z + 2, rows, :])
                tzf[z + 1, tile_of(g), :] = t
                d = [c[k] - u[k, z + 2, rows, :] for k in range(3)]
                s_z[g] = s_z[g] + t * (dk[0] * d[0] + dk[1] * d[1] + dk[2] * d[2])
        return tuple(tuple(s) for s in (s_res, s_dia, s_ty, s_tx, s_hx, s_hy, s_z))

    carry = ((nil8,) * groups,) * 7
    trips = (nz - 1) // 2

    def two(i, carry):
        return assemble(2 * i + 1, assemble(2 * i, carry))

    carry = lax.fori_loop(0, trips, two, carry)
    for z in range(2 * trips, nz):
        carry = assemble(z, carry, upper=z < nz - 1)
    s_res, s_dia, s_ty, s_tx, s_hx, s_hy, s_z = (list(c) for c in carry)

    for g in range(groups):
        shifted[0, padded(g, 0), :] = s_hy[g]
        shifted[1, padded(g, 0), :] = s_ty[g]
    p_rhs, p_dia = [], []
    for g in range(groups):
        p_rhs.append(s_res[g] - s_z[g] - (s_hx[g] - pltpu.roll(s_hx[g], 1, 1)) - (s_hy[g] - shifted[0, padded(g, -1), :]))
        p_dia.append(s_dia[g] + s_ty[g] + shifted[1, padded(g, -1), :] + s_tx[g] + pltpu.roll(s_tx[g], 1, 1))

    @pl.when(has_below)
    def _():
        z_up.wait_recv()

    @pl.when(has_above)
    def _():
        z_down.wait_recv()
    for slot, z, inside in ((0, 0, 1), (nz + 1, nz - 1, nz)):
        k0 = [coefficient(ktab, z, 0, k) for k in range(3)]
        for g in range(groups):
            rows = padded(g, 0)
            there = u[3, slot, rows, :]
            t = jnp.where(there > 0.0, 1.0 / (u[3, inside, rows, :] + there), 0.0)
            tzf[0 if slot == 0 else nz, tile_of(g), :] = t
            d = [u[k, inside, rows, :] - u[k, slot, rows, :] for k in range(3)]
            p_rhs[g] = p_rhs[g] - t * (k0[0] * d[0] + k0[1] * d[1] + k0[2] * d[2])
    mine = [[swapped(xsend[0, i, t]) for t in range(xtiles)] for i in range(2)]
    pl.semaphore_wait(near_sem, beside_y + beside_x + (ngz - 1))
    signal_peers(far_sem)

    planes = [p_rhs, p_dia, s_ty, s_tx]
    group8 = lax.shift_right_logical(lane8, 4)
    last_head = len(packing[:2]) - 1
    for p in range(PLANES):
        ystrips[0, p] = planes[p][0]
        ystrips[1, p] = planes[p][groups - 1]
    for i, tiles in enumerate(packing):
        strip = nil8
        for j, g in enumerate(tiles):
            for p in range(PLANES):
                slot = j * PLANES + p
                strip = jnp.where(group8 == slot, pltpu.roll(planes[p][g], (2 * HALO * slot + HALO) % nx, 1), strip)
        strips[i] = strip

    pl.semaphore_wait(far_sem, ngz - 1)

    def to_all(dy, dx, src, dst, sem):
        return [(exists(dy, dx), remote(src, dst, c_send.at[sem], c_recv.at[sem],
                                        {"gx": ix + dx, "gy": iy + dy, "gz": lax.rem(iz + d, ngz)})) for d in range(ngz)]

    for dy, dx in SIDES[4:]:
        start(to_all(dy, dx, strips.at[0 if dy < 0 else last_head], cdrecv.at[(1 - dy) + (1 - dx) // 2, iz], 3))
    for dx in (-1, 1):
        start(to_all(0, dx, strips, cxrecv.at[(1 - dx) // 2, iz], 2))
    for dy in (-1, 1):
        start(to_all(dy, 0, ystrips.at[(1 + dy) // 2], cyrecv.at[(1 - dy) // 2, iz], 1))

    wait_y(0, False)
    top8, bottom8 = row8 == 0, row8 == HALO - 1
    lines = nil8
    for side, g, here, beyond in ((0, 0, top8, bottom8), (1, groups - 1, bottom8, top8)):
        there = yrecv[0, side, nz:, :]
        t = jnp.where(there > 0.0, 1.0 / (ysend[0, side, nz:, :] + there), 0.0)
        moved = jnp.sum(t * (ysend[0, side, :nz, :] - yrecv[0, side, :nz, :]), axis=0, keepdims=True)
        weight = jnp.sum(rowk[0] * t, axis=0, keepdims=True)
        changes = [jnp.where(here, -moved, jnp.where(beyond, moved, 0.0)),
                   jnp.where(jnp.logical_or(here, beyond), weight, 0.0),
                   jnp.where(bottom8, weight, 0.0)]
        packed = nil8
        for p in range(3):
            packed = jnp.where(group8 == p, pltpu.roll(changes[p], 2 * HALO * p + HALO, 1), packed)
        vsend[side] = packed
        for z in range(nz):
            edge_row = HALO - 1 + side * ny
            ty[z, edge_row:edge_row + 1, :] = t[z:z + 1]
        for p in range(3 if side else 2):
            planes[p][g] = planes[p][g] + jnp.where(here, changes[p], 0.0)
        lines = jnp.where(row8 == 2 * side, moved, jnp.where(row8 == 2 * side + 1, weight, lines))
    zplanes[iz, PLANES * groups] = lines
    for dx in (-1, 1):
        start(to_all(0, dx, vsend, vrecv.at[(1 - dx) // 2, iz], 4))

    wait_x(0, False)
    flux, weights, faces, outside = [], [], [], []
    for t in range(xtiles):
        there = [jnp.where(even8, xrecv[0, 0, i, t], xrecv[0, 1, i, t]) for i in range(2)]
        face = jnp.where(there[1] > 0.0, 1.0 / (mine[1][t] + there[1]), 0.0)
        flux.append(face * (mine[0][t] - there[0]))
        weights.append(face * lanek[0])
        faces.append(face)
        outside.append(there[0])
    in16 = lax.rem(lane8, 2 * HALO)
    for i, tiles in enumerate(packing):
        across = nil8
        for j, g in enumerate(tiles):
            low = (g % per) * 2 * nz
            block = jnp.logical_and(lane8 >= low, lane8 < low + 2 * nz)
            sums = []
            for values in (flux, weights):
                for parity in (even8, jnp.logical_not(even8)):
                    chosen = jnp.where(jnp.logical_and(block, parity), values[g // per], 0.0)
                    sums.append(jnp.sum(chosen, axis=1, keepdims=True))
            flux_l, flux_r, weight_l, weight_r = sums
            changes = [jnp.where(first8, -flux_l, jnp.where(last8, -flux_r, 0.0)),
                       jnp.where(first8, weight_l, jnp.where(last8, weight_r, 0.0)),
                       jnp.where(last8, weight_r, 0.0)]
            for p, change in zip((0, 1, 3), changes):
                planes[p][g] = planes[p][g] + change
            for p, left, right in ((0, flux_l, flux_r), (1, weight_l, weight_r), (3, weight_l, 0.0)):
                slot = (j * PLANES + p) * 2 * HALO
                across = jnp.where(lane8 == slot + HALO - 1, left, jnp.where(lane8 == slot + HALO, right, across))
            for side, head in ((0, 0), (1, groups - 1)):
                if g == head:
                    for n in range(3):
                        lsend[side, n] = changes[n]
        zplanes[iz, PLANES * groups + 1 + i] = across
        for side, head in ((0, 0), (1, last_head)):
            if i == head:
                lsend[side, 3] = across
    for dy in (-1, 1):
        start(to_all(dy, 0, lsend.at[(1 + dy) // 2], lrecv.at[(1 - dy) // 2, iz], 5))
    for p in range(PLANES):
        for g in range(groups):
            zplanes[iz, p * groups + g] = planes[p][g]
    for d in range(1, ngz):
        remote(zplanes.at[iz], zplanes.at[iz], c_send.at[0], c_recv.at[0],
               {"gx": ix, "gy": iy, "gz": lax.rem(iz + d, ngz)}).start()

    wait_y(1, False)
    wait_x(1, False)
    invrow = 1.0 / rowk[0]
    for side, at_row in ((0, HALO - 1), (1, HALO + ny)):
        one, two_ = yrecv[1, side, :nz, :], yrecv[1, side, nz:, :]
        zero_ = (yrecv[0, side, :nz, :] - rowk[1] * one - rowk[2] * two_) * invrow
        for z in range(nz):
            for k, x in enumerate((zero_, one, two_)):
                u[k, z + 1, at_row:at_row + 1, :] = x[z:z + 1]
    invlane = 1.0 / lanek[0]
    for t in range(xtiles):
        one, two_ = (jnp.where(even8, xrecv[1, 0, i, t], xrecv[1, 1, i, t]) for i in range(2))
        zero_ = (outside[t] - lanek[1] * one - lanek[2] * two_) * invlane
        for k, x in enumerate((zero_, one, two_)):
            edge[k, t] = swapped(faces[t] * x)
        edge[3, t] = swapped(faces[t])

    outer8 = jnp.logical_or(first8, last8)

    def solve(z, _):
        volume = poreb[z].astype(f32)
        f = facies[z]
        kinv = [[ctab[KINV + 3 * r + c, f] for c in range(3)] for r in range(3)]
        n = [[ctab[NMAT + 3 * r + c, f] for c in range(3)] for r in range(3)]
        adj = [[ctab[NADJ + 3 * r + c, f] for c in range(3)] for r in range(3)]
        dia = [ctab[NDIA + i, f] for i in range(3)]
        trace, minors, det_n = ctab[NTR, f], ctab[NC2, f], ctab[NDET, f]
        for g in range(groups):
            rows = padded(g, 0)
            tile = tile_of(g)
            shift = lax.rem(2 * nx - (2 * nz * (g % per) + 1) - 2 * z, nx)
            lateral = [jnp.where(outer8, pltpu.roll(edge[k, g // per], shift, 1), 0.0) for k in range(4)]
            tzm, tzp = tzf[z, tile, :], tzf[z + 1, tile, :]
            typ, tym = ty[z, rows, :], ty[z, padded(g, -1), :]
            xp = txp[z, tile, :]
            xm = pltpu.roll(xp, 1, 1)
            tz = tzm + tzp
            tzs[z, tile, :] = tz
            total = tz + (typ + tym) + (xp + xm) + lateral[3]
            txp[z, tile, :] = xp + jnp.where(last8, lateral[3], 0.0)
            txm[z, tile, :] = xm + jnp.where(first8, lateral[3], 0.0)
            near = []
            for k in range(3):
                c = u[k, z + 1, rows, :]
                near.append(tzp * u[k, z + 2, rows, :] + tzm * u[k, z, rows, :]
                            + typ * u[k, z + 1, padded(g, 1), :] + tym * u[k, z + 1, padded(g, -1), :]
                            + xp * pltpu.roll(c, nx - 1, 1) + xm * pltpu.roll(c, 1, 1) + lateral[k])
            given = [rhs[k, z, tile, :] for k in range(3)]
            b = [near[r] + kinv[r][0] * given[0] + kinv[r][1] * given[1] + kinv[r][2] * given[2] for r in range(3)]
            v = volume[tile]
            s = total * (1.0 / v)
            e = [[s * (s + dia[r]) + adj[r][r] if r == c else adj[r][c] - s * n[r][c] for c in range(3)] for r in range(3)]
            det = ((s + trace) * s + minors) * s + det_n
            inv = 1.0 / (v * det)
            for r in range(3):
                w[r, z, tile, :] = (e[r][0] * b[0] + e[r][1] * b[1] + e[r][2] * b[2]) * inv
                qv[r, z, tile, :] = e[r][0] * inv
        return 0

    def solve_two(i, carry):
        return solve(2 * i + 1, solve(2 * i, carry))

    lax.fori_loop(0, nz // 2, solve_two, 0)
    if nz % 2:
        solve(nz - 1, 0)

    corners = beside_y * beside_x
    if ngz > 1:
        others = zplanes.at[0:ngz - 1]
        remote(others, others, c_send.at[0], c_recv.at[0], z_device(0)).wait_recv()
    y_cases = ((1, cyrecv.at[0]), (2, cyrecv))
    x_cases = ((1, cxrecv.at[0]), (2, cxrecv))
    d_cases = ((1, cdrecv.at[0]), (2, cdrecv.at[0:2]), (4, cdrecv))
    wait_many(beside_y, y_cases, c_send.at[1], c_recv.at[1], False)
    wait_many(beside_x, x_cases, c_send.at[2], c_recv.at[2], False)
    wait_many(corners, d_cases, c_send.at[3], c_recv.at[3], False)
    v_cases = ((1, vrecv.at[0]), (2, vrecv))
    l_cases = ((1, lrecv.at[0]), (2, lrecv))
    wait_many(beside_x, v_cases, c_send.at[4], c_recv.at[4], False)
    wait_many(beside_y, l_cases, c_send.at[5], c_recv.at[5], False)

    def gathered(part):
        total = part(0)
        for i in range(1, ngz):
            total = total + part(i)
        return total

    rows = ny + 2 * HALO
    elane = lax.broadcasted_iota(jnp.int32, (rows, nx), 1)
    efirst, elast = elane == 0, elane == nx - 1
    left_part = in16 < HALO
    lines = gathered(lambda i: zplanes[i, PLANES * groups])
    late = [jnp.where(left_part, gathered(lambda i: vrecv[0, i, v]), gathered(lambda i: vrecv[1, i, v])) for v in range(2)]
    beside = [[gathered(lambda i: lrecv[side, i, n]) for n in range(4)] for side in range(2)]
    side_tiles = [jnp.where(left_part, gathered(lambda i: cxrecv[0, i, t]), gathered(lambda i: cxrecv[1, i, t]))
                  + gathered(lambda i: zplanes[i, PLANES * groups + 1 + t]) for t in range(len(packing))]
    side_tiles[0] = side_tiles[0] + jnp.where(top8, late[0], 0.0)
    side_tiles[last_head] = side_tiles[last_head] + jnp.where(bottom8, late[1], 0.0)
    corner_tiles = [jnp.where(left_part, gathered(lambda i: cdrecv[2 * v, i]), gathered(lambda i: cdrecv[2 * v + 1, i]))
                    + jnp.where(bottom8 if v == 0 else top8, late[v], 0.0) + beside[v][3] for v in range(2)]
    end_tiles = []
    for side, here in ((0, bottom8), (1, top8)):
        moved, weight = lines[2 * side:2 * side + 1], lines[2 * side + 1:2 * side + 2]
        tiles = [gathered(lambda i: cyrecv[side, i, p]) for p in range(PLANES)]
        for n, p in enumerate((0, 1, 3)):
            tiles[p] = tiles[p] + beside[side][n]
        tiles[0] = tiles[0] + jnp.where(here, moved, 0.0)
        tiles[1] = tiles[1] + jnp.where(here, weight, 0.0)
        if side == 0:
            tiles[2] = tiles[2] + jnp.where(here, weight, 0.0)
        end_tiles.append(tiles)
    where_is = {g: (i, j) for i, tiles in enumerate(packing) for j, g in enumerate(tiles)}
    strip8 = jnp.logical_or(lane8 < HALO, lane8 >= nx - HALO)

    def border_of(p, g):
        if 0 <= g < groups:
            i, j = where_is[g]
            tile, slot = side_tiles[i], j * PLANES + p
        else:
            tile, slot = corner_tiles[0 if g < 0 else 1], p
        return jnp.where(strip8, pltpu.roll(tile, (2 * nx - 2 * HALO * slot - HALO) % nx, 1), 0.0)

    b = [jnp.concatenate([border_of(p, g) for g in range(-1, groups + 1)], axis=0) for p in range(PLANES)]
    a = [jnp.concatenate([end_tiles[0][p]] + [gathered(lambda i: zplanes[i, p * groups + g]) for g in range(groups)]
                         + [end_tiles[1][p]], axis=0) for p in range(PLANES)]

    def east(a, b):
        ra, rb = pltpu.roll(a, nx - 1, 1), pltpu.roll(b, nx - 1, 1)
        return jnp.where(elast, rb, ra), jnp.where(elast, ra, rb)

    def west(a, b):
        ra, rb = pltpu.roll(a, 1, 1), pltpu.roll(b, 1, 1)
        return jnp.where(efirst, rb, ra), jnp.where(efirst, ra, rb)

    mid = slice(HALO, HALO + rows)
    wests = west(a[3], b[3])
    terms = []
    for s, planes_ in enumerate((a, b)):
        there = planes_[1] > 0.0
        inv = jnp.where(there, RELAX / jnp.where(there, planes_[1], 1.0), 0.0)
        field[s, mid, :] = planes_[2]
        south = field[s, HALO - 1:HALO - 1 + rows, :]
        terms.append((planes_[0] * inv, planes_[2] * inv, south * inv, planes_[3] * inv, wests[s] * inv))

    c = [terms[0][0], terms[1][0]]
    for sweep in range(1, SWEEPS):
        e, ws = east(*c), west(*c)
        for s in range(2):
            field[s, mid, :] = c[s]
        nxt = []
        for s in range(2):
            r, tyn, tys, txe, txw = terms[s]
            nxt.append((1.0 - RELAX) * c[s] + r
                       + tyn * field[s, HALO + 1:HALO + 1 + rows, :] + tys * field[s, HALO - 1:HALO - 1 + rows, :]
                       + txe * e[s] + txw * ws[s])
        c = nxt
    e, ws = east(*c), west(*c)
    final[0] = c[0]
    final[1] = e[0]
    final[2] = ws[0]
    @pl.when(has_above)
    def _():
        z_up.wait_send()

    @pl.when(has_below)
    def _():
        z_down.wait_send()
    for batch in range(2):
        wait_y(batch, True)
        wait_x(batch, True)
    if ngz > 1:
        remote(others, others, c_send.at[0], c_recv.at[0], z_device(0)).wait_send()
    wait_many(beside_y, y_cases, c_send.at[1], c_recv.at[1], True)
    wait_many(beside_x, x_cases, c_send.at[2], c_recv.at[2], True)
    wait_many(corners, d_cases, c_send.at[3], c_recv.at[3], True)
    wait_many(beside_x, v_cases, c_send.at[4], c_recv.at[4], True)
    wait_many(beside_y, l_cases, c_send.at[5], c_recv.at[5], True)


def finish_kernel(parts, w, qv, tzs, ty, txp, txm, final, new_hbm, corr_hbm, out, out_sem):
    nz, ny, nx = tzs.shape
    own = slice(HALO, HALO + ny)
    corr = pltpu.make_async_copy(final.at[0, own], corr_hbm, out_sem.at[parts])
    corr.start()
    cc, ce, cw = (final[k, own, :] for k in range(3))
    cn, cs = final[0, HALO + 1:HALO + 1 + ny, :], final[0, HALO - 1:HALO - 1 + ny, :]

    def finish(z, _):
        g = (tzs[z] * cc + ty[z, own, :] * cn + ty[z, HALO - 1:HALO + ny - 1, :] * cs
             + txp[z] * ce + txm[z] * cw)
        for r in range(3):
            out[r, z] = w[r, z] + qv[r, z] * g
        return 0

    step = nz // parts
    outs = [corr]
    for part in range(parts):
        lax.fori_loop(part * step, (part + 1) * step, finish, 0)
        chunk = slice(part * step, (part + 1) * step)
        outs.append(pltpu.make_async_copy(out.at[:, chunk], new_hbm.at[:, chunk], out_sem.at[part]))
        outs[-1].start()
    for copy in outs:
        copy.wait()


def per_device(sizes, state, right_side, permeability, pore_volume, facies, storage_table, coupling_table):
    _, nz, ny, nx = state.shape
    sizes = sizes + (nz, ny, nx)
    f32 = jnp.float32
    ngz = sizes[2]
    cells = (nz, ny, nx)
    vmem = lambda *shape: pltpu.VMEM(shape, f32)
    hbm = pl.BlockSpec(memory_space=pltpu.HBM)
    dma = lambda n: pltpu.SemaphoreType.DMA((n,))
    ey = ny + 2 * HALO
    groups, per, xtiles = column_plan(nz, ny, nx)
    strips = len(strip_plan(ny, nx))
    facets = storage_table.shape[0]
    in_vmem = pl.BlockSpec(memory_space=pltpu.VMEM)
    handed = 4 * nx * (9 * nz * ny + nz * ey + 3 * ey)
    limit = 16384 * ((VMEM_BYTES - handed) // 16384)
    middle = pl.pallas_call(
        functools.partial(kernel, sizes),
        out_shape=(vmem(3, *cells), vmem(3, *cells), vmem(*cells), vmem(nz, ey, nx), vmem(*cells), vmem(*cells),
                   vmem(3, ey, nx)),
        in_specs=[hbm, hbm, hbm, hbm, hbm, hbm, hbm],
        out_specs=(in_vmem,) * 7,
        scratch_shapes=[
            vmem(4, nz + 2, ey, nx), vmem(nz, ey, nx), vmem(3, *cells),
            pltpu.VMEM(cells, permeability.dtype), pltpu.VMEM(cells, pore_volume.dtype),
            vmem(2, 2, 2 * nz, nx), vmem(2, 2, 2 * nz, nx),
            vmem(2, 2, xtiles, HALO, nx), vmem(2, 2, 2, xtiles, HALO, nx), vmem(4, xtiles, HALO, nx),
            vmem(3, nz, nx), vmem(nz + 1, ny, nx), vmem(2, ey, nx),
            vmem(ngz, PLANES * groups + 1 + strips, HALO, nx), vmem(2, PLANES, HALO, nx), vmem(strips, HALO, nx),
            vmem(2, ngz, PLANES, HALO, nx), vmem(2, ngz, strips, HALO, nx), vmem(4, ngz, HALO, nx),
            vmem(2, HALO, nx), vmem(2, ngz, 2, HALO, nx), vmem(2, 4, HALO, nx), vmem(2, ngz, 4, HALO, nx),
            vmem(2, ey + 2 * HALO, nx),
            pltpu.SMEM((nz,), facies.dtype), pltpu.SMEM((3, facets, 3), f32), pltpu.SMEM((3, facets, 3), f32),
            pltpu.SMEM((NCOEF, facets), f32),
            pltpu.SemaphoreType.REGULAR, pltpu.SemaphoreType.REGULAR, dma(7), dma(6), dma(6), dma(6), dma(6),
        ],
        compiler_params=pltpu.CompilerParams(collective_id=0, has_side_effects=True, vmem_limit_bytes=limit),
        name="cpr_apply",
    )(facies, storage_table.transpose(1, 0, 2), coupling_table.transpose(1, 0, 2),
      state, right_side, permeability, pore_volume)
    parts = 8 if nz % 8 == 0 else 1
    return tuple(pl.pallas_call(
        functools.partial(finish_kernel, parts),
        out_shape=(jax.ShapeDtypeStruct(state.shape, f32), jax.ShapeDtypeStruct((ny, nx), f32)),
        in_specs=[in_vmem] * 7,
        out_specs=(hbm, hbm),
        scratch_shapes=[vmem(3, *cells), dma(parts + 1)],
        compiler_params=pltpu.CompilerParams(vmem_limit_bytes=16 * 2**20),
        name="cpr_finish",
    )(*middle))


def solution(mesh):
    sizes = (mesh.shape["gx"], mesh.shape["gy"], mesh.shape["gz"])
    return jax.shard_map(
        functools.partial(per_device, sizes),
        mesh=mesh,
        in_specs=(
            P(None, "gz", "gy", "gx"),
            P(None, "gz", "gy", "gx"),
            P("gz", "gy", "gx"),
            P("gz", "gy", "gx"),
            P("gz"),
            P(),
            P(),
        ),
        out_specs=(P(None, "gz", "gy", "gx"), P("gy", "gx")),
        check_vma=False,
    )
```

```python
import functools
import jax
import jax.numpy as jnp
from jax import lax
from jax.experimental import pallas as pl
from jax.experimental.pallas import tpu as pltpu
from jax.sharding import PartitionSpec as P

SWEEPS = 8
RELAX = 0.8
MESH = pl.DeviceIdType.MESH
HALO = 8
VMEM_BYTES = 67043328

PLANES = 4
SIDES = [(-1, 0), (1, 0), (0, -1), (0, 1), (-1, -1), (-1, 1), (1, -1), (1, 1)]

KINV, NMAT, NADJ, NDIA, NTR, NC2, NDET, NCOEF = 0, 9, 18, 27, 30, 31, 32, 33


def cofactor(e, r, c):
    return (e[(r + 1) % 3][(c + 1) % 3] * e[(r + 2) % 3][(c + 2) % 3]
            - e[(r + 1) % 3][(c + 2) % 3] * e[(r + 2) % 3][(c + 1) % 3])


def block_scalars(m, k):
    kf = [[cofactor(k, r, c) for c in range(3)] for r in range(3)]
    inv = 1.0 / (k[0][0] * kf[0][0] + k[0][1] * kf[0][1] + k[0][2] * kf[0][2])
    kinv = [[kf[c][r] * inv for c in range(3)] for r in range(3)]
    n = [[kinv[r][0] * m[0][c] + kinv[r][1] * m[1][c] + kinv[r][2] * m[2][c] for c in range(3)] for r in range(3)]
    nf = [[cofactor(n, r, c) for c in range(3)] for r in range(3)]
    trace = n[0][0] + n[1][1] + n[2][2]
    return ([kinv[r][c] for r in range(3) for c in range(3)] + [n[r][c] for r in range(3) for c in range(3)]
            + [nf[c][r] for r in range(3) for c in range(3)] + [trace - n[i][i] for i in range(3)]
            + [trace, nf[0][0] + nf[1][1] + nf[2][2], n[0][0] * nf[0][0] + n[0][1] * nf[0][1] + n[0][2] * nf[0][2]])


def column_plan(nz, ny, nx):
    groups = ny // HALO
    per = nx // (2 * nz)
    return groups, per, -(-groups // per)


def strip_plan(ny, nx):
    groups = ny // HALO
    per = nx // (2 * HALO * PLANES)
    heads = [0] if groups == 1 else [0, groups - 1]
    others = list(range(1, groups - 1))
    packed = [[head] + [others.pop(0) for _ in range(per - 1) if others] for head in heads]
    while others:
        packed.append([others.pop(0) for _ in range(per) if others])
    return packed


def kernel(sizes, facies_hbm, mtab_hbm, ktab_hbm, state_hbm, rhs_hbm, perm_hbm, pore_hbm,
           w, qv, tzs, ty, txp, txm, final,
           u, pcb, rhs, permb, poreb, ysend, yrecv, xsend, xrecv, edge, rowk, tzf, shifted,
           zplanes, ystrips, strips, cyrecv, cxrecv, cdrecv, vsend, lsend, field,
           facies, mtab, ktab, ctab, near_sem, far_sem, in_sem, h_recv, c_recv):
    ngx, ngy, ngz, nz, ny, nx = sizes
    ix, iy, iz = lax.axis_index("gx"), lax.axis_index("gy"), lax.axis_index("gz")
    own = slice(HALO, HALO + ny)
    groups, per, xtiles = column_plan(nz, ny, nx)
    packing = strip_plan(ny, nx)
    f32 = jnp.float32
    send_y, send_x, send_z, send_cy, send_cx, send_cd, send_cz = (in_sem.at[i] for i in (0, 1, 4, 5, 6, 2, 3))

    def exists(dy, dx):
        ok = None
        for d, i, n in ((dy, iy, ngy), (dx, ix, ngx)):
            if d:
                here = (i > 0) if d < 0 else (i < n - 1)
                ok = here if ok is None else jnp.logical_and(ok, here)
        return ok

    def at(dy, dx):
        return {"gx": ix + dx, "gy": iy + dy, "gz": iz}

    barrier = pltpu.get_barrier_semaphore()
    for side in (SIDES[2], SIDES[3], SIDES[0], SIDES[1]):
        @pl.when(exists(*side))
        def _(side=side):
            pl.semaphore_signal(barrier, inc=1, device_id=at(*side), device_id_type=MESH)

    def signal_peers(sem):
        for d in range(1, ngz):
            pl.semaphore_signal(sem, inc=1, device_id={"gx": ix, "gy": iy, "gz": lax.rem(iz + d, ngz)},
                                device_id_type=MESH)

    signal_peers(barrier)

    loads = [
        pltpu.make_async_copy(perm_hbm, permb, in_sem.at[0]),
        pltpu.make_async_copy(state_hbm, u.at[0:3, 1:nz + 1, own], in_sem.at[1]),
        pltpu.make_async_copy(pore_hbm, poreb, in_sem.at[2]),
        pltpu.make_async_copy(rhs_hbm, rhs, in_sem.at[3]),
        pltpu.make_async_copy(facies_hbm, facies, in_sem.at[4]),
        pltpu.make_async_copy(mtab_hbm, mtab, in_sem.at[5]),
        pltpu.make_async_copy(ktab_hbm, ktab, in_sem.at[6]),
    ]
    for i in (4, 6, 5, 0, 1, 2, 3):
        loads[i].start()

    def zero(ref):
        ref[...] = jnp.zeros(ref.shape, ref.dtype)

    for cond, refs in (
        (iz == 0, [u.at[:, 0, own]]),
        (iz == ngz - 1, [u.at[:, nz + 1, own]]),
        (iy == 0, [yrecv.at[:, 0], cyrecv.at[0]]),
        (iy == ngy - 1, [yrecv.at[:, 1], cyrecv.at[1]]),
        (ix == 0, [xrecv.at[:, 0], cxrecv.at[0]]),
        (ix == ngx - 1, [xrecv.at[:, 1], cxrecv.at[1]]),
        (jnp.logical_or(iy == 0, ix == 0), [cdrecv.at[0]]),
        (jnp.logical_or(iy == 0, ix == ngx - 1), [cdrecv.at[1]]),
        (jnp.logical_or(iy == ngy - 1, ix == 0), [cdrecv.at[2]]),
        (jnp.logical_or(iy == ngy - 1, ix == ngx - 1), [cdrecv.at[3]]),
    ):
        @pl.when(cond)
        def _(refs=refs):
            for ref in refs:
                zero(ref)
    zero(field)
    for z in range(nz):
        zero(pcb.at[z, HALO + ny:])
    zero(shifted.at[:, 0:HALO])

    for i in (4, 6, 5):
        loads[i].wait()

    def coefficient(table, z, r, c):
        return table[r, facies[z], c]

    lane8 = lax.broadcasted_iota(jnp.int32, (HALO, nx), 1)
    row8 = lax.broadcasted_iota(jnp.int32, (HALO, nx), 0)
    pair8 = lax.shift_right_logical(lane8, 1)
    even8 = lax.rem(lane8, 2) == 0
    first8, last8 = lane8 == 0, lane8 == nx - 1
    nil8 = jnp.zeros((HALO, nx), f32)

    def packed_columns(values):
        out = [nil8] * xtiles
        for z, g, x in values:
            place = (g % per) * nz + z
            out[g // per] = jnp.where(pair8 == place, pltpu.roll(x, 2 * place + 1, 1), out[g // per])
        return out

    def swapped(x):
        return jnp.where(even8, pltpu.roll(x, nx - 1, 1), pltpu.roll(x, 1, 1))

    loads[0].wait()
    values = []
    for z in range(nz):
        r = 0.5 / permb[z].astype(f32)
        u[3, z + 1, own, :] = r
        for side, at_row in ((0, 0), (1, ny - 1)):
            ysend[0, side, nz + z:nz + z + 1, :] = r[at_row:at_row + 1]
        values += [(z, g, r[g * HALO:(g + 1) * HALO]) for g in range(groups)]
    packed = packed_columns(values)
    for t in range(xtiles):
        xsend[0, 1, t] = packed[t]

    loads[1].wait()
    values = []
    for z in range(nz):
        k0 = [coefficient(ktab, z, 0, k) for k in range(3)]
        pc = k0[0] * u[0, z + 1, own, :] + k0[1] * u[1, z + 1, own, :] + k0[2] * u[2, z + 1, own, :]
        pcb[z, own, :] = pc
        for side, at_row in ((0, 0), (1, ny - 1)):
            ysend[0, side, z:z + 1, :] = pc[at_row:at_row + 1]
        values += [(z, g, pc[g * HALO:(g + 1) * HALO]) for g in range(groups)]
    packed = packed_columns(values)
    for t in range(xtiles):
        xsend[0, 0, t] = packed[t]

    beside_y = exists(-1, 0).astype(jnp.int32) + exists(1, 0).astype(jnp.int32)
    beside_x = exists(0, -1).astype(jnp.int32) + exists(0, 1).astype(jnp.int32)
    pl.semaphore_wait(barrier, beside_y + beside_x + (ngz - 1))

    def remote(src, dst, send, recv, device):
        return pltpu.make_async_remote_copy(src_ref=src, dst_ref=dst, send_sem=send, recv_sem=recv,
                                            device_id=device, device_id_type=MESH)

    def start(copies):
        for sends, copy in copies:
            @pl.when(sends)
            def _(copy=copy):
                copy.start()

    def y_copies(batch):
        s = send_y, h_recv.at[1 + batch]
        return [(exists(1, 0), remote(ysend.at[batch, 1], yrecv.at[batch, 0], *s, at(1, 0))),
                (exists(-1, 0), remote(ysend.at[batch, 0], yrecv.at[batch, 1], *s, at(-1, 0)))]

    def x_copies(batch):
        s = send_x, h_recv.at[3 + batch]
        return [(exists(0, 1), remote(xsend.at[batch], xrecv.at[batch, 0], *s, at(0, 1))),
                (exists(0, -1), remote(xsend.at[batch], xrecv.at[batch, 1], *s, at(0, -1)))]

    def z_device(d):
        return {"gx": ix, "gy": iy, "gz": iz + d}

    z_up = remote(u.at[:, nz, own], u.at[:, 0, own], send_z, h_recv.at[0], z_device(1))
    z_down = remote(u.at[:, 1, own], u.at[:, nz + 1, own], send_z, h_recv.at[0], z_device(-1))
    has_below, has_above = iz > 0, iz < ngz - 1

    start(y_copies(0))
    start(x_copies(0))
    start([(has_above, z_up), (has_below, z_down)])
    for side in SIDES[:4]:
        @pl.when(exists(*side))
        def _(side=side):
            pl.semaphore_signal(near_sem, inc=1, device_id=at(*side), device_id_type=MESH)
    signal_peers(near_sem)

    def counted(count, cases, descriptor, done):
        for n, ref in cases:
            @pl.when(count == n)
            def _(ref=ref):
                done(descriptor(ref))

    def wait_many(count, cases, send, recv, sent):
        counted(count, cases, lambda ref: remote(ref, ref, send, recv, z_device(0)),
                (lambda c: c.wait_send()) if sent else (lambda c: c.wait_recv()))

    def wait_y(batch):
        wait_many(beside_y, ((1, yrecv.at[batch, 0]), (2, yrecv.at[batch])), send_y, h_recv.at[1 + batch], False)

    def wait_x(batch):
        wait_many(beside_x, ((1, xrecv.at[batch, 0]), (2, xrecv.at[batch])), send_x, h_recv.at[3 + batch], False)

    beside_z = has_below.astype(jnp.int32) + has_above.astype(jnp.int32)
    z_cases = ((1, u.at[:, 1, own]), (2, u.at[:, 1:3, own]))

    for i in range(2):
        values = []
        for z in range(nz):
            c = u[1 + i, z + 1, own, :]
            for side, at_row in ((0, 0), (1, ny - 1)):
                ysend[1, side, i * nz + z:i * nz + z + 1, :] = c[at_row:at_row + 1]
            values += [(z, g, c[g * HALO:(g + 1) * HALO]) for g in range(groups)]
        packed = packed_columns(values)
        for t in range(xtiles):
            xsend[1, i, t] = packed[t]
    start(x_copies(1))
    start(y_copies(1))

    for f in range(ktab.shape[1]):
        values = block_scalars([[mtab[r, f, c] for c in range(3)] for r in range(3)],
                               [[ktab[r, f, c] for c in range(3)] for r in range(3)])
        for i, value in enumerate(values):
            ctab[i, f] = value
    layer_of_lane = lax.rem(lane8[0:1], 2 * nz) // 2
    lanek = [jnp.zeros((1, nx), f32) for _ in range(3)]
    for z in range(nz):
        for k in range(3):
            value = coefficient(ktab, z, 0, k)
            rowk[k, z:z + 1, :] = jnp.full((1, nx), value, f32)
            lanek[k] = jnp.where(layer_of_lane == z, value, lanek[k])

    loads[2].wait()
    loads[3].wait()

    def tile_of(g):
        return slice(g * HALO, (g + 1) * HALO)

    def padded(g, shift):
        return slice(HALO + g * HALO + shift, HALO + (g + 1) * HALO + shift)

    def assemble(z, carry, upper=True):
        s_res, s_dia, s_ty, s_tx, s_hx, s_hy, s_z = (list(c) for c in carry)
        volume = poreb[z].astype(f32)
        k00 = coefficient(ktab, z, 0, 0)
        m0 = [coefficient(mtab, z, 0, k) for k in range(3)]
        if upper:
            dk = [coefficient(ktab, z, 0, k) - coefficient(ktab, z + 1, 0, k) for k in range(3)]
        for g in range(groups):
            rows = padded(g, 0)
            r = u[3, z + 1, rows, :]
            typ = 1.0 / (r + u[3, z + 1, padded(g, 1), :])
            if g == groups - 1:
                typ = jnp.where(row8 < HALO - 1, typ, 0.0)
            xp = jnp.where(last8, 0.0, 1.0 / (r + pltpu.roll(r, nx - 1, 1)))
            ty[z, rows, :] = typ
            txp[z, tile_of(g), :] = xp
            pc = pcb[z, rows, :]
            s_hx[g] = s_hx[g] + xp * (pc - pltpu.roll(pc, nx - 1, 1))
            s_hy[g] = s_hy[g] + typ * (pc - pcb[z, padded(g, 1), :])
            v = volume[tile_of(g)]
            c = [u[k, z + 1, rows, :] for k in range(3)]
            s_res[g] = s_res[g] + (rhs[0, z, tile_of(g), :] - v * (m0[0] * c[0] + m0[1] * c[1] + m0[2] * c[2]))
            s_dia[g] = s_dia[g] + v * m0[0]
            s_ty[g] = s_ty[g] + k00 * typ
            s_tx[g] = s_tx[g] + k00 * xp
            if upper:
                t = 1.0 / (r + u[3, z + 2, rows, :])
                tzf[z + 1, tile_of(g), :] = t
                d = [c[k] - u[k, z + 2, rows, :] for k in range(3)]
                s_z[g] = s_z[g] + t * (dk[0] * d[0] + dk[1] * d[1] + dk[2] * d[2])
        return tuple(tuple(s) for s in (s_res, s_dia, s_ty, s_tx, s_hx, s_hy, s_z))

    carry = ((nil8,) * groups,) * 7
    trips = (nz - 1) // 2

    def two(i, carry):
        return assemble(2 * i + 1, assemble(2 * i, carry))

    carry = lax.fori_loop(0, trips, two, carry)
    for z in range(2 * trips, nz):
        carry = assemble(z, carry, upper=z < nz - 1)
    s_res, s_dia, s_ty, s_tx, s_hx, s_hy, s_z = (list(c) for c in carry)

    for g in range(groups):
        shifted[0, padded(g, 0), :] = s_hy[g]
        shifted[1, padded(g, 0), :] = s_ty[g]
    p_rhs, p_dia = [], []
    for g in range(groups):
        p_rhs.append(s_res[g] - s_z[g] - (s_hx[g] - pltpu.roll(s_hx[g], 1, 1)) - (s_hy[g] - shifted[0, padded(g, -1), :]))
        p_dia.append(s_dia[g] + s_ty[g] + shifted[1, padded(g, -1), :] + s_tx[g] + pltpu.roll(s_tx[g], 1, 1))

    wait_many(beside_z, z_cases, send_z, h_recv.at[0], False)
    for slot, z, inside in ((0, 0, 1), (nz + 1, nz - 1, nz)):
        k0 = [coefficient(ktab, z, 0, k) for k in range(3)]
        for g in range(groups):
            rows = padded(g, 0)
            there = u[3, slot, rows, :]
            t = jnp.where(there > 0.0, 1.0 / (u[3, inside, rows, :] + there), 0.0)
            tzf[0 if slot == 0 else nz, tile_of(g), :] = t
            d = [u[k, inside, rows, :] - u[k, slot, rows, :] for k in range(3)]
            p_rhs[g] = p_rhs[g] - t * (k0[0] * d[0] + k0[1] * d[1] + k0[2] * d[2])
    mine = [[swapped(xsend[0, i, t]) for t in range(xtiles)] for i in range(2)]
    pl.semaphore_wait(near_sem, beside_y + beside_x + (ngz - 1))
    signal_peers(far_sem)

    planes = [p_rhs, p_dia, s_ty, s_tx]
    group8 = lax.shift_right_logical(lane8, 4)
    last_head = len(packing[:2]) - 1
    for p in range(PLANES):
        ystrips[0, p] = planes[p][0]
        ystrips[1, p] = planes[p][groups - 1]
    for i, tiles in enumerate(packing):
        strip = nil8
        for j, g in enumerate(tiles):
            for p in range(PLANES):
                slot = j * PLANES + p
                strip = jnp.where(group8 == slot, pltpu.roll(planes[p][g], (2 * HALO * slot + HALO) % nx, 1), strip)
        strips[i] = strip

    pl.semaphore_wait(far_sem, ngz - 1)

    def to_all(dy, dx, src, dst, send, recv):
        return [(exists(dy, dx), remote(src, dst, send, c_recv.at[recv],
                                        {"gx": ix + dx, "gy": iy + dy, "gz": lax.rem(iz + d, ngz)})) for d in range(ngz)]

    nstrips = len(packing)
    for dy, dx in SIDES[4:]:
        start(to_all(dy, dx, strips.at[0 if dy < 0 else last_head], cdrecv.at[(1 - dy) + (1 - dx) // 2, iz], send_cd, 3))
    for dx in (-1, 1):
        start(to_all(0, dx, strips, cxrecv.at[(1 - dx) // 2, iz, 0:nstrips], send_cx, 2))
    for dy in (-1, 1):
        start(to_all(dy, 0, ystrips.at[(1 + dy) // 2], cyrecv.at[(1 - dy) // 2, iz, 0:PLANES], send_cy, 1))

    wait_y(0)
    top8, bottom8 = row8 == 0, row8 == HALO - 1
    lines = nil8
    y_faces = []
    for side, g, here in ((0, 0, top8), (1, groups - 1, bottom8)):
        there = yrecv[0, side, nz:, :]
        t = jnp.where(there > 0.0, 1.0 / (ysend[0, side, nz:, :] + there), 0.0)
        moved = jnp.sum(t * (ysend[0, side, :nz, :] - yrecv[0, side, :nz, :]), axis=0, keepdims=True)
        weight = jnp.sum(rowk[0] * t, axis=0, keepdims=True)
        lines = jnp.where(row8 == 2 * side, moved, jnp.where(row8 == 2 * side + 1, weight, lines))
        y_faces.append((side, g, here, t, moved, weight))
    vsend[...] = lines
    for dx in (-1, 1):
        start(to_all(0, dx, vsend, cxrecv.at[(1 - dx) // 2, iz, nstrips], send_cx, 4))
    wait_x(0)
    flux, weights, faces, outside = [], [], [], []
    for t in range(xtiles):
        there = [jnp.where(even8, xrecv[0, 0, i, t], xrecv[0, 1, i, t]) for i in range(2)]
        face = jnp.where(there[1] > 0.0, 1.0 / (mine[1][t] + there[1]), 0.0)
        flux.append(face * (mine[0][t] - there[0]))
        weights.append(face * lanek[0])
        faces.append(face)
        outside.append(there[0])

    def side_sums(g):
        low = (g % per) * 2 * nz
        block = jnp.logical_and(lane8 >= low, lane8 < low + 2 * nz)
        sums = []
        for values in (flux, weights):
            for parity in (even8, jnp.logical_not(even8)):
                chosen = jnp.where(jnp.logical_and(block, parity), values[g // per], 0.0)
                sums.append(jnp.sum(chosen, axis=1, keepdims=True))
        return sums

    def at_sides(left, right):
        return jnp.where(first8, left, jnp.where(last8, right, 0.0))

    sums = {}
    for side, g in ((0, 0), (1, groups - 1)):
        if g not in sums:
            sums[g] = side_sums(g)
        flux_l, flux_r, weight_l, weight_r = sums[g]
        tile = nil8
        for i, column in enumerate((-flux_r, -flux_l, weight_r, weight_l, flux_l, flux_r, weight_l, weight_r)):
            tile = jnp.where(lane8 == i, column, tile)
        lsend[side] = tile
    for dy in (-1, 1):
        start(to_all(dy, 0, lsend.at[(1 + dy) // 2], cyrecv.at[(1 - dy) // 2, iz, PLANES], send_cy, 5))

    for side, g, here, t, moved, weight in y_faces:
        for p, change in ((0, -moved), (1, weight), (2, weight))[:3 if side else 2]:
            planes[p][g] = planes[p][g] + jnp.where(here, change, 0.0)
        for z in range(nz):
            edge_row = HALO - 1 + side * ny
            ty[z, edge_row:edge_row + 1, :] = t[z:z + 1]
    zplanes[iz, PLANES * groups] = lines
    in16 = lax.rem(lane8, 2 * HALO)
    for i, tiles in enumerate(packing):
        across = nil8
        for j, g in enumerate(tiles):
            if g not in sums:
                sums[g] = side_sums(g)
            flux_l, flux_r, weight_l, weight_r = sums[g]
            for p, change in ((0, at_sides(-flux_l, -flux_r)), (1, at_sides(weight_l, weight_r)),
                              (3, jnp.where(last8, weight_r, 0.0))):
                planes[p][g] = planes[p][g] + change
            for p, left, right in ((0, flux_l, flux_r), (1, weight_l, weight_r), (3, weight_l, 0.0)):
                slot = (j * PLANES + p) * 2 * HALO
                across = jnp.where(lane8 == slot + HALO - 1, left, jnp.where(lane8 == slot + HALO, right, across))
        zplanes[iz, PLANES * groups + 1 + i] = across
    for p in range(PLANES):
        for g in range(groups):
            zplanes[iz, p * groups + g] = planes[p][g]
    for d in range(1, ngz):
        remote(zplanes.at[iz], zplanes.at[iz], send_cz, c_recv.at[0],
               {"gx": ix, "gy": iy, "gz": lax.rem(iz + d, ngz)}).start()

    wait_y(1)
    wait_x(1)
    invrow = 1.0 / rowk[0]
    for side, at_row in ((0, HALO - 1), (1, HALO + ny)):
        one, two_ = yrecv[1, side, :nz, :], yrecv[1, side, nz:, :]
        zero_ = (yrecv[0, side, :nz, :] - rowk[1] * one - rowk[2] * two_) * invrow
        for z in range(nz):
            for k, x in enumerate((zero_, one, two_)):
                u[k, z + 1, at_row:at_row + 1, :] = x[z:z + 1]
    invlane = 1.0 / lanek[0]
    for t in range(xtiles):
        one, two_ = (jnp.where(even8, xrecv[1, 0, i, t], xrecv[1, 1, i, t]) for i in range(2))
        zero_ = (outside[t] - lanek[1] * one - lanek[2] * two_) * invlane
        for k, x in enumerate((zero_, one, two_)):
            edge[k, t] = swapped(faces[t] * x)
        edge[3, t] = swapped(faces[t])

    outer8 = jnp.logical_or(first8, last8)

    def solve(z, _):
        volume = poreb[z].astype(f32)
        f = facies[z]
        kinv = [[ctab[KINV + 3 * r + c, f] for c in range(3)] for r in range(3)]
        n = [[ctab[NMAT + 3 * r + c, f] for c in range(3)] for r in range(3)]
        adj = [[ctab[NADJ + 3 * r + c, f] for c in range(3)] for r in range(3)]
        dia = [ctab[NDIA + i, f] for i in range(3)]
        trace, minors, det_n = ctab[NTR, f], ctab[NC2, f], ctab[NDET, f]
        for g in range(groups):
            rows = padded(g, 0)
            tile = tile_of(g)
            shift = lax.rem(2 * nx - (2 * nz * (g % per) + 1) - 2 * z, nx)
            lateral = [jnp.where(outer8, pltpu.roll(edge[k, g // per], shift, 1), 0.0) for k in range(4)]
            tzm, tzp = tzf[z, tile, :], tzf[z + 1, tile, :]
            typ, tym = ty[z, rows, :], ty[z, padded(g, -1), :]
            xp = txp[z, tile, :]
            xm = pltpu.roll(xp, 1, 1)
            tz = tzm + tzp
            tzs[z, tile, :] = tz
            total = tz + (typ + tym) + (xp + xm) + lateral[3]
            txp[z, tile, :] = xp + jnp.where(last8, lateral[3], 0.0)
            txm[z, tile, :] = xm + jnp.where(first8, lateral[3], 0.0)
            near = []
            for k in range(3):
                c = u[k, z + 1, rows, :]
                near.append(tzp * u[k, z + 2, rows, :] + tzm * u[k, z, rows, :]
                            + typ * u[k, z + 1, padded(g, 1), :] + tym * u[k, z + 1, padded(g, -1), :]
                            + xp * pltpu.roll(c, nx - 1, 1) + xm * pltpu.roll(c, 1, 1) + lateral[k])
            given = [rhs[k, z, tile, :] for k in range(3)]
            b = [near[r] + kinv[r][0] * given[0] + kinv[r][1] * given[1] + kinv[r][2] * given[2] for r in range(3)]
            v = volume[tile]
            s = total * (1.0 / v)
            e = [[s * (s + dia[r]) + adj[r][r] if r == c else adj[r][c] - s * n[r][c] for c in range(3)] for r in range(3)]
            det = ((s + trace) * s + minors) * s + det_n
            inv = 1.0 / (v * det)
            for r in range(3):
                w[r, z, tile, :] = (e[r][0] * b[0] + e[r][1] * b[1] + e[r][2] * b[2]) * inv
                qv[r, z, tile, :] = e[r][0] * inv
        return 0

    def solve_two(i, carry):
        return solve(2 * i + 1, solve(2 * i, carry))

    lax.fori_loop(0, nz // 2, solve_two, 0)
    if nz % 2:
        solve(nz - 1, 0)

    corners = beside_y * beside_x
    if ngz > 1:
        others = zplanes.at[0:ngz - 1]
        remote(others, others, send_cz, c_recv.at[0], z_device(0)).wait_recv()
    d_cases = ((1, cdrecv.at[0]), (2, cdrecv.at[0:2]), (4, cdrecv))
    wait_many(beside_y, ((1, cyrecv.at[0, :, 0:PLANES]), (2, cyrecv.at[:, :, 0:PLANES])), send_cy, c_recv.at[1], False)
    wait_many(beside_x, ((1, cxrecv.at[0, :, 0:nstrips]), (2, cxrecv.at[:, :, 0:nstrips])), send_cx, c_recv.at[2], False)
    wait_many(corners, d_cases, send_cd, c_recv.at[3], False)

    def gathered(part):
        total = part(0)
        for i in range(1, ngz):
            total = total + part(i)
        return total

    tiles_in = groups + 2
    left_part = in16 < HALO
    side_tiles = [jnp.where(left_part, gathered(lambda i: cxrecv[0, i, t]), gathered(lambda i: cxrecv[1, i, t]))
                  + gathered(lambda i: zplanes[i, PLANES * groups + 1 + t]) for t in range(nstrips)]
    corner_tiles = [jnp.where(left_part, gathered(lambda i: cdrecv[2 * v, i]), gathered(lambda i: cdrecv[2 * v + 1, i]))
                    for v in range(2)]
    where_is = {g: (i, j) for i, tiles in enumerate(packing) for j, g in enumerate(tiles)}
    on_right, on_left = lane8 < HALO, lane8 >= nx - HALO
    strip8 = jnp.logical_or(on_right, on_left)

    def border_of(p, g):
        if 0 <= g < groups:
            i, j = where_is[g]
            tile, slot = side_tiles[i], j * PLANES + p
        else:
            tile, slot = corner_tiles[0 if g < 0 else 1], p
        return jnp.where(strip8, pltpu.roll(tile, (2 * nx - 2 * HALO * slot - HALO) % nx, 1), 0.0)

    b = [[border_of(p, g) for g in range(-1, groups + 1)] for p in range(PLANES)]
    own_lines = gathered(lambda i: zplanes[i, PLANES * groups])
    a = [[gathered(lambda i: cyrecv[0, i, p])] + [gathered(lambda i: zplanes[i, p * groups + g]) for g in range(groups)]
         + [gathered(lambda i: cyrecv[1, i, p])] for p in range(PLANES)]

    def beyond(grid, lines):
        for side, t, here in ((0, 0, bottom8), (1, tiles_in - 1, top8)):
            moved, weight = lines[2 * side:2 * side + 1], lines[2 * side + 1:2 * side + 2]
            for p, change in ((0, moved), (1, weight), (2, weight))[:2 if side else 3]:
                grid[p][t] = grid[p][t] + jnp.where(here, change, 0.0)

    beyond(a, own_lines)

    def east(ra, rb):
        return jnp.where(last8, rb, ra), jnp.where(last8, ra, rb)

    def west(ra, rb):
        return jnp.where(first8, rb, ra), jnp.where(first8, ra, rb)

    def fill(buffer, s, tiles):
        for t in range(tiles_in):
            field[buffer, s, (t + 1) * HALO:(t + 2) * HALO, :] = tiles[t]

    def above(buffer, s, t):
        return field[buffer, s, (t + 1) * HALO - 1:(t + 2) * HALO - 1, :]

    def below(buffer, s, t):
        return field[buffer, s, (t + 1) * HALO + 1:(t + 2) * HALO + 1, :]

    terms = [[None] * tiles_in for _ in range(2)]
    grids = (a, b)

    def prepare(s, t):
        rhs_, dia, down, right = (grids[s][p][t] for p in range(PLANES))
        there = dia > 0.0
        inv = jnp.where(there, RELAX / jnp.where(there, dia, 1.0), 0.0)
        left = west(*(pltpu.roll(grid[3][t], 1, 1) for grid in grids))[s]
        terms[s][t] = [rhs_ * inv, down * inv, above(0, s, t) * inv, right * inv, left * inv]

    fill(0, 0, a[2])
    late_b = (0, 1, groups, groups + 1)
    for t in range(1, tiles_in - 1):
        prepare(0, t)

    wait_many(beside_x, ((1, cxrecv.at[0, :, nstrips]), (2, cxrecv.at[:, :, nstrips])), send_cx, c_recv.at[4], False)
    lines = jnp.where(on_left, gathered(lambda i: cxrecv[0, i, nstrips]),
                      jnp.where(on_right, gathered(lambda i: cxrecv[1, i, nstrips]), 0.0))
    beyond(b, lines)
    for side, t, here in ((0, 1, top8), (1, groups, bottom8)):
        moved, weight = lines[2 * side:2 * side + 1], lines[2 * side + 1:2 * side + 2]
        for p, change in ((0, -moved), (1, weight), (2, weight))[:3 if side else 2]:
            b[p][t] = b[p][t] + jnp.where(here, change, 0.0)
    fill(0, 1, b[2])
    for t in range(1, tiles_in - 1):
        prepare(1, t)
    wait_many(beside_y, ((1, cyrecv.at[0, :, PLANES]), (2, cyrecv.at[:, :, PLANES])), send_cy, c_recv.at[5], False)
    for side, t in ((0, 0), (1, tiles_in - 1)):
        columns = gathered(lambda i: cyrecv[side, i, PLANES])
        flux_, weight_, flux_past, weight_past = (
            jnp.where(outer8, pltpu.roll(columns, nx - 2 * n - 1, 1), 0.0) for n in range(4))
        for grid, change, weight in ((a, flux_, weight_), (b, flux_past, weight_past)):
            grid[0][t] = grid[0][t] + change
            grid[1][t] = grid[1][t] + weight
            grid[3][t] = grid[3][t] + jnp.where(last8, weight, 0.0)
        for s in range(2):
            prepare(s, t)

    c = [[terms[s][t][0] for t in range(tiles_in)] for s in range(2)]
    for sweep in range(1, SWEEPS):
        buffer = sweep % 2
        for s in range(2):
            fill(buffer, s, c[s])
        nxt = [[None] * tiles_in for _ in range(2)]
        for t in range(tiles_in):
            e = east(*(pltpu.roll(c[s][t], nx - 1, 1) for s in range(2)))
            ws = west(*(pltpu.roll(c[s][t], 1, 1) for s in range(2)))
            for s in range(2):
                r, tyn, tys, txe, txw = terms[s][t]
                nxt[s][t] = (((1.0 - RELAX) * c[s][t] + r) + (tyn * below(buffer, s, t) + tys * above(buffer, s, t))
                             + (txe * e[s] + txw * ws[s]))
        c = nxt
    for t in range(tiles_in):
        rows = slice(t * HALO, (t + 1) * HALO)
        final[0, rows, :] = c[0][t]
        if 0 < t < tiles_in - 1:
            final[1, rows, :] = east(*(pltpu.roll(c[s][t], nx - 1, 1) for s in range(2)))[0]
            final[2, rows, :] = west(*(pltpu.roll(c[s][t], 1, 1) for s in range(2)))[0]
    for count, cases, sem in (
        (beside_y, ((1, yrecv.at[0]), (2, yrecv)), send_y),
        (beside_x, ((1, xrecv.at[0]), (2, xrecv)), send_x),
        (beside_z, z_cases, send_z),
        (beside_y, ((1, cyrecv.at[0]), (2, cyrecv)), send_cy),
        (beside_x, ((1, cxrecv.at[0]), (2, cxrecv)), send_cx),
        (corners, d_cases, send_cd),
    ):
        wait_many(count, cases, sem, h_recv.at[0], True)
    if ngz > 1:
        remote(others, others, send_cz, c_recv.at[0], z_device(0)).wait_send()


def finish_kernel(parts, w, qv, tzs, ty, txp, txm, final, new_hbm, corr_hbm, out, out_sem):
    nz, ny, nx = tzs.shape
    own = slice(HALO, HALO + ny)
    corr = pltpu.make_async_copy(final.at[0, own], corr_hbm, out_sem.at[parts])
    corr.start()
    cc, ce, cw = (final[k, own, :] for k in range(3))
    cn, cs = final[0, HALO + 1:HALO + 1 + ny, :], final[0, HALO - 1:HALO - 1 + ny, :]

    def finish(z, _):
        g = (tzs[z] * cc + ty[z, own, :] * cn + ty[z, HALO - 1:HALO + ny - 1, :] * cs
             + txp[z] * ce + txm[z] * cw)
        for r in range(3):
            out[r, z] = w[r, z] + qv[r, z] * g
        return 0

    step = nz // parts
    outs = [corr]
    for part in range(parts):
        lax.fori_loop(part * step, (part + 1) * step, finish, 0)
        chunk = slice(part * step, (part + 1) * step)
        outs.append(pltpu.make_async_copy(out.at[:, chunk], new_hbm.at[:, chunk], out_sem.at[part]))
        outs[-1].start()
    for copy in outs:
        copy.wait()


def per_device(sizes, state, right_side, permeability, pore_volume, facies, storage_table, coupling_table):
    _, nz, ny, nx = state.shape
    sizes = sizes + (nz, ny, nx)
    f32 = jnp.float32
    ngz = sizes[2]
    cells = (nz, ny, nx)
    vmem = lambda *shape: pltpu.VMEM(shape, f32)
    hbm = pl.BlockSpec(memory_space=pltpu.HBM)
    dma = lambda n: pltpu.SemaphoreType.DMA((n,))
    ey = ny + 2 * HALO
    groups, per, xtiles = column_plan(nz, ny, nx)
    strips = len(strip_plan(ny, nx))
    facets = storage_table.shape[0]
    in_vmem = pl.BlockSpec(memory_space=pltpu.VMEM)
    handed = 4 * nx * (9 * nz * ny + nz * ey + 3 * ey)
    limit = 16384 * ((VMEM_BYTES - handed) // 16384)
    middle = pl.pallas_call(
        functools.partial(kernel, sizes),
        out_shape=(vmem(3, *cells), vmem(3, *cells), vmem(*cells), vmem(nz, ey, nx), vmem(*cells), vmem(*cells),
                   vmem(3, ey, nx)),
        in_specs=[hbm, hbm, hbm, hbm, hbm, hbm, hbm],
        out_specs=(in_vmem,) * 7,
        scratch_shapes=[
            vmem(4, nz + 2, ey, nx), vmem(nz, ey, nx), vmem(3, *cells),
            pltpu.VMEM(cells, permeability.dtype), pltpu.VMEM(cells, pore_volume.dtype),
            vmem(2, 2, 2 * nz, nx), vmem(2, 2, 2 * nz, nx),
            vmem(2, 2, xtiles, HALO, nx), vmem(2, 2, 2, xtiles, HALO, nx), vmem(4, xtiles, HALO, nx),
            vmem(3, nz, nx), vmem(nz + 1, ny, nx), vmem(2, ey, nx),
            vmem(ngz, PLANES * groups + 1 + strips, HALO, nx), vmem(2, PLANES, HALO, nx), vmem(strips, HALO, nx),
            vmem(2, ngz, PLANES + 1, HALO, nx), vmem(2, ngz, strips + 1, HALO, nx), vmem(4, ngz, HALO, nx),
            vmem(HALO, nx), vmem(2, HALO, nx), vmem(2, 2, ey + 2 * HALO, nx),
            pltpu.SMEM((nz,), facies.dtype), pltpu.SMEM((3, facets, 3), f32), pltpu.SMEM((3, facets, 3), f32),
            pltpu.SMEM((NCOEF, facets), f32),
            pltpu.SemaphoreType.REGULAR, pltpu.SemaphoreType.REGULAR, dma(7), dma(5), dma(6),
        ],
        compiler_params=pltpu.CompilerParams(collective_id=0, has_side_effects=True, vmem_limit_bytes=limit),
        name="cpr_apply",
    )(facies, storage_table.transpose(1, 0, 2), coupling_table.transpose(1, 0, 2),
      state, right_side, permeability, pore_volume)
    parts = 8 if nz % 8 == 0 else 1
    return tuple(pl.pallas_call(
        functools.partial(finish_kernel, parts),
        out_shape=(jax.ShapeDtypeStruct(state.shape, f32), jax.ShapeDtypeStruct((ny, nx), f32)),
        in_specs=[in_vmem] * 7,
        out_specs=(hbm, hbm),
        scratch_shapes=[vmem(3, *cells), dma(parts + 1)],
        compiler_params=pltpu.CompilerParams(vmem_limit_bytes=16 * 2**20),
        name="cpr_finish",
    )(*middle))


def solution(mesh):
    sizes = (mesh.shape["gx"], mesh.shape["gy"], mesh.shape["gz"])
    return jax.shard_map(
        functools.partial(per_device, sizes),
        mesh=mesh,
        in_specs=(
            P(None, "gz", "gy", "gx"),
            P(None, "gz", "gy", "gx"),
            P("gz", "gy", "gx"),
            P("gz", "gy", "gx"),
            P("gz"),
            P(),
            P(),
        ),
        out_specs=(P(None, "gz", "gy", "gx"), P("gy", "gx")),
        check_vma=False,
    )
```

```python
import functools
import jax
import jax.numpy as jnp
from jax import lax
from jax.experimental import pallas as pl
from jax.experimental.pallas import tpu as pltpu
from jax.sharding import PartitionSpec as P

SWEEPS = 8
RELAX = 0.8
MESH = pl.DeviceIdType.MESH
HALO = 8
VMEM_BYTES = 67043328

PLANES = 4
SIDES = [(-1, 0), (1, 0), (0, -1), (0, 1), (-1, -1), (-1, 1), (1, -1), (1, 1)]

KINV, NMAT, NADJ, NDIA, NTR, NC2, NDET, NCOEF = 0, 9, 18, 27, 30, 31, 32, 33


def cofactor(e, r, c):
    return (e[(r + 1) % 3][(c + 1) % 3] * e[(r + 2) % 3][(c + 2) % 3]
            - e[(r + 1) % 3][(c + 2) % 3] * e[(r + 2) % 3][(c + 1) % 3])


def block_scalars(m, k):
    kf = [[cofactor(k, r, c) for c in range(3)] for r in range(3)]
    inv = 1.0 / (k[0][0] * kf[0][0] + k[0][1] * kf[0][1] + k[0][2] * kf[0][2])
    kinv = [[kf[c][r] * inv for c in range(3)] for r in range(3)]
    n = [[kinv[r][0] * m[0][c] + kinv[r][1] * m[1][c] + kinv[r][2] * m[2][c] for c in range(3)] for r in range(3)]
    nf = [[cofactor(n, r, c) for c in range(3)] for r in range(3)]
    trace = n[0][0] + n[1][1] + n[2][2]
    return ([kinv[r][c] for r in range(3) for c in range(3)] + [n[r][c] for r in range(3) for c in range(3)]
            + [nf[c][r] for r in range(3) for c in range(3)] + [trace - n[i][i] for i in range(3)]
            + [trace, nf[0][0] + nf[1][1] + nf[2][2], n[0][0] * nf[0][0] + n[0][1] * nf[0][1] + n[0][2] * nf[0][2]])


def column_plan(nz, ny, nx):
    groups = ny // HALO
    per = nx // (2 * nz)
    return groups, per, -(-groups // per)


def strip_plan(ny, nx):
    groups = ny // HALO
    per = nx // (2 * HALO * PLANES)
    heads = [0] if groups == 1 else [0, groups - 1]
    others = list(range(1, groups - 1))
    packed = [[head] + [others.pop(0) for _ in range(per - 1) if others] for head in heads]
    while others:
        packed.append([others.pop(0) for _ in range(per) if others])
    return packed


def kernel(sizes, facies_hbm, mtab_hbm, ktab_hbm, state_hbm, rhs_hbm, perm_hbm, pore_hbm,
           w, qv, tzs, ty, txp, txm, final,
           u, pcb, rhs, permb, poreb, ysend, yrecv, xsend, xrecv, edge, rowk, tzf, shifted,
           zplanes, ystrips, strips, cyrecv, cxrecv, cdrecv, rpsend, dsend, field,
           facies, mtab, ktab, ctab, near, far_sem, in_sem, h_recv, c_recv):
    ngx, ngy, ngz, nz, ny, nx = sizes
    ix, iy, iz = lax.axis_index("gx"), lax.axis_index("gy"), lax.axis_index("gz")
    own = slice(HALO, HALO + ny)
    groups, per, xtiles = column_plan(nz, ny, nx)
    packing = strip_plan(ny, nx)
    nstrips = len(packing)
    last_head = len(packing[:2]) - 1
    layers = nz // HALO
    ends = ((0, 0), (1, groups - 1))
    first_part = PLANES * groups + 1 + nstrips
    f32 = jnp.float32
    send_y, send_x, send_z, send_cy, send_cx, send_cd, send_cz = (in_sem.at[i] for i in (0, 1, 4, 5, 6, 2, 3))

    def exists(dy, dx):
        ok = None
        for d, i, n in ((dy, iy, ngy), (dx, ix, ngx)):
            if d:
                here = (i > 0) if d < 0 else (i < n - 1)
                ok = here if ok is None else jnp.logical_and(ok, here)
        return ok

    def at(dy, dx):
        return {"gx": ix + dx, "gy": iy + dy, "gz": iz}

    barrier = pltpu.get_barrier_semaphore()
    for side in (SIDES[0], SIDES[2], SIDES[1], SIDES[3]):
        @pl.when(exists(*side))
        def _(side=side):
            pl.semaphore_signal(barrier, inc=1, device_id=at(*side), device_id_type=MESH)

    def signal_peers(sem):
        for d in range(1, ngz):
            pl.semaphore_signal(sem, inc=1, device_id={"gx": ix, "gy": iy, "gz": lax.rem(iz + d, ngz)},
                                device_id_type=MESH)

    signal_peers(barrier)

    loads = [
        pltpu.make_async_copy(perm_hbm, permb, in_sem.at[0]),
        pltpu.make_async_copy(state_hbm, u.at[0:3, 1:nz + 1, own], in_sem.at[1]),
        pltpu.make_async_copy(pore_hbm, poreb, in_sem.at[2]),
        pltpu.make_async_copy(rhs_hbm, rhs, in_sem.at[3]),
        pltpu.make_async_copy(facies_hbm, facies, in_sem.at[4]),
        pltpu.make_async_copy(mtab_hbm, mtab, in_sem.at[5]),
        pltpu.make_async_copy(ktab_hbm, ktab, in_sem.at[6]),
    ]
    for i in (4, 6, 5, 0, 1, 2, 3):
        loads[i].start()

    def zero(ref):
        ref[...] = jnp.zeros(ref.shape, ref.dtype)

    for cond, refs in (
        (iz == 0, [u.at[:, 0, own]]),
        (iz == ngz - 1, [u.at[:, nz + 1, own]]),
        (iy == 0, [yrecv.at[:, 0], cyrecv.at[0]]),
        (iy == ngy - 1, [yrecv.at[:, 1], cyrecv.at[1]]),
        (ix == 0, [xrecv.at[:, 0], cxrecv.at[0]]),
        (ix == ngx - 1, [xrecv.at[:, 1], cxrecv.at[1]]),
        (jnp.logical_or(iy == 0, ix == 0), [cdrecv.at[0]]),
        (jnp.logical_or(iy == 0, ix == ngx - 1), [cdrecv.at[1]]),
        (jnp.logical_or(iy == ngy - 1, ix == 0), [cdrecv.at[2]]),
        (jnp.logical_or(iy == ngy - 1, ix == ngx - 1), [cdrecv.at[3]]),
    ):
        @pl.when(cond)
        def _(refs=refs):
            for ref in refs:
                zero(ref)
    zero(field)
    for z in range(nz):
        zero(pcb.at[z, HALO + ny:])
    zero(shifted.at[:, 0:HALO])

    for i in (4, 6, 5):
        loads[i].wait()

    def coefficient(table, z, r, c):
        return table[r, facies[z], c]

    lane8 = lax.broadcasted_iota(jnp.int32, (HALO, nx), 1)
    row8 = lax.broadcasted_iota(jnp.int32, (HALO, nx), 0)
    pair8 = lax.shift_right_logical(lane8, 1)
    even8 = lax.rem(lane8, 2) == 0
    first8, last8 = lane8 == 0, lane8 == nx - 1
    nil8 = jnp.zeros((HALO, nx), f32)
    group8 = lax.shift_right_logical(lane8, 4)
    in16 = lax.rem(lane8, 2 * HALO)
    left_part = in16 < HALO

    def packed_columns(values):
        out = [nil8] * xtiles
        for z, g, x in values:
            place = (g % per) * nz + z
            out[g // per] = jnp.where(pair8 == place, pltpu.roll(x, 2 * place + 1, 1), out[g // per])
        return out

    def swapped(x):
        return jnp.where(even8, pltpu.roll(x, nx - 1, 1), pltpu.roll(x, 1, 1))

    loads[0].wait()
    values = []
    for z in range(nz):
        r = 0.5 / permb[z].astype(f32)
        u[3, z + 1, own, :] = r
        for side, at_row in ((0, 0), (1, ny - 1)):
            ysend[0, side, nz + z:nz + z + 1, :] = r[at_row:at_row + 1]
        values += [(z, g, r[g * HALO:(g + 1) * HALO]) for g in range(groups)]
    packed = packed_columns(values)
    for t in range(xtiles):
        xsend[0, 1, t] = packed[t]

    loads[1].wait()
    values = []
    for z in range(nz):
        k0 = [coefficient(ktab, z, 0, k) for k in range(3)]
        pc = k0[0] * u[0, z + 1, own, :] + k0[1] * u[1, z + 1, own, :] + k0[2] * u[2, z + 1, own, :]
        pcb[z, own, :] = pc
        for side, at_row in ((0, 0), (1, ny - 1)):
            ysend[0, side, z:z + 1, :] = pc[at_row:at_row + 1]
        values += [(z, g, pc[g * HALO:(g + 1) * HALO]) for g in range(groups)]
    packed = packed_columns(values)
    for t in range(xtiles):
        xsend[0, 0, t] = packed[t]

    beside_y = exists(-1, 0).astype(jnp.int32) + exists(1, 0).astype(jnp.int32)
    beside_x = exists(0, -1).astype(jnp.int32) + exists(0, 1).astype(jnp.int32)
    pl.semaphore_wait(barrier, beside_y + beside_x + (ngz - 1))

    def remote(src, dst, send, recv, device):
        return pltpu.make_async_remote_copy(src_ref=src, dst_ref=dst, send_sem=send, recv_sem=recv,
                                            device_id=device, device_id_type=MESH)

    def start(copies):
        for sends, copy in copies:
            @pl.when(sends)
            def _(copy=copy):
                copy.start()

    def y_copies(batch):
        s = send_y, h_recv.at[1 + batch]
        return [(exists(1, 0), remote(ysend.at[batch, 1], yrecv.at[batch, 0], *s, at(1, 0))),
                (exists(-1, 0), remote(ysend.at[batch, 0], yrecv.at[batch, 1], *s, at(-1, 0)))]

    def x_copies(batch):
        s = send_x, h_recv.at[3 + batch]
        return [(exists(0, 1), remote(xsend.at[batch], xrecv.at[batch, 0], *s, at(0, 1))),
                (exists(0, -1), remote(xsend.at[batch], xrecv.at[batch, 1], *s, at(0, -1)))]

    def z_device(d):
        return {"gx": ix, "gy": iy, "gz": iz + d}

    z_up = remote(u.at[:, nz, own], u.at[:, 0, own], send_z, h_recv.at[0], z_device(1))
    z_down = remote(u.at[:, 1, own], u.at[:, nz + 1, own], send_z, h_recv.at[0], z_device(-1))
    has_below, has_above = iz > 0, iz < ngz - 1

    start(y_copies(0))
    start(x_copies(0))
    start([(has_above, z_up), (has_below, z_down)])
    for n, dy in ((1, -1), (0, 1)):
        @pl.when(exists(dy, 0))
        def _(n=n, dy=dy):
            pl.semaphore_signal(near.at[n], inc=1, device_id=at(dy, 0), device_id_type=MESH)
    signal_peers(near.at[2])

    def counted(count, cases, descriptor, done):
        for n, ref in cases:
            @pl.when(count == n)
            def _(ref=ref):
                done(descriptor(ref))

    def wait_many(count, cases, send, recv, sent):
        counted(count, cases, lambda ref: remote(ref, ref, send, recv, z_device(0)),
                (lambda c: c.wait_send()) if sent else (lambda c: c.wait_recv()))

    def wait_y(batch):
        wait_many(beside_y, ((1, yrecv.at[batch, 0]), (2, yrecv.at[batch])), send_y, h_recv.at[1 + batch], False)

    def wait_x(batch):
        wait_many(beside_x, ((1, xrecv.at[batch, 0]), (2, xrecv.at[batch])), send_x, h_recv.at[3 + batch], False)

    beside_z = has_below.astype(jnp.int32) + has_above.astype(jnp.int32)
    z_cases = ((1, u.at[:, 1, own]), (2, u.at[:, 1:3, own]))

    for i in range(2):
        values = []
        for z in range(nz):
            c = u[1 + i, z + 1, own, :]
            for side, at_row in ((0, 0), (1, ny - 1)):
                ysend[1, side, i * nz + z:i * nz + z + 1, :] = c[at_row:at_row + 1]
            values += [(z, g, c[g * HALO:(g + 1) * HALO]) for g in range(groups)]
        packed = packed_columns(values)
        for t in range(xtiles):
            xsend[1, i, t] = packed[t]
    start(x_copies(1))
    start(y_copies(1))
    for i in range(2):
        here, swap = nil8, nil8
        for side in range(2):
            for k in range(layers):
                rows = slice(i * nz + k * HALO, i * nz + (k + 1) * HALO)
                for other in range(2):
                    slot = (side if not other else 1 - side) * layers + k
                    moved = pltpu.roll(ysend[0, side, rows, :], (2 * HALO * slot + HALO) % nx, 1)
                    if other:
                        swap = jnp.where(group8 == slot, moved, swap)
                    else:
                        here = jnp.where(group8 == slot, moved, here)
        rpsend[i] = here
        for side, g in ends:
            dsend[side, i] = swap
            dsend[side, 2 + i] = xsend[0, i, g // per]

    def ways(dy, dx, copy):
        @pl.when(exists(dy, dx))
        def _():
            copy.start()

    for dx in (-1, 1):
        ways(0, dx, remote(rpsend, cxrecv.at[(1 - dx) // 2, ngz * nstrips:], send_cx, h_recv.at[5], at(0, dx)))
    for dy in (-1, 1):
        ways(dy, 0, remote(dsend.at[(1 + dy) // 2, 2:], cyrecv.at[(1 - dy) // 2, ngz * PLANES:], send_cy, h_recv.at[5], at(dy, 0)))

    def raw_corners(dy):
        @pl.when(exists(dy, 0))
        def _():
            pl.semaphore_wait(near.at[(1 + dy) // 2], 1)
        for dx in (-1, 1):
            ways(dy, dx, remote(dsend.at[(1 + dy) // 2], cdrecv.at[(1 - dy) + (1 - dx) // 2, ngz:], send_cd, h_recv.at[6],
                                at(dy, dx)))


    layer_of_lane = lax.rem(lane8[0:1], 2 * nz) // 2
    lanek = [jnp.zeros((1, nx), f32) for _ in range(3)]
    for z in range(nz):
        for k in range(3):
            value = coefficient(ktab, z, 0, k)
            rowk[k, z:z + 1, :] = jnp.full((1, nx), value, f32)
            lanek[k] = jnp.where(layer_of_lane == z, value, lanek[k])
    loads[2].wait()
    loads[3].wait()

    raw_corners(-1)

    for f in range(ktab.shape[1]):
        values = block_scalars([[mtab[r, f, c] for c in range(3)] for r in range(3)],
                               [[ktab[r, f, c] for c in range(3)] for r in range(3)])
        for i, value in enumerate(values):
            ctab[i, f] = value

    def tile_of(g):
        return slice(g * HALO, (g + 1) * HALO)

    def padded(g, shift):
        return slice(HALO + g * HALO + shift, HALO + (g + 1) * HALO + shift)

    def assemble(z, carry, upper=True):
        s_res, s_dia, s_ty, s_tx, s_hx, s_hy, s_z = (list(c) for c in carry)
        volume = poreb[z].astype(f32)
        k00 = coefficient(ktab, z, 0, 0)
        m0 = [coefficient(mtab, z, 0, k) for k in range(3)]
        if upper:
            dk = [coefficient(ktab, z, 0, k) - coefficient(ktab, z + 1, 0, k) for k in range(3)]
        for g in range(groups):
            rows = padded(g, 0)
            r = u[3, z + 1, rows, :]
            typ = 1.0 / (r + u[3, z + 1, padded(g, 1), :])
            if g == groups - 1:
                typ = jnp.where(row8 < HALO - 1, typ, 0.0)
            xp = jnp.where(last8, 0.0, 1.0 / (r + pltpu.roll(r, nx - 1, 1)))
            ty[z, rows, :] = typ
            txp[z, tile_of(g), :] = xp
            pc = pcb[z, rows, :]
            s_hx[g] = s_hx[g] + xp * (pc - pltpu.roll(pc, nx - 1, 1))
            s_hy[g] = s_hy[g] + typ * (pc - pcb[z, padded(g, 1), :])
            v = volume[tile_of(g)]
            c = [u[k, z + 1, rows, :] for k in range(3)]
            s_res[g] = s_res[g] + (rhs[0, z, tile_of(g), :] - v * (m0[0] * c[0] + m0[1] * c[1] + m0[2] * c[2]))
            s_dia[g] = s_dia[g] + v * m0[0]
            s_ty[g] = s_ty[g] + k00 * typ
            s_tx[g] = s_tx[g] + k00 * xp
            if upper:
                t = 1.0 / (r + u[3, z + 2, rows, :])
                tzf[z + 1, tile_of(g), :] = t
                d = [c[k] - u[k, z + 2, rows, :] for k in range(3)]
                s_z[g] = s_z[g] + t * (dk[0] * d[0] + dk[1] * d[1] + dk[2] * d[2])
        return tuple(tuple(s) for s in (s_res, s_dia, s_ty, s_tx, s_hx, s_hy, s_z))

    carry = ((nil8,) * groups,) * 7
    trips = (nz - 1) // 2

    def two(i, carry):
        return assemble(2 * i + 1, assemble(2 * i, carry))

    carry = lax.fori_loop(0, trips, two, carry)
    for z in range(2 * trips, nz):
        carry = assemble(z, carry, upper=z < nz - 1)
    s_res, s_dia, s_ty, s_tx, s_hx, s_hy, s_z = (list(c) for c in carry)

    for g in range(groups):
        shifted[0, padded(g, 0), :] = s_hy[g]
        shifted[1, padded(g, 0), :] = s_ty[g]
    p_rhs, p_dia = [], []
    for g in range(groups):
        p_rhs.append(s_res[g] - s_z[g] - (s_hx[g] - pltpu.roll(s_hx[g], 1, 1)) - (s_hy[g] - shifted[0, padded(g, -1), :]))
        p_dia.append(s_dia[g] + s_ty[g] + shifted[1, padded(g, -1), :] + s_tx[g] + pltpu.roll(s_tx[g], 1, 1))

    wait_many(beside_z, z_cases, send_z, h_recv.at[0], False)
    for slot, z, inside in ((0, 0, 1), (nz + 1, nz - 1, nz)):
        k0 = [coefficient(ktab, z, 0, k) for k in range(3)]
        for g in range(groups):
            rows = padded(g, 0)
            there = u[3, slot, rows, :]
            t = jnp.where(there > 0.0, 1.0 / (u[3, inside, rows, :] + there), 0.0)
            tzf[0 if slot == 0 else nz, tile_of(g), :] = t
            d = [u[k, inside, rows, :] - u[k, slot, rows, :] for k in range(3)]
            p_rhs[g] = p_rhs[g] - t * (k0[0] * d[0] + k0[1] * d[1] + k0[2] * d[2])
    mine = [[swapped(xsend[0, i, t]) for t in range(xtiles)] for i in range(2)]
    raw_corners(1)
    pl.semaphore_wait(near.at[2], ngz - 1)
    signal_peers(far_sem)

    planes = [p_rhs, p_dia, s_ty, s_tx]
    for p in range(PLANES):
        ystrips[0, p] = planes[p][0]
        ystrips[1, p] = planes[p][groups - 1]
    for i, tiles in enumerate(packing):
        strip = nil8
        for j, g in enumerate(tiles):
            for p in range(PLANES):
                slot = j * PLANES + p
                strip = jnp.where(group8 == slot, pltpu.roll(planes[p][g], (2 * HALO * slot + HALO) % nx, 1), strip)
        strips[i] = strip

    pl.semaphore_wait(far_sem, ngz - 1)

    def to_all(dy, dx, src, dst, send, recv):
        return [(exists(dy, dx), remote(src, dst, send, c_recv.at[recv],
                                        {"gx": ix + dx, "gy": iy + dy, "gz": lax.rem(iz + d, ngz)})) for d in range(ngz)]

    for dy, dx in SIDES[4:]:
        start(to_all(dy, dx, strips.at[0 if dy < 0 else last_head], cdrecv.at[(1 - dy) + (1 - dx) // 2, iz], send_cd, 3))
    for dx in (-1, 1):
        start(to_all(0, dx, strips, cxrecv.at[(1 - dx) // 2, pl.ds(iz * nstrips, nstrips)], send_cx, 2))
    for dy in (-1, 1):
        start(to_all(dy, 0, ystrips.at[(1 + dy) // 2], cyrecv.at[(1 - dy) // 2, pl.ds(iz * PLANES, PLANES)], send_cy, 1))

    wait_y(0)
    top8, bottom8 = row8 == 0, row8 == HALO - 1
    lines = nil8
    y_faces = []
    for side, g, here in ((0, 0, top8), (1, groups - 1, bottom8)):
        there = yrecv[0, side, nz:, :]
        t = jnp.where(there > 0.0, 1.0 / (ysend[0, side, nz:, :] + there), 0.0)
        moved = jnp.sum(t * (ysend[0, side, :nz, :] - yrecv[0, side, :nz, :]), axis=0, keepdims=True)
        weight = jnp.sum(rowk[0] * t, axis=0, keepdims=True)
        lines = jnp.where(row8 == 2 * side, moved, jnp.where(row8 == 2 * side + 1, weight, lines))
        y_faces.append((side, g, here, t, moved, weight))
    wait_x(0)
    flux, weights, faces, outside = [], [], [], []
    for t in range(xtiles):
        there = [jnp.where(even8, xrecv[0, 0, i, t], xrecv[0, 1, i, t]) for i in range(2)]
        face = jnp.where(there[1] > 0.0, 1.0 / (mine[1][t] + there[1]), 0.0)
        flux.append(face * (mine[0][t] - there[0]))
        weights.append(face * lanek[0])
        faces.append(face)
        outside.append(there[0])

    def sums_of(flux, weights, low):
        block = jnp.logical_and(lane8 >= low, lane8 < low + 2 * nz)
        sums = []
        for values in (flux, weights):
            for parity in (even8, jnp.logical_not(even8)):
                sums.append(jnp.sum(jnp.where(jnp.logical_and(block, parity), values, 0.0), axis=1, keepdims=True))
        return sums

    def lanes_of(g):
        return (g % per) * 2 * nz

    def at_sides(left, right):
        return jnp.where(first8, left, jnp.where(last8, right, 0.0))

    for side, g, here, t, moved, weight in y_faces:
        for p, change in ((0, -moved), (1, weight), (2, weight))[:3 if side else 2]:
            planes[p][g] = planes[p][g] + jnp.where(here, change, 0.0)
        for z in range(nz):
            edge_row = HALO - 1 + side * ny
            ty[z, edge_row:edge_row + 1, :] = t[z:z + 1]
    zplanes[iz, PLANES * groups] = lines
    for i, tiles in enumerate(packing):
        across = nil8
        for j, g in enumerate(tiles):
            flux_l, flux_r, weight_l, weight_r = sums_of(flux[g // per], weights[g // per], lanes_of(g))
            for p, change in ((0, at_sides(-flux_l, -flux_r)), (1, at_sides(weight_l, weight_r)),
                              (3, jnp.where(last8, weight_r, 0.0))):
                planes[p][g] = planes[p][g] + change
            for p, left, right in ((0, flux_l, flux_r), (1, weight_l, weight_r), (3, weight_l, 0.0)):
                slot = (j * PLANES + p) * 2 * HALO
                across = jnp.where(lane8 == slot + HALO - 1, left, jnp.where(lane8 == slot + HALO, right, across))
        zplanes[iz, PLANES * groups + 1 + i] = across
    for p in range(PLANES):
        for g in range(groups):
            zplanes[iz, p * groups + g] = planes[p][g]
    for d in range(1, ngz):
        remote(zplanes.at[iz, 0:first_part], zplanes.at[iz, 0:first_part], send_cz, c_recv.at[0],
               {"gx": ix, "gy": iy, "gz": lax.rem(iz + d, ngz)}).start()

    wait_y(1)
    wait_x(1)
    invrow = 1.0 / rowk[0]
    for side, at_row in ((0, HALO - 1), (1, HALO + ny)):
        one, two_ = yrecv[1, side, :nz, :], yrecv[1, side, nz:, :]
        zero_ = (yrecv[0, side, :nz, :] - rowk[1] * one - rowk[2] * two_) * invrow
        for z in range(nz):
            for k, x in enumerate((zero_, one, two_)):
                u[k, z + 1, at_row:at_row + 1, :] = x[z:z + 1]
    invlane = 1.0 / lanek[0]
    for t in range(xtiles):
        one, two_ = (jnp.where(even8, xrecv[1, 0, i, t], xrecv[1, 1, i, t]) for i in range(2))
        zero_ = (outside[t] - lanek[1] * one - lanek[2] * two_) * invlane
        for k, x in enumerate((zero_, one, two_)):
            edge[k, t] = swapped(faces[t] * x)
        edge[3, t] = swapped(faces[t])

    outer8 = jnp.logical_or(first8, last8)

    def solve(z, _):
        volume = poreb[z].astype(f32)
        f = facies[z]
        kinv = [[ctab[KINV + 3 * r + c, f] for c in range(3)] for r in range(3)]
        n = [[ctab[NMAT + 3 * r + c, f] for c in range(3)] for r in range(3)]
        adj = [[ctab[NADJ + 3 * r + c, f] for c in range(3)] for r in range(3)]
        dia = [ctab[NDIA + i, f] for i in range(3)]
        trace, minors, det_n = ctab[NTR, f], ctab[NC2, f], ctab[NDET, f]
        for g in range(groups):
            rows = padded(g, 0)
            tile = tile_of(g)
            shift = lax.rem(2 * nx - (2 * nz * (g % per) + 1) - 2 * z, nx)
            lateral = [jnp.where(outer8, pltpu.roll(edge[k, g // per], shift, 1), 0.0) for k in range(4)]
            tzm, tzp = tzf[z, tile, :], tzf[z + 1, tile, :]
            typ, tym = ty[z, rows, :], ty[z, padded(g, -1), :]
            xp = txp[z, tile, :]
            xm = pltpu.roll(xp, 1, 1)
            tz = tzm + tzp
            tzs[z, tile, :] = tz
            total = tz + (typ + tym) + (xp + xm) + lateral[3]
            txp[z, tile, :] = xp + jnp.where(last8, lateral[3], 0.0)
            txm[z, tile, :] = xm + jnp.where(first8, lateral[3], 0.0)
            near = []
            for k in range(3):
                c = u[k, z + 1, rows, :]
                near.append(tzp * u[k, z + 2, rows, :] + tzm * u[k, z, rows, :]
                            + typ * u[k, z + 1, padded(g, 1), :] + tym * u[k, z + 1, padded(g, -1), :]
                            + xp * pltpu.roll(c, nx - 1, 1) + xm * pltpu.roll(c, 1, 1) + lateral[k])
            given = [rhs[k, z, tile, :] for k in range(3)]
            b = [near[r] + kinv[r][0] * given[0] + kinv[r][1] * given[1] + kinv[r][2] * given[2] for r in range(3)]
            v = volume[tile]
            s = total * (1.0 / v)
            e = [[s * (s + dia[r]) + adj[r][r] if r == c else adj[r][c] - s * n[r][c] for c in range(3)] for r in range(3)]
            det = ((s + trace) * s + minors) * s + det_n
            inv = 1.0 / (v * det)
            for r in range(3):
                w[r, z, tile, :] = (e[r][0] * b[0] + e[r][1] * b[1] + e[r][2] * b[2]) * inv
                qv[r, z, tile, :] = e[r][0] * inv
        return 0

    def solve_part(begin, end):
        def solve_two(i, carry):
            return solve(begin + 2 * i + 1, solve(begin + 2 * i, carry))

        lax.fori_loop(0, (end - begin) // 2, solve_two, 0)
        if (end - begin) % 2:
            solve(end - 1, 0)

    solve_part(0, nz // 2)

    corners = beside_y * beside_x
    wait_many(beside_y + beside_x, [(n, zplanes.at[0, 0:2 * n]) for n in range(1, 5)], send_cx, h_recv.at[5], False)
    wait_many(corners, ((1, cdrecv.at[0, ngz:]), (2, cdrecv.at[0:2, ngz:]), (4, cdrecv.at[:, ngz:])), send_cd, h_recv.at[6], False)
    from_top = group8 < layers
    ours, theirs = [], []
    for i in range(2):
        ours.append(jnp.where(left_part, cxrecv[0, ngz * nstrips + i], cxrecv[1, ngz * nstrips + i]))
        theirs.append(jnp.where(from_top, jnp.where(left_part, cdrecv[0, ngz + i], cdrecv[1, ngz + i]),
                                jnp.where(left_part, cdrecv[2, ngz + i], cdrecv[3, ngz + i])))
    t = jnp.where(theirs[1] > 0.0, 1.0 / (ours[1] + theirs[1]), 0.0)
    pattern = nil8
    for k in range(layers):
        pattern = jnp.where(lax.rem(group8, layers) == k, rowk[0, k * HALO:(k + 1) * HALO, :], pattern)
    both = jnp.where(top8, jnp.sum(t * (ours[0] - theirs[0]), axis=0, keepdims=True),
                     jnp.sum(t * pattern, axis=0, keepdims=True))
    summed = both
    for k in range(1, layers):
        summed = summed + pltpu.roll(both, nx - 2 * HALO * k, 1)
    upper = pltpu.roll(summed, nx - HALO, 1)
    lower = pltpu.roll(summed, (2 * nx - 2 * HALO * layers - HALO) % nx, 1)
    zplanes[iz, first_part] = jnp.where(row8 < 2, upper, pltpu.roll(lower, 2, 0))
    for side, g in ends:
        tiles = [swapped(cyrecv[side, ngz * PLANES + i]) for i in range(2)]
        there = [jnp.where(even8, cdrecv[2 * side, ngz + 2 + i], cdrecv[2 * side + 1, ngz + 2 + i]) for i in range(2)]
        face = jnp.where(there[1] > 0.0, 1.0 / (tiles[1] + there[1]), 0.0)
        flux_l, flux_r, weight_l, weight_r = sums_of(face * (tiles[0] - there[0]), face * lanek[0], lanes_of(ends[1 - side][1]))
        for n, tile in enumerate((at_sides(-flux_l, -flux_r), at_sides(weight_l, weight_r),
                                  at_sides(flux_r, flux_l), at_sides(weight_r, weight_l))):
            zplanes[iz, first_part + 1 + 4 * side + n] = tile
    for d in range(1, ngz):
        remote(zplanes.at[iz, first_part:], zplanes.at[iz, first_part:], send_cz, c_recv.at[4],
               {"gx": ix, "gy": iy, "gz": lax.rem(iz + d, ngz)}).start()
    solve_part(nz // 2, nz)

    if ngz > 1:
        others = zplanes.at[0:ngz - 1, 0:first_part]
        remote(others, others, send_cz, c_recv.at[0], z_device(0)).wait_recv()
    y_early, x_early = slice(0, ngz * PLANES), slice(0, ngz * nstrips)
    wait_many(beside_y, ((1, cyrecv.at[0, y_early]), (2, cyrecv.at[:, y_early])), send_cy, c_recv.at[1], False)
    wait_many(beside_x, ((1, cxrecv.at[0, x_early]), (2, cxrecv.at[:, x_early])), send_cx, c_recv.at[2], False)
    wait_many(corners, ((1, cdrecv.at[0, 0:ngz]), (2, cdrecv.at[0:2, 0:ngz]), (4, cdrecv.at[:, 0:ngz])), send_cd, c_recv.at[3], False)

    def gathered(part):
        total = part(0)
        for i in range(1, ngz):
            total = total + part(i)
        return total

    tiles_in = groups + 2
    side_tiles = [jnp.where(left_part, gathered(lambda i: cxrecv[0, i * nstrips + t]), gathered(lambda i: cxrecv[1, i * nstrips + t]))
                  + gathered(lambda i: zplanes[i, PLANES * groups + 1 + t]) for t in range(nstrips)]
    corner_tiles = [jnp.where(left_part, gathered(lambda i: cdrecv[2 * v, i]), gathered(lambda i: cdrecv[2 * v + 1, i]))
                    for v in range(2)]
    where_is = {g: (i, j) for i, tiles in enumerate(packing) for j, g in enumerate(tiles)}
    on_right, on_left = lane8 < HALO, lane8 >= nx - HALO
    strip8 = jnp.logical_or(on_right, on_left)

    def border_of(p, g):
        if 0 <= g < groups:
            i, j = where_is[g]
            tile, slot = side_tiles[i], j * PLANES + p
        else:
            tile, slot = corner_tiles[0 if g < 0 else 1], p
        return jnp.where(strip8, pltpu.roll(tile, (2 * nx - 2 * HALO * slot - HALO) % nx, 1), 0.0)

    b = [[border_of(p, g) for g in range(-1, groups + 1)] for p in range(PLANES)]
    own_lines = gathered(lambda i: zplanes[i, PLANES * groups])
    a = [[gathered(lambda i: cyrecv[0, i * PLANES + p])] + [gathered(lambda i: zplanes[i, p * groups + g]) for g in range(groups)]
         + [gathered(lambda i: cyrecv[1, i * PLANES + p])] for p in range(PLANES)]

    def beyond(grid, lines):
        for side, t, here in ((0, 0, bottom8), (1, tiles_in - 1, top8)):
            moved, weight = lines[2 * side:2 * side + 1], lines[2 * side + 1:2 * side + 2]
            for p, change in ((0, moved), (1, weight), (2, weight))[:2 if side else 3]:
                grid[p][t] = grid[p][t] + jnp.where(here, change, 0.0)

    beyond(a, own_lines)

    def east(ra, rb):
        return jnp.where(last8, rb, ra), jnp.where(last8, ra, rb)

    def west(ra, rb):
        return jnp.where(first8, rb, ra), jnp.where(first8, ra, rb)

    def fill(buffer, s, tiles):
        for t in range(tiles_in):
            field[buffer, s, (t + 1) * HALO:(t + 2) * HALO, :] = tiles[t]

    def above(buffer, s, t):
        return field[buffer, s, (t + 1) * HALO - 1:(t + 2) * HALO - 1, :]

    def below(buffer, s, t):
        return field[buffer, s, (t + 1) * HALO + 1:(t + 2) * HALO + 1, :]

    terms = [[None] * tiles_in for _ in range(2)]
    grids = (a, b)

    def prepare(s, t):
        rhs_, dia, down, right = (grids[s][p][t] for p in range(PLANES))
        there = dia > 0.0
        inv = jnp.where(there, RELAX / jnp.where(there, dia, 1.0), 0.0)
        left = west(*(pltpu.roll(grid[3][t], 1, 1) for grid in grids))[s]
        terms[s][t] = [rhs_ * inv, down * inv, above(0, s, t) * inv, right * inv, left * inv]

    fill(0, 0, a[2])
    late_b = (0, 1, groups, groups + 1)
    for t in range(1, tiles_in - 1):
        prepare(0, t)

    if ngz > 1:
        rest = zplanes.at[0:ngz - 1, first_part:]
        remote(rest, rest, send_cz, c_recv.at[4], z_device(0)).wait_recv()
    lines = jnp.where(strip8, gathered(lambda i: zplanes[i, first_part]), 0.0)
    beyond(b, lines)
    for side, t, here in ((0, 1, top8), (1, groups, bottom8)):
        moved, weight = lines[2 * side:2 * side + 1], lines[2 * side + 1:2 * side + 2]
        for p, change in ((0, -moved), (1, weight), (2, weight))[:3 if side else 2]:
            b[p][t] = b[p][t] + jnp.where(here, change, 0.0)
    fill(0, 1, b[2])
    for t in range(1, tiles_in - 1):
        prepare(1, t)
    for side, t in ((0, 0), (1, tiles_in - 1)):
        flux_, weight_, flux_past, weight_past = (
            gathered(lambda i: zplanes[i, first_part + 1 + 4 * side + n]) for n in range(4))
        for grid, change, weight in ((a, flux_, weight_), (b, flux_past, weight_past)):
            grid[0][t] = grid[0][t] + change
            grid[1][t] = grid[1][t] + weight
            grid[3][t] = grid[3][t] + jnp.where(last8, weight, 0.0)
        for s in range(2):
            prepare(s, t)

    c = [[terms[s][t][0] for t in range(tiles_in)] for s in range(2)]
    for sweep in range(1, SWEEPS):
        buffer = sweep % 2
        for s in range(2):
            fill(buffer, s, c[s])
        nxt = [[None] * tiles_in for _ in range(2)]
        for t in range(tiles_in):
            e = east(*(pltpu.roll(c[s][t], nx - 1, 1) for s in range(2)))
            ws = west(*(pltpu.roll(c[s][t], 1, 1) for s in range(2)))
            for s in range(2):
                r, tyn, tys, txe, txw = terms[s][t]
                nxt[s][t] = (((1.0 - RELAX) * c[s][t] + r) + (tyn * below(buffer, s, t) + tys * above(buffer, s, t))
                             + (txe * e[s] + txw * ws[s]))
        c = nxt
    for t in range(tiles_in):
        rows = slice(t * HALO, (t + 1) * HALO)
        final[0, rows, :] = c[0][t]
        if 0 < t < tiles_in - 1:
            final[1, rows, :] = east(*(pltpu.roll(c[s][t], nx - 1, 1) for s in range(2)))[0]
            final[2, rows, :] = west(*(pltpu.roll(c[s][t], 1, 1) for s in range(2)))[0]
    for count, cases, sem in (
        (beside_y, ((1, yrecv.at[0]), (2, yrecv)), send_y),
        (beside_x, ((1, xrecv.at[0]), (2, xrecv)), send_x),
        (beside_z, z_cases, send_z),
        (beside_y, ((1, cyrecv.at[0]), (2, cyrecv)), send_cy),
        (beside_x, ((1, cxrecv.at[0]), (2, cxrecv)), send_cx),
        (corners, ((1, cdrecv.at[0]), (2, cdrecv.at[0:2]), (4, cdrecv)), send_cd),
    ):
        wait_many(count, cases, sem, h_recv.at[0], True)
    if ngz > 1:
        others = zplanes.at[0:ngz - 1]
        remote(others, others, send_cz, c_recv.at[0], z_device(0)).wait_send()


def finish_kernel(parts, w, qv, tzs, ty, txp, txm, final, new_hbm, corr_hbm, out, out_sem):
    nz, ny, nx = tzs.shape
    own = slice(HALO, HALO + ny)
    corr = pltpu.make_async_copy(final.at[0, own], corr_hbm, out_sem.at[parts])
    corr.start()
    cc, ce, cw = (final[k, own, :] for k in range(3))
    cn, cs = final[0, HALO + 1:HALO + 1 + ny, :], final[0, HALO - 1:HALO - 1 + ny, :]

    def finish(z, _):
        g = (tzs[z] * cc + ty[z, own, :] * cn + ty[z, HALO - 1:HALO + ny - 1, :] * cs
             + txp[z] * ce + txm[z] * cw)
        for r in range(3):
            out[r, z] = w[r, z] + qv[r, z] * g
        return 0

    step = nz // parts
    outs = [corr]
    for part in range(parts):
        lax.fori_loop(part * step, (part + 1) * step, finish, 0)
        chunk = slice(part * step, (part + 1) * step)
        outs.append(pltpu.make_async_copy(out.at[:, chunk], new_hbm.at[:, chunk], out_sem.at[part]))
        outs[-1].start()
    for copy in outs:
        copy.wait()


def per_device(sizes, state, right_side, permeability, pore_volume, facies, storage_table, coupling_table):
    _, nz, ny, nx = state.shape
    sizes = sizes + (nz, ny, nx)
    f32 = jnp.float32
    ngz = sizes[2]
    cells = (nz, ny, nx)
    vmem = lambda *shape: pltpu.VMEM(shape, f32)
    hbm = pl.BlockSpec(memory_space=pltpu.HBM)
    dma = lambda n: pltpu.SemaphoreType.DMA((n,))
    ey = ny + 2 * HALO
    groups, per, xtiles = column_plan(nz, ny, nx)
    strips = len(strip_plan(ny, nx))
    facets = storage_table.shape[0]
    in_vmem = pl.BlockSpec(memory_space=pltpu.VMEM)
    handed = 4 * nx * (9 * nz * ny + nz * ey + 3 * ey)
    limit = 16384 * ((VMEM_BYTES - handed) // 16384)
    middle = pl.pallas_call(
        functools.partial(kernel, sizes),
        out_shape=(vmem(3, *cells), vmem(3, *cells), vmem(*cells), vmem(nz, ey, nx), vmem(*cells), vmem(*cells),
                   vmem(3, ey, nx)),
        in_specs=[hbm, hbm, hbm, hbm, hbm, hbm, hbm],
        out_specs=(in_vmem,) * 7,
        scratch_shapes=[
            vmem(4, nz + 2, ey, nx), vmem(nz, ey, nx), vmem(3, *cells),
            pltpu.VMEM(cells, permeability.dtype), pltpu.VMEM(cells, pore_volume.dtype),
            vmem(2, 2, 2 * nz, nx), vmem(2, 2, 2 * nz, nx),
            vmem(2, 2, xtiles, HALO, nx), vmem(2, 2, 2, xtiles, HALO, nx), vmem(4, xtiles, HALO, nx),
            vmem(3, nz, nx), vmem(nz + 1, ny, nx), vmem(2, ey, nx),
            vmem(ngz, PLANES * groups + 1 + strips + 9, HALO, nx), vmem(2, PLANES, HALO, nx), vmem(strips, HALO, nx),
            vmem(2, ngz * PLANES + 2, HALO, nx), vmem(2, ngz * strips + 2, HALO, nx), vmem(4, ngz + 4, HALO, nx),
            vmem(2, HALO, nx), vmem(2, 4, HALO, nx), vmem(2, 2, ey + 2 * HALO, nx),
            pltpu.SMEM((nz,), facies.dtype), pltpu.SMEM((3, facets, 3), f32), pltpu.SMEM((3, facets, 3), f32),
            pltpu.SMEM((NCOEF, facets), f32),
            pltpu.SemaphoreType.REGULAR((3,)), pltpu.SemaphoreType.REGULAR, dma(7), dma(7), dma(5),
        ],
        compiler_params=pltpu.CompilerParams(collective_id=0, has_side_effects=True, vmem_limit_bytes=limit),
        name="cpr_apply",
    )(facies, storage_table.transpose(1, 0, 2), coupling_table.transpose(1, 0, 2),
      state, right_side, permeability, pore_volume)
    parts = 8 if nz % 8 == 0 else 1
    return tuple(pl.pallas_call(
        functools.partial(finish_kernel, parts),
        out_shape=(jax.ShapeDtypeStruct(state.shape, f32), jax.ShapeDtypeStruct((ny, nx), f32)),
        in_specs=[in_vmem] * 7,
        out_specs=(hbm, hbm),
        scratch_shapes=[vmem(3, *cells), dma(parts + 1)],
        compiler_params=pltpu.CompilerParams(vmem_limit_bytes=16 * 2**20),
        name="cpr_finish",
    )(*middle))


def solution(mesh):
    sizes = (mesh.shape["gx"], mesh.shape["gy"], mesh.shape["gz"])
    return jax.shard_map(
        functools.partial(per_device, sizes),
        mesh=mesh,
        in_specs=(
            P(None, "gz", "gy", "gx"),
            P(None, "gz", "gy", "gx"),
            P("gz", "gy", "gx"),
            P("gz", "gy", "gx"),
            P("gz"),
            P(),
            P(),
        ),
        out_specs=(P(None, "gz", "gy", "gx"), P("gy", "gx")),
        check_vma=False,
    )
```

```python
import functools
import jax
import jax.numpy as jnp
from jax import lax
from jax.experimental import pallas as pl
from jax.experimental.pallas import tpu as pltpu
from jax.sharding import PartitionSpec as P

SWEEPS = 8
RELAX = 0.8
MESH = pl.DeviceIdType.MESH
HALO = 8
VMEM_BYTES = 67043328

PLANES = 4
SIDES = [(-1, 0), (1, 0), (0, -1), (0, 1), (-1, -1), (-1, 1), (1, -1), (1, 1)]

KINV, NMAT, NADJ, NDIA, NTR, NC2, NDET, NCOEF = 0, 9, 18, 27, 30, 31, 32, 33


def cofactor(e, r, c):
    return (e[(r + 1) % 3][(c + 1) % 3] * e[(r + 2) % 3][(c + 2) % 3]
            - e[(r + 1) % 3][(c + 2) % 3] * e[(r + 2) % 3][(c + 1) % 3])


def block_scalars(m, k):
    kf = [[cofactor(k, r, c) for c in range(3)] for r in range(3)]
    inv = 1.0 / (k[0][0] * kf[0][0] + k[0][1] * kf[0][1] + k[0][2] * kf[0][2])
    kinv = [[kf[c][r] * inv for c in range(3)] for r in range(3)]
    n = [[kinv[r][0] * m[0][c] + kinv[r][1] * m[1][c] + kinv[r][2] * m[2][c] for c in range(3)] for r in range(3)]
    nf = [[cofactor(n, r, c) for c in range(3)] for r in range(3)]
    trace = n[0][0] + n[1][1] + n[2][2]
    return ([kinv[r][c] for r in range(3) for c in range(3)] + [n[r][c] for r in range(3) for c in range(3)]
            + [nf[c][r] for r in range(3) for c in range(3)] + [trace - n[i][i] for i in range(3)]
            + [trace, nf[0][0] + nf[1][1] + nf[2][2], n[0][0] * nf[0][0] + n[0][1] * nf[0][1] + n[0][2] * nf[0][2]])


def column_plan(nz, ny, nx):
    groups = ny // HALO
    per = nx // (2 * nz)
    return groups, per, -(-groups // per)


def strip_plan(ny, nx):
    groups = ny // HALO
    per = nx // (2 * HALO * PLANES)
    heads = [0] if groups == 1 else [0, groups - 1]
    others = list(range(1, groups - 1))
    packed = [[head] + [others.pop(0) for _ in range(per - 1) if others] for head in heads]
    while others:
        packed.append([others.pop(0) for _ in range(per) if others])
    return packed


def kernel(sizes, facies_hbm, mtab_hbm, ktab_hbm, state_hbm, rhs_hbm, perm_hbm, pore_hbm,
           w, qv, tzs, ty, txp, txm, final,
           u, pcb, rhs, permb, poreb, ysend, yrecv, xsend, xrecv, edge, rowk, tzf, shifted,
           zplanes, ystrips, strips, cyrecv, cxrecv, cdrecv, rpsend, dsend, yedge, field,
           facies, mtab, ktab, ctab, near, far, in_sem, h_recv, c_recv):
    ngx, ngy, ngz, nz, ny, nx = sizes
    ix, iy, iz = lax.axis_index("gx"), lax.axis_index("gy"), lax.axis_index("gz")
    own = slice(HALO, HALO + ny)
    groups, per, xtiles = column_plan(nz, ny, nx)
    packing = strip_plan(ny, nx)
    nstrips = len(packing)
    last_head = len(packing[:2]) - 1
    layers = nz // HALO
    ends = ((0, 0), (1, groups - 1))
    first_part = PLANES * groups + 1 + nstrips
    raw_lane = nx - 4 * HALO * layers
    assert nz % HALO == 0 and raw_lane >= 2 * nz
    f32 = jnp.float32
    send_y, send_x, send_z, send_cy, send_cx, send_cd, send_cz = (in_sem.at[i] for i in (0, 1, 4, 5, 6, 2, 3))

    def exists(dy, dx):
        ok = None
        for d, i, n in ((dy, iy, ngy), (dx, ix, ngx)):
            if d:
                here = (i > 0) if d < 0 else (i < n - 1)
                ok = here if ok is None else jnp.logical_and(ok, here)
        return ok

    def at(dy, dx):
        return {"gx": ix + dx, "gy": iy + dy, "gz": iz}

    barrier = pltpu.get_barrier_semaphore()
    for side in (SIDES[0], SIDES[2], SIDES[1], SIDES[3]):
        @pl.when(exists(*side))
        def _(side=side):
            pl.semaphore_signal(barrier, inc=1, device_id=at(*side), device_id_type=MESH)

    def signal_peers(sem):
        for d in range(1, ngz):
            pl.semaphore_signal(sem, inc=1, device_id={"gx": ix, "gy": iy, "gz": lax.rem(iz + d, ngz)},
                                device_id_type=MESH)

    signal_peers(barrier)

    loads = [
        pltpu.make_async_copy(perm_hbm, permb, in_sem.at[0]),
        pltpu.make_async_copy(state_hbm, u.at[0:3, 1:nz + 1, own], in_sem.at[1]),
        pltpu.make_async_copy(pore_hbm, poreb, in_sem.at[2]),
        pltpu.make_async_copy(rhs_hbm, rhs, in_sem.at[3]),
        pltpu.make_async_copy(facies_hbm, facies, in_sem.at[4]),
        pltpu.make_async_copy(mtab_hbm, mtab, in_sem.at[5]),
        pltpu.make_async_copy(ktab_hbm, ktab, in_sem.at[6]),
    ]
    for i in (4, 6, 5, 0, 1, 2, 3):
        loads[i].start()

    def zero(ref):
        ref[...] = jnp.zeros(ref.shape, ref.dtype)

    for cond, refs in (
        (iz == 0, [u.at[:, 0, own]]),
        (iz == ngz - 1, [u.at[:, nz + 1, own]]),
        (iy == 0, [yrecv.at[:, 0], cyrecv.at[0]]),
        (iy == ngy - 1, [yrecv.at[:, 1], cyrecv.at[1]]),
        (ix == 0, [xrecv.at[:, 0], cxrecv.at[0]]),
        (ix == ngx - 1, [xrecv.at[:, 1], cxrecv.at[1]]),
        (jnp.logical_or(iy == 0, ix == 0), [cdrecv.at[0]]),
        (jnp.logical_or(iy == 0, ix == ngx - 1), [cdrecv.at[1]]),
        (jnp.logical_or(iy == ngy - 1, ix == 0), [cdrecv.at[2]]),
        (jnp.logical_or(iy == ngy - 1, ix == ngx - 1), [cdrecv.at[3]]),
    ):
        @pl.when(cond)
        def _(refs=refs):
            for ref in refs:
                zero(ref)
    zero(field)
    for z in range(nz):
        zero(pcb.at[z, HALO + ny:])
        zero(ty.at[z, 0:HALO])
        for k in range(3):
            zero(u.at[k, z + 1, 0:HALO])
            zero(u.at[k, z + 1, HALO + ny:])
    zero(shifted.at[:, 0:HALO])

    for i in (4, 6, 5):
        loads[i].wait()

    def coefficient(table, z, r, c):
        return table[r, facies[z], c]

    lane8 = lax.broadcasted_iota(jnp.int32, (HALO, nx), 1)
    row8 = lax.broadcasted_iota(jnp.int32, (HALO, nx), 0)
    pair8 = lax.shift_right_logical(lane8, 1)
    even8 = lax.rem(lane8, 2) == 0
    first8, last8 = lane8 == 0, lane8 == nx - 1
    nil8 = jnp.zeros((HALO, nx), f32)
    group8 = lax.shift_right_logical(lane8, 4)
    in16 = lax.rem(lane8, 2 * HALO)
    left_part = in16 < HALO

    def packed_columns(values):
        out = [nil8] * xtiles
        for z, g, x in values:
            place = (g % per) * nz + z
            out[g // per] = jnp.where(pair8 == place, pltpu.roll(x, 2 * place + 1, 1), out[g // per])
        return out

    def swapped(x):
        return jnp.where(even8, pltpu.roll(x, nx - 1, 1), pltpu.roll(x, 1, 1))

    loads[0].wait()
    values = []
    for z in range(nz):
        r = 0.5 / permb[z].astype(f32)
        u[3, z + 1, own, :] = r
        for side, at_row in ((0, 0), (1, ny - 1)):
            ysend[0, side, nz + z:nz + z + 1, :] = r[at_row:at_row + 1]
        values += [(z, g, r[g * HALO:(g + 1) * HALO]) for g in range(groups)]
    packed = packed_columns(values)
    for t in range(xtiles):
        xsend[0, 1, t] = packed[t]

    loads[1].wait()
    values = []
    for z in range(nz):
        k0 = [coefficient(ktab, z, 0, k) for k in range(3)]
        pc = k0[0] * u[0, z + 1, own, :] + k0[1] * u[1, z + 1, own, :] + k0[2] * u[2, z + 1, own, :]
        pcb[z, own, :] = pc
        for side, at_row in ((0, 0), (1, ny - 1)):
            ysend[0, side, z:z + 1, :] = pc[at_row:at_row + 1]
        values += [(z, g, pc[g * HALO:(g + 1) * HALO]) for g in range(groups)]
    packed = packed_columns(values)
    for t in range(xtiles):
        xsend[0, 0, t] = packed[t]

    beside_y = exists(-1, 0).astype(jnp.int32) + exists(1, 0).astype(jnp.int32)
    beside_x = exists(0, -1).astype(jnp.int32) + exists(0, 1).astype(jnp.int32)
    pl.semaphore_wait(barrier, beside_y + beside_x + (ngz - 1))

    def remote(src, dst, send, recv, device):
        return pltpu.make_async_remote_copy(src_ref=src, dst_ref=dst, send_sem=send, recv_sem=recv,
                                            device_id=device, device_id_type=MESH)

    def start(copies):
        for sends, copy in copies:
            @pl.when(sends)
            def _(copy=copy):
                copy.start()

    def y_copies(batch):
        s = send_y, h_recv.at[1 + batch]
        return [(exists(1, 0), remote(ysend.at[batch, 1], yrecv.at[batch, 0], *s, at(1, 0))),
                (exists(-1, 0), remote(ysend.at[batch, 0], yrecv.at[batch, 1], *s, at(-1, 0)))]

    def x_copies(batch):
        s = send_x, h_recv.at[3 + batch]
        return [(exists(0, 1), remote(xsend.at[batch], xrecv.at[batch, 0], *s, at(0, 1))),
                (exists(0, -1), remote(xsend.at[batch], xrecv.at[batch, 1], *s, at(0, -1)))]

    def z_device(d):
        return {"gx": ix, "gy": iy, "gz": iz + d}

    z_up = remote(u.at[:, nz, own], u.at[:, 0, own], send_z, h_recv.at[0], z_device(1))
    z_down = remote(u.at[:, 1, own], u.at[:, nz + 1, own], send_z, h_recv.at[0], z_device(-1))
    has_below, has_above = iz > 0, iz < ngz - 1

    start(y_copies(0))
    start(x_copies(0))
    start([(has_above, z_up), (has_below, z_down)])
    for n, dy, dx in ((1, -1, 0), (0, 1, 0), (3, 0, 1)):
        @pl.when(exists(dy, dx))
        def _(n=n, dy=dy, dx=dx):
            pl.semaphore_signal(near.at[n], inc=1, device_id=at(dy, dx), device_id_type=MESH)
    signal_peers(near.at[2])

    def counted(count, cases, descriptor, done):
        for n, ref in cases:
            @pl.when(count == n)
            def _(ref=ref):
                done(descriptor(ref))

    def wait_many(count, cases, send, recv, sent):
        counted(count, cases, lambda ref: remote(ref, ref, send, recv, z_device(0)),
                (lambda c: c.wait_send()) if sent else (lambda c: c.wait_recv()))

    def wait_y(batch):
        wait_many(beside_y, ((1, yrecv.at[batch, 0]), (2, yrecv.at[batch])), send_y, h_recv.at[1 + batch], False)

    def wait_x(batch):
        wait_many(beside_x, ((1, xrecv.at[batch, 0]), (2, xrecv.at[batch])), send_x, h_recv.at[3 + batch], False)

    beside_z = has_below.astype(jnp.int32) + has_above.astype(jnp.int32)
    z_cases = ((1, u.at[:, 1, own]), (2, u.at[:, 1:3, own]))

    for i in range(2):
        values = []
        for z in range(nz):
            c = u[1 + i, z + 1, own, :]
            for side, at_row in ((0, 0), (1, ny - 1)):
                ysend[1, side, i * nz + z:i * nz + z + 1, :] = c[at_row:at_row + 1]
            values += [(z, g, c[g * HALO:(g + 1) * HALO]) for g in range(groups)]
        packed = packed_columns(values)
        for t in range(xtiles):
            xsend[1, i, t] = packed[t]
    start(x_copies(1))
    start(y_copies(1))
    raw_group8 = group8 - raw_lane // (2 * HALO)

    def lanes_of(g):
        return (g % per) * 2 * nz

    for i in range(2):
        here, swap = nil8, nil8
        for side in range(2):
            for k in range(layers):
                rows = slice(i * nz + k * HALO, i * nz + (k + 1) * HALO)
                for other in range(2):
                    slot = (side if not other else 1 - side) * layers + k
                    moved = pltpu.roll(ysend[0, side, rows, :], (raw_lane + 2 * HALO * slot + HALO) % nx, 1)
                    if other:
                        swap = jnp.where(raw_group8 == slot, moved, swap)
                    else:
                        here = jnp.where(raw_group8 == slot, moved, here)
        rpsend[i] = here
        for side, g in ends:
            column = xsend[0, i, g // per]
            if lanes_of(g):
                column = pltpu.roll(column, nx - lanes_of(g), 1)
            dsend[side, i] = jnp.where(lane8 < 2 * nz, column, swap)

    def ways(dy, dx, copy):
        @pl.when(exists(dy, dx))
        def _():
            copy.start()

    for dx in (-1, 1):
        ways(0, dx, remote(rpsend, cxrecv.at[(1 - dx) // 2, ngz * nstrips:], send_cx, h_recv.at[5], at(0, dx)))
    for dy in (-1, 1):
        ways(dy, 0, remote(dsend.at[(1 + dy) // 2], cyrecv.at[(1 - dy) // 2, ngz * PLANES:], send_cy, h_recv.at[5], at(dy, 0)))

    def known(n, dy, dx):
        @pl.when(exists(dy, dx))
        def _():
            pl.semaphore_wait(near.at[n], 1)

    def raw_corner(dy, dx):
        ways(dy, dx, remote(dsend.at[(1 + dy) // 2], cdrecv.at[(1 - dy) + (1 - dx) // 2, ngz:], send_cd, h_recv.at[6], at(dy, dx)))


    layer_of_lane = lax.rem(lane8[0:1], 2 * nz) // 2
    lanek = [jnp.zeros((1, nx), f32) for _ in range(3)]
    for z in range(nz):
        for k in range(3):
            value = coefficient(ktab, z, 0, k)
            rowk[k, z:z + 1, :] = jnp.full((1, nx), value, f32)
            lanek[k] = jnp.where(layer_of_lane == z, value, lanek[k])
    loads[2].wait()
    loads[3].wait()

    known(0, -1, 0)
    raw_corner(-1, -1)
    raw_corner(-1, 1)
    signal_peers(far.at[0])

    def tile_of(g):
        return slice(g * HALO, (g + 1) * HALO)

    def padded(g, shift):
        return slice(HALO + g * HALO + shift, HALO + (g + 1) * HALO + shift)

    def assemble(z, carry, upper=True):
        s_res, s_dia, s_ty, s_tx, s_hx, s_hy, s_z = (list(c) for c in carry)
        volume = poreb[z].astype(f32)
        k00 = coefficient(ktab, z, 0, 0)
        m0 = [coefficient(mtab, z, 0, k) for k in range(3)]
        if upper:
            dk = [coefficient(ktab, z, 0, k) - coefficient(ktab, z + 1, 0, k) for k in range(3)]
        for g in range(groups):
            rows = padded(g, 0)
            r = u[3, z + 1, rows, :]
            typ = 1.0 / (r + u[3, z + 1, padded(g, 1), :])
            if g == groups - 1:
                typ = jnp.where(row8 < HALO - 1, typ, 0.0)
            xp = jnp.where(last8, 0.0, 1.0 / (r + pltpu.roll(r, nx - 1, 1)))
            ty[z, rows, :] = typ
            txp[z, tile_of(g), :] = xp
            pc = pcb[z, rows, :]
            s_hx[g] = s_hx[g] + xp * (pc - pltpu.roll(pc, nx - 1, 1))
            s_hy[g] = s_hy[g] + typ * (pc - pcb[z, padded(g, 1), :])
            v = volume[tile_of(g)]
            c = [u[k, z + 1, rows, :] for k in range(3)]
            s_res[g] = s_res[g] + (rhs[0, z, tile_of(g), :] - v * (m0[0] * c[0] + m0[1] * c[1] + m0[2] * c[2]))
            s_dia[g] = s_dia[g] + v * m0[0]
            s_ty[g] = s_ty[g] + k00 * typ
            s_tx[g] = s_tx[g] + k00 * xp
            if upper:
                t = 1.0 / (r + u[3, z + 2, rows, :])
                tzf[z + 1, tile_of(g), :] = t
                d = [c[k] - u[k, z + 2, rows, :] for k in range(3)]
                s_z[g] = s_z[g] + t * (dk[0] * d[0] + dk[1] * d[1] + dk[2] * d[2])
        return tuple(tuple(s) for s in (s_res, s_dia, s_ty, s_tx, s_hx, s_hy, s_z))

    carry = ((nil8,) * groups,) * 7
    trips = (nz - 1) // 2

    def two(i, carry):
        return assemble(2 * i + 1, assemble(2 * i, carry))

    carry = lax.fori_loop(0, trips, two, carry)
    for z in range(2 * trips, nz):
        carry = assemble(z, carry, upper=z < nz - 1)
    s_res, s_dia, s_ty, s_tx, s_hx, s_hy, s_z = (list(c) for c in carry)

    for g in range(groups):
        shifted[0, padded(g, 0), :] = s_hy[g]
        shifted[1, padded(g, 0), :] = s_ty[g]
    p_rhs, p_dia = [], []
    for g in range(groups):
        p_rhs.append(s_res[g] - s_z[g] - (s_hx[g] - pltpu.roll(s_hx[g], 1, 1)) - (s_hy[g] - shifted[0, padded(g, -1), :]))
        p_dia.append(s_dia[g] + s_ty[g] + shifted[1, padded(g, -1), :] + s_tx[g] + pltpu.roll(s_tx[g], 1, 1))

    wait_many(beside_z, z_cases, send_z, h_recv.at[0], False)
    for slot, z, inside in ((0, 0, 1), (nz + 1, nz - 1, nz)):
        k0 = [coefficient(ktab, z, 0, k) for k in range(3)]
        for g in range(groups):
            rows = padded(g, 0)
            there = u[3, slot, rows, :]
            t = jnp.where(there > 0.0, 1.0 / (u[3, inside, rows, :] + there), 0.0)
            tzf[0 if slot == 0 else nz, tile_of(g), :] = t
            d = [u[k, inside, rows, :] - u[k, slot, rows, :] for k in range(3)]
            p_rhs[g] = p_rhs[g] - t * (k0[0] * d[0] + k0[1] * d[1] + k0[2] * d[2])
    mine = [[swapped(xsend[0, i, t]) for t in range(xtiles)] for i in range(2)]

    planes = [p_rhs, p_dia, s_ty, s_tx]
    for p in range(PLANES):
        ystrips[0, p] = planes[p][0]
        ystrips[1, p] = planes[p][groups - 1]
    for i, tiles in enumerate(packing):
        strip = nil8
        for j, g in enumerate(tiles):
            for p in range(PLANES):
                slot = j * PLANES + p
                strip = jnp.where(group8 == slot, pltpu.roll(planes[p][g], (2 * HALO * slot + HALO) % nx, 1), strip)
        strips[i] = strip

    def to_all(dy, dx, src, dst, send, recv, parts=range(ngz)):
        return [(exists(dy, dx), remote(src, dst, send, c_recv.at[recv],
                                        {"gx": ix + dx, "gy": iy + dy, "gz": lax.rem(iz + d, ngz)})) for d in parts]

    def corner_strips(dy, dx, parts):
        start(to_all(dy, dx, strips.at[0 if dy < 0 else last_head], cdrecv.at[(1 - dy) + (1 - dx) // 2, iz], send_cd, 3, parts))

    pl.semaphore_wait(far.at[0], ngz - 1)
    pl.semaphore_wait(near.at[2], ngz - 1)
    corner_strips(-1, -1, range(ngz))
    corner_strips(-1, 1, range(ngz))
    known(3, 0, -1)
    raw_corner(1, -1)
    corner_strips(1, -1, range(1))
    for dx in (-1, 1):
        start(to_all(0, dx, strips, cxrecv.at[(1 - dx) // 2, pl.ds(iz * nstrips, nstrips)], send_cx, 2))
    for dy in (-1, 1):
        start(to_all(dy, 0, ystrips.at[(1 + dy) // 2], cyrecv.at[(1 - dy) // 2, pl.ds(iz * PLANES, PLANES)], send_cy, 1))

    for f in range(ktab.shape[1]):
        values = block_scalars([[mtab[r, f, c] for c in range(3)] for r in range(3)],
                               [[ktab[r, f, c] for c in range(3)] for r in range(3)])
        for i, value in enumerate(values):
            ctab[i, f] = value

    known(1, 1, 0)
    raw_corner(1, 1)
    signal_peers(far.at[1])
    corner_strips(1, 1, range(1))

    def inside(z, _):
        f = facies[z]
        kinv = [[ctab[KINV + 3 * r + c, f] for c in range(3)] for r in range(3)]
        for g in range(groups):
            rows = padded(g, 0)
            tile = tile_of(g)
            tzm, tzp = tzf[z, tile, :], tzf[z + 1, tile, :]
            typ, tym = ty[z, rows, :], ty[z, padded(g, -1), :]
            xp = txp[z, tile, :]
            xm = pltpu.roll(xp, 1, 1)
            tz = tzm + tzp
            tzs[z, tile, :] = tz
            txm[z, tile, :] = xm
            qv[0, z, tile, :] = tz + (typ + tym) + (xp + xm)
            given = [rhs[k, z, tile, :] for k in range(3)]
            for k in range(3):
                c = u[k, z + 1, rows, :]
                w[k, z, tile, :] = ((tzp * u[k, z + 2, rows, :] + tzm * u[k, z, rows, :])
                                    + (typ * u[k, z + 1, padded(g, 1), :] + tym * u[k, z + 1, padded(g, -1), :])
                                    + (xp * pltpu.roll(c, nx - 1, 1) + xm * pltpu.roll(c, 1, 1))
                                    + (kinv[k][0] * given[0] + kinv[k][1] * given[1] + kinv[k][2] * given[2]))
        return 0

    def layers_of(step, begin, end):
        def several(i, carry):
            return step(begin + 2 * i + 1, step(begin + 2 * i, carry))

        lax.fori_loop(0, (end - begin) // 2, several, 0)
        if (end - begin) % 2:
            step(end - 1, 0)

    layers_of(inside, 0, nz // 2)
    pl.semaphore_wait(far.at[1], ngz - 1)
    corner_strips(1, -1, range(1, ngz))
    corner_strips(1, 1, range(1, ngz))
    layers_of(inside, nz // 2, nz)

    wait_y(0)
    top8, bottom8 = row8 == 0, row8 == HALO - 1
    lines = nil8
    y_faces = []
    for side, g, here in ((0, 0, top8), (1, groups - 1, bottom8)):
        there = yrecv[0, side, nz:, :]
        t = jnp.where(there > 0.0, 1.0 / (ysend[0, side, nz:, :] + there), 0.0)
        moved = jnp.sum(t * (ysend[0, side, :nz, :] - yrecv[0, side, :nz, :]), axis=0, keepdims=True)
        weight = jnp.sum(rowk[0] * t, axis=0, keepdims=True)
        lines = jnp.where(row8 == 2 * side, moved, jnp.where(row8 == 2 * side + 1, weight, lines))
        y_faces.append((side, g, here, t, moved, weight))
    wait_x(0)
    flux, weights, faces, outside = [], [], [], []
    for t in range(xtiles):
        there = [jnp.where(even8, xrecv[0, 0, i, t], xrecv[0, 1, i, t]) for i in range(2)]
        face = jnp.where(there[1] > 0.0, 1.0 / (mine[1][t] + there[1]), 0.0)
        flux.append(face * (mine[0][t] - there[0]))
        weights.append(face * lanek[0])
        faces.append(face)
        outside.append(there[0])

    def sums_of(flux, weights, low):
        block = jnp.logical_and(lane8 >= low, lane8 < low + 2 * nz)
        sums = []
        for values in (flux, weights):
            for parity in (even8, jnp.logical_not(even8)):
                sums.append(jnp.sum(jnp.where(jnp.logical_and(block, parity), values, 0.0), axis=1, keepdims=True))
        return sums

    def at_sides(left, right):
        return jnp.where(first8, left, jnp.where(last8, right, 0.0))

    for side, g, here, t, moved, weight in y_faces:
        for p, change in ((0, -moved), (1, weight), (2, weight))[:3 if side else 2]:
            planes[p][g] = planes[p][g] + jnp.where(here, change, 0.0)
        for z in range(nz):
            edge_row = HALO - 1 + side * ny
            ty[z, edge_row:edge_row + 1, :] = t[z:z + 1]
    zplanes[iz, PLANES * groups] = lines
    for i, tiles in enumerate(packing):
        across = nil8
        for j, g in enumerate(tiles):
            flux_l, flux_r, weight_l, weight_r = sums_of(flux[g // per], weights[g // per], lanes_of(g))
            for p, change in ((0, at_sides(-flux_l, -flux_r)), (1, at_sides(weight_l, weight_r)),
                              (3, jnp.where(last8, weight_r, 0.0))):
                planes[p][g] = planes[p][g] + change
            for p, left, right in ((0, flux_l, flux_r), (1, weight_l, weight_r), (3, weight_l, 0.0)):
                slot = (j * PLANES + p) * 2 * HALO
                across = jnp.where(lane8 == slot + HALO - 1, left, jnp.where(lane8 == slot + HALO, right, across))
        zplanes[iz, PLANES * groups + 1 + i] = across
    for p in range(PLANES):
        for g in range(groups):
            zplanes[iz, p * groups + g] = planes[p][g]
    for d in range(1, ngz):
        remote(zplanes.at[iz, 0:first_part], zplanes.at[iz, 0:first_part], send_cz, c_recv.at[0],
               {"gx": ix, "gy": iy, "gz": lax.rem(iz + d, ngz)}).start()

    wait_y(1)
    wait_x(1)
    invrow = 1.0 / rowk[0]
    for side, _, _, t, _, _ in y_faces:
        one, two_ = yrecv[1, side, :nz, :], yrecv[1, side, nz:, :]
        zero_ = (yrecv[0, side, :nz, :] - rowk[1] * one - rowk[2] * two_) * invrow
        for k, x in enumerate((zero_, one, two_)):
            yedge[side, k] = t * x
        yedge[side, 3] = t
    invlane = 1.0 / lanek[0]
    for t in range(xtiles):
        one, two_ = (jnp.where(even8, xrecv[1, 0, i, t], xrecv[1, 1, i, t]) for i in range(2))
        zero_ = (outside[t] - lanek[1] * one - lanek[2] * two_) * invlane
        for k, x in enumerate((zero_, one, two_)):
            edge[k, t] = swapped(faces[t] * x)
        edge[3, t] = swapped(faces[t])

    outer8 = jnp.logical_or(first8, last8)

    def solve(z, _):
        volume = poreb[z].astype(f32)
        f = facies[z]
        n = [[ctab[NMAT + 3 * r + c, f] for c in range(3)] for r in range(3)]
        adj = [[ctab[NADJ + 3 * r + c, f] for c in range(3)] for r in range(3)]
        dia = [ctab[NDIA + i, f] for i in range(3)]
        trace, minors, det_n = ctab[NTR, f], ctab[NC2, f], ctab[NDET, f]
        for g in range(groups):
            tile = tile_of(g)
            shift = lax.rem(2 * nx - (lanes_of(g) + 1) - 2 * z, nx)
            added = [jnp.where(outer8, pltpu.roll(edge[k, g // per], shift, 1), 0.0) for k in range(4)]
            txp[z, tile, :] = txp[z, tile, :] + jnp.where(last8, added[3], 0.0)
            txm[z, tile, :] = txm[z, tile, :] + jnp.where(first8, added[3], 0.0)
            for side, head in ends:
                if g == head:
                    here = top8 if side == 0 else bottom8
                    added = [added[k] + jnp.where(here, yedge[side, k, pl.ds(z, 1), :], 0.0) for k in range(4)]
            b = [w[r, z, tile, :] + added[r] for r in range(3)]
            v = volume[tile]
            s = (qv[0, z, tile, :] + added[3]) * (1.0 / v)
            e = [[s * (s + dia[r]) + adj[r][r] if r == c else adj[r][c] - s * n[r][c] for c in range(3)] for r in range(3)]
            det = ((s + trace) * s + minors) * s + det_n
            inv = 1.0 / (v * det)
            for r in range(3):
                w[r, z, tile, :] = (e[r][0] * b[0] + e[r][1] * b[1] + e[r][2] * b[2]) * inv
                qv[r, z, tile, :] = e[r][0] * inv
        return 0

    most = nz * 5 // 8
    layers_of(solve, 0, most)

    corners = beside_y * beside_x
    wait_many(beside_y + beside_x, [(n, zplanes.at[0, 0:2 * n]) for n in range(1, 5)], send_cx, h_recv.at[5], False)
    wait_many(corners, ((1, cdrecv.at[0, ngz:]), (2, cdrecv.at[0:2, ngz:]), (4, cdrecv.at[:, ngz:])), send_cd, h_recv.at[6], False)
    from_top = raw_group8 < layers
    ours, theirs = [], []
    for i in range(2):
        ours.append(jnp.where(left_part, cxrecv[0, ngz * nstrips + i], cxrecv[1, ngz * nstrips + i]))
        theirs.append(jnp.where(from_top, jnp.where(left_part, cdrecv[0, ngz + i], cdrecv[1, ngz + i]),
                                jnp.where(left_part, cdrecv[2, ngz + i], cdrecv[3, ngz + i])))
    t = jnp.where(jnp.logical_and(raw_group8 >= 0, theirs[1] > 0.0), 1.0 / (ours[1] + theirs[1]), 0.0)
    pattern = nil8
    for k in range(layers):
        pattern = jnp.where(lax.rem(group8, layers) == (k + raw_lane // (2 * HALO)) % layers, rowk[0, k * HALO:(k + 1) * HALO, :], pattern)
    both = jnp.where(top8, jnp.sum(t * (ours[0] - theirs[0]), axis=0, keepdims=True),
                     jnp.sum(t * pattern, axis=0, keepdims=True))
    summed = both
    for k in range(1, layers):
        summed = summed + pltpu.roll(both, nx - 2 * HALO * k, 1)
    upper = pltpu.roll(summed, (2 * nx - raw_lane - HALO) % nx, 1)
    lower = pltpu.roll(summed, (2 * nx - raw_lane - 2 * HALO * layers - HALO) % nx, 1)
    zplanes[iz, first_part] = jnp.where(row8 < 2, upper, pltpu.roll(lower, 2, 0))
    for side, g in ends:
        tiles = [swapped(cyrecv[side, ngz * PLANES + i]) for i in range(2)]
        there = [jnp.where(even8, cdrecv[2 * side, ngz + i], cdrecv[2 * side + 1, ngz + i]) for i in range(2)]
        face = jnp.where(there[1] > 0.0, 1.0 / (tiles[1] + there[1]), 0.0)
        flux_l, flux_r, weight_l, weight_r = sums_of(face * (tiles[0] - there[0]), face * lanek[0], 0)
        for n, tile in enumerate((at_sides(-flux_l, -flux_r), at_sides(weight_l, weight_r),
                                  at_sides(flux_r, flux_l), at_sides(weight_r, weight_l))):
            zplanes[iz, first_part + 1 + 4 * side + n] = tile
    for d in range(1, ngz):
        remote(zplanes.at[iz, first_part:], zplanes.at[iz, first_part:], send_cz, c_recv.at[4],
               {"gx": ix, "gy": iy, "gz": lax.rem(iz + d, ngz)}).start()
    layers_of(solve, most, nz)

    if ngz > 1:
        others = zplanes.at[0:ngz - 1, 0:first_part]
        remote(others, others, send_cz, c_recv.at[0], z_device(0)).wait_recv()
    y_early, x_early = slice(0, ngz * PLANES), slice(0, ngz * nstrips)
    wait_many(beside_y, ((1, cyrecv.at[0, y_early]), (2, cyrecv.at[:, y_early])), send_cy, c_recv.at[1], False)
    wait_many(beside_x, ((1, cxrecv.at[0, x_early]), (2, cxrecv.at[:, x_early])), send_cx, c_recv.at[2], False)
    wait_many(corners, ((1, cdrecv.at[0, 0:ngz]), (2, cdrecv.at[0:2, 0:ngz]), (4, cdrecv.at[:, 0:ngz])), send_cd, c_recv.at[3], False)

    def gathered(part):
        total = part(0)
        for i in range(1, ngz):
            total = total + part(i)
        return total

    tiles_in = groups + 2
    side_tiles = [jnp.where(left_part, gathered(lambda i: cxrecv[0, i * nstrips + t]), gathered(lambda i: cxrecv[1, i * nstrips + t]))
                  + gathered(lambda i: zplanes[i, PLANES * groups + 1 + t]) for t in range(nstrips)]
    corner_tiles = [jnp.where(left_part, gathered(lambda i: cdrecv[2 * v, i]), gathered(lambda i: cdrecv[2 * v + 1, i]))
                    for v in range(2)]
    where_is = {g: (i, j) for i, tiles in enumerate(packing) for j, g in enumerate(tiles)}
    on_right, on_left = lane8 < HALO, lane8 >= nx - HALO
    strip8 = jnp.logical_or(on_right, on_left)

    def border_of(p, g):
        if 0 <= g < groups:
            i, j = where_is[g]
            tile, slot = side_tiles[i], j * PLANES + p
        else:
            tile, slot = corner_tiles[0 if g < 0 else 1], p
        return jnp.where(strip8, pltpu.roll(tile, (2 * nx - 2 * HALO * slot - HALO) % nx, 1), 0.0)

    b = [[border_of(p, g) for g in range(-1, groups + 1)] for p in range(PLANES)]
    own_lines = gathered(lambda i: zplanes[i, PLANES * groups])
    a = [[gathered(lambda i: cyrecv[0, i * PLANES + p])] + [gathered(lambda i: zplanes[i, p * groups + g]) for g in range(groups)]
         + [gathered(lambda i: cyrecv[1, i * PLANES + p])] for p in range(PLANES)]

    def beyond(grid, lines):
        for side, t, here in ((0, 0, bottom8), (1, tiles_in - 1, top8)):
            moved, weight = lines[2 * side:2 * side + 1], lines[2 * side + 1:2 * side + 2]
            for p, change in ((0, moved), (1, weight), (2, weight))[:2 if side else 3]:
                grid[p][t] = grid[p][t] + jnp.where(here, change, 0.0)

    beyond(a, own_lines)

    def east(ra, rb):
        return jnp.where(last8, rb, ra), jnp.where(last8, ra, rb)

    def west(ra, rb):
        return jnp.where(first8, rb, ra), jnp.where(first8, ra, rb)

    def fill(buffer, s, tiles):
        for t in range(tiles_in):
            field[buffer, s, (t + 1) * HALO:(t + 2) * HALO, :] = tiles[t]

    def above(buffer, s, t):
        return field[buffer, s, (t + 1) * HALO - 1:(t + 2) * HALO - 1, :]

    def below(buffer, s, t):
        return field[buffer, s, (t + 1) * HALO + 1:(t + 2) * HALO + 1, :]

    terms = [[None] * tiles_in for _ in range(2)]
    grids = (a, b)

    def prepare(s, t):
        rhs_, dia, down, right = (grids[s][p][t] for p in range(PLANES))
        there = dia > 0.0
        inv = jnp.where(there, RELAX / jnp.where(there, dia, 1.0), 0.0)
        left = west(*(pltpu.roll(grid[3][t], 1, 1) for grid in grids))[s]
        terms[s][t] = [rhs_ * inv, down * inv, above(0, s, t) * inv, right * inv, left * inv]

    fill(0, 0, a[2])
    late_b = (0, 1, groups, groups + 1)
    for t in range(1, tiles_in - 1):
        prepare(0, t)

    if ngz > 1:
        rest = zplanes.at[0:ngz - 1, first_part:]
        remote(rest, rest, send_cz, c_recv.at[4], z_device(0)).wait_recv()
    lines = jnp.where(strip8, gathered(lambda i: zplanes[i, first_part]), 0.0)
    beyond(b, lines)
    for side, t, here in ((0, 1, top8), (1, groups, bottom8)):
        moved, weight = lines[2 * side:2 * side + 1], lines[2 * side + 1:2 * side + 2]
        for p, change in ((0, -moved), (1, weight), (2, weight))[:3 if side else 2]:
            b[p][t] = b[p][t] + jnp.where(here, change, 0.0)
    fill(0, 1, b[2])
    for t in range(1, tiles_in - 1):
        prepare(1, t)
    for side, t in ((0, 0), (1, tiles_in - 1)):
        flux_, weight_, flux_past, weight_past = (
            gathered(lambda i: zplanes[i, first_part + 1 + 4 * side + n]) for n in range(4))
        for grid, change, weight in ((a, flux_, weight_), (b, flux_past, weight_past)):
            grid[0][t] = grid[0][t] + change
            grid[1][t] = grid[1][t] + weight
            grid[3][t] = grid[3][t] + jnp.where(last8, weight, 0.0)
        for s in range(2):
            prepare(s, t)

    c = [[terms[s][t][0] for t in range(tiles_in)] for s in range(2)]
    for sweep in range(1, SWEEPS):
        buffer = sweep % 2
        for s in range(2):
            fill(buffer, s, c[s])
        nxt = [[None] * tiles_in for _ in range(2)]
        for t in range(tiles_in):
            e = east(*(pltpu.roll(c[s][t], nx - 1, 1) for s in range(2)))
            ws = west(*(pltpu.roll(c[s][t], 1, 1) for s in range(2)))
            for s in range(2):
                r, tyn, tys, txe, txw = terms[s][t]
                nxt[s][t] = (((1.0 - RELAX) * c[s][t] + r) + (tyn * below(buffer, s, t) + tys * above(buffer, s, t))
                             + (txe * e[s] + txw * ws[s]))
        c = nxt
    for t in range(tiles_in):
        rows = slice(t * HALO, (t + 1) * HALO)
        final[0, rows, :] = c[0][t]
        if 0 < t < tiles_in - 1:
            final[1, rows, :] = east(*(pltpu.roll(c[s][t], nx - 1, 1) for s in range(2)))[0]
            final[2, rows, :] = west(*(pltpu.roll(c[s][t], 1, 1) for s in range(2)))[0]
    for count, cases, sem in (
        (beside_y, ((1, yrecv.at[0]), (2, yrecv)), send_y),
        (beside_x, ((1, xrecv.at[0]), (2, xrecv)), send_x),
        (beside_z, z_cases, send_z),
        (beside_y, ((1, cyrecv.at[0]), (2, cyrecv)), send_cy),
        (beside_x, ((1, cxrecv.at[0]), (2, cxrecv)), send_cx),
        (corners, ((1, cdrecv.at[0]), (2, cdrecv.at[0:2]), (4, cdrecv)), send_cd),
    ):
        wait_many(count, cases, sem, h_recv.at[0], True)
    if ngz > 1:
        others = zplanes.at[0:ngz - 1]
        remote(others, others, send_cz, c_recv.at[0], z_device(0)).wait_send()


def finish_kernel(parts, w, qv, tzs, ty, txp, txm, final, new_hbm, corr_hbm, out, out_sem):
    nz, ny, nx = tzs.shape
    own = slice(HALO, HALO + ny)
    corr = pltpu.make_async_copy(final.at[0, own], corr_hbm, out_sem.at[parts])
    corr.start()
    cc, ce, cw = (final[k, own, :] for k in range(3))
    cn, cs = final[0, HALO + 1:HALO + 1 + ny, :], final[0, HALO - 1:HALO - 1 + ny, :]

    def finish(z, _):
        g = (tzs[z] * cc + ty[z, own, :] * cn + ty[z, HALO - 1:HALO + ny - 1, :] * cs
             + txp[z] * ce + txm[z] * cw)
        for r in range(3):
            out[r, z] = w[r, z] + qv[r, z] * g
        return 0

    step = nz // parts
    outs = [corr]
    for part in range(parts):
        lax.fori_loop(part * step, (part + 1) * step, finish, 0)
        chunk = slice(part * step, (part + 1) * step)
        outs.append(pltpu.make_async_copy(out.at[:, chunk], new_hbm.at[:, chunk], out_sem.at[part]))
        outs[-1].start()
    for copy in outs:
        copy.wait()


def per_device(sizes, state, right_side, permeability, pore_volume, facies, storage_table, coupling_table):
    _, nz, ny, nx = state.shape
    sizes = sizes + (nz, ny, nx)
    f32 = jnp.float32
    ngz = sizes[2]
    cells = (nz, ny, nx)
    vmem = lambda *shape: pltpu.VMEM(shape, f32)
    hbm = pl.BlockSpec(memory_space=pltpu.HBM)
    dma = lambda n: pltpu.SemaphoreType.DMA((n,))
    ey = ny + 2 * HALO
    groups, per, xtiles = column_plan(nz, ny, nx)
    strips = len(strip_plan(ny, nx))
    facets = storage_table.shape[0]
    in_vmem = pl.BlockSpec(memory_space=pltpu.VMEM)
    handed = 4 * nx * (9 * nz * ny + nz * ey + 3 * ey)
    limit = 16384 * ((VMEM_BYTES - handed) // 16384)
    middle = pl.pallas_call(
        functools.partial(kernel, sizes),
        out_shape=(vmem(3, *cells), vmem(3, *cells), vmem(*cells), vmem(nz, ey, nx), vmem(*cells), vmem(*cells),
                   vmem(3, ey, nx)),
        in_specs=[hbm, hbm, hbm, hbm, hbm, hbm, hbm],
        out_specs=(in_vmem,) * 7,
        scratch_shapes=[
            vmem(4, nz + 2, ey, nx), vmem(nz, ey, nx), vmem(3, *cells),
            pltpu.VMEM(cells, permeability.dtype), pltpu.VMEM(cells, pore_volume.dtype),
            vmem(2, 2, 2 * nz, nx), vmem(2, 2, 2 * nz, nx),
            vmem(2, 2, xtiles, HALO, nx), vmem(2, 2, 2, xtiles, HALO, nx), vmem(4, xtiles, HALO, nx),
            vmem(3, nz, nx), vmem(nz + 1, ny, nx), vmem(2, ey, nx),
            vmem(ngz, PLANES * groups + 1 + strips + 9, HALO, nx), vmem(2, PLANES, HALO, nx), vmem(strips, HALO, nx),
            vmem(2, ngz * PLANES + 2, HALO, nx), vmem(2, ngz * strips + 2, HALO, nx), vmem(4, ngz + 2, HALO, nx),
            vmem(2, HALO, nx), vmem(2, 2, HALO, nx), vmem(2, 4, nz, nx), vmem(2, 2, ey + 2 * HALO, nx),
            pltpu.SMEM((nz,), facies.dtype), pltpu.SMEM((3, facets, 3), f32), pltpu.SMEM((3, facets, 3), f32),
            pltpu.SMEM((NCOEF, facets), f32),
            pltpu.SemaphoreType.REGULAR((4,)), pltpu.SemaphoreType.REGULAR((2,)), dma(7), dma(7), dma(5),
        ],
        compiler_params=pltpu.CompilerParams(collective_id=0, has_side_effects=True, vmem_limit_bytes=limit),
        name="cpr_apply",
    )(facies, storage_table.transpose(1, 0, 2), coupling_table.transpose(1, 0, 2),
      state, right_side, permeability, pore_volume)
    parts = 8 if nz % 8 == 0 else 1
    return tuple(pl.pallas_call(
        functools.partial(finish_kernel, parts),
        out_shape=(jax.ShapeDtypeStruct(state.shape, f32), jax.ShapeDtypeStruct((ny, nx), f32)),
        in_specs=[in_vmem] * 7,
        out_specs=(hbm, hbm),
        scratch_shapes=[vmem(3, *cells), dma(parts + 1)],
        compiler_params=pltpu.CompilerParams(vmem_limit_bytes=16 * 2**20),
        name="cpr_finish",
    )(*middle))


def solution(mesh):
    sizes = (mesh.shape["gx"], mesh.shape["gy"], mesh.shape["gz"])
    return jax.shard_map(
        functools.partial(per_device, sizes),
        mesh=mesh,
        in_specs=(
            P(None, "gz", "gy", "gx"),
            P(None, "gz", "gy", "gx"),
            P("gz", "gy", "gx"),
            P("gz", "gy", "gx"),
            P("gz"),
            P(),
            P(),
        ),
        out_specs=(P(None, "gz", "gy", "gx"), P("gy", "gx")),
        check_vma=False,
    )
```

```python
import functools
import jax
import jax.numpy as jnp
from jax import lax
from jax.experimental import pallas as pl
from jax.experimental.pallas import tpu as pltpu
from jax.sharding import PartitionSpec as P

SWEEPS = 8
RELAX = 0.8
MESH = pl.DeviceIdType.MESH
HALO = 8
VMEM_BYTES = 67043328

PLANES = 4
SIDES = [(-1, 0), (1, 0), (0, -1), (0, 1), (-1, -1), (-1, 1), (1, -1), (1, 1)]

KINV, NMAT, NADJ, NDIA, NTR, NC2, NDET, NCOEF = 0, 9, 18, 27, 30, 31, 32, 33


def cofactor(e, r, c):
    return (e[(r + 1) % 3][(c + 1) % 3] * e[(r + 2) % 3][(c + 2) % 3]
            - e[(r + 1) % 3][(c + 2) % 3] * e[(r + 2) % 3][(c + 1) % 3])


def block_scalars(m, k):
    kf = [[cofactor(k, r, c) for c in range(3)] for r in range(3)]
    inv = 1.0 / (k[0][0] * kf[0][0] + k[0][1] * kf[0][1] + k[0][2] * kf[0][2])
    kinv = [[kf[c][r] * inv for c in range(3)] for r in range(3)]
    n = [[kinv[r][0] * m[0][c] + kinv[r][1] * m[1][c] + kinv[r][2] * m[2][c] for c in range(3)] for r in range(3)]
    nf = [[cofactor(n, r, c) for c in range(3)] for r in range(3)]
    trace = n[0][0] + n[1][1] + n[2][2]
    return ([kinv[r][c] for r in range(3) for c in range(3)] + [n[r][c] for r in range(3) for c in range(3)]
            + [nf[c][r] for r in range(3) for c in range(3)] + [trace - n[i][i] for i in range(3)]
            + [trace, nf[0][0] + nf[1][1] + nf[2][2], n[0][0] * nf[0][0] + n[0][1] * nf[0][1] + n[0][2] * nf[0][2]])


def column_plan(nz, ny, nx):
    groups = ny // HALO
    per = nx // (2 * nz)
    return groups, per, -(-groups // per)


def strip_plan(ny, nx):
    groups = ny // HALO
    per = nx // (2 * HALO * PLANES)
    heads = [0] if groups == 1 else [0, groups - 1]
    others = list(range(1, groups - 1))
    packed = [[head] + [others.pop(0) for _ in range(per - 1) if others] for head in heads]
    while others:
        packed.append([others.pop(0) for _ in range(per) if others])
    return packed


def kernel(sizes, facies_hbm, mtab_hbm, ktab_hbm, state_hbm, rhs_hbm, perm_hbm, pore_hbm,
           w, qv, tzs, ty, txp, txm, final,
           u, pcb, rhs, permb, poreb, ysend, yrecv, xsend, xrecv, edge, rowk, tzf, shifted,
           zplanes, ystrips, strips, cyrecv, cxrecv, cdrecv, rpsend, dsend, yedge, field,
           facies, mtab, ktab, ctab, near, far, in_sem, h_recv, c_recv):
    ngx, ngy, ngz, nz, ny, nx = sizes
    ix, iy, iz = lax.axis_index("gx"), lax.axis_index("gy"), lax.axis_index("gz")
    own = slice(HALO, HALO + ny)
    groups, per, xtiles = column_plan(nz, ny, nx)
    packing = strip_plan(ny, nx)
    nstrips = len(packing)
    last_head = len(packing[:2]) - 1
    layers = nz // HALO
    ends = ((0, 0), (1, groups - 1))
    first_part = PLANES * groups + 1 + nstrips
    raw_lane = nx - 4 * HALO * layers
    assert nz % HALO == 0 and raw_lane >= 2 * nz
    f32 = jnp.float32
    send_y, send_x, send_z, send_cy, send_cx, send_cd, send_cz = (in_sem.at[i] for i in (0, 1, 4, 5, 6, 2, 3))

    def exists(dy, dx):
        ok = None
        for d, i, n in ((dy, iy, ngy), (dx, ix, ngx)):
            if d:
                here = (i > 0) if d < 0 else (i < n - 1)
                ok = here if ok is None else jnp.logical_and(ok, here)
        return ok

    def at(dy, dx):
        return {"gx": ix + dx, "gy": iy + dy, "gz": iz}

    barrier = pltpu.get_barrier_semaphore()
    for side in (SIDES[0], SIDES[2], SIDES[1], SIDES[3]):
        @pl.when(exists(*side))
        def _(side=side):
            pl.semaphore_signal(barrier, inc=1, device_id=at(*side), device_id_type=MESH)

    def signal_peers(sem):
        for d in range(1, ngz):
            pl.semaphore_signal(sem, inc=1, device_id={"gx": ix, "gy": iy, "gz": lax.rem(iz + d, ngz)},
                                device_id_type=MESH)

    signal_peers(barrier)

    loads = [
        pltpu.make_async_copy(perm_hbm, permb, in_sem.at[0]),
        pltpu.make_async_copy(state_hbm, u.at[0:3, 1:nz + 1, own], in_sem.at[1]),
        pltpu.make_async_copy(pore_hbm, poreb, in_sem.at[2]),
        pltpu.make_async_copy(rhs_hbm, rhs, in_sem.at[3]),
        pltpu.make_async_copy(facies_hbm, facies, in_sem.at[4]),
        pltpu.make_async_copy(mtab_hbm, mtab, in_sem.at[5]),
        pltpu.make_async_copy(ktab_hbm, ktab, in_sem.at[6]),
    ]
    for i in (4, 6, 5, 0, 1, 2, 3):
        loads[i].start()

    def zero(ref):
        ref[...] = jnp.zeros(ref.shape, ref.dtype)

    for cond, refs in (
        (iz == 0, [u.at[:, 0, own]]),
        (iz == ngz - 1, [u.at[:, nz + 1, own]]),
        (iy == 0, [yrecv.at[:, 0], cyrecv.at[0]]),
        (iy == ngy - 1, [yrecv.at[:, 1], cyrecv.at[1]]),
        (ix == 0, [xrecv.at[:, 0], cxrecv.at[0]]),
        (ix == ngx - 1, [xrecv.at[:, 1], cxrecv.at[1]]),
        (jnp.logical_or(iy == 0, ix == 0), [cdrecv.at[0]]),
        (jnp.logical_or(iy == 0, ix == ngx - 1), [cdrecv.at[1]]),
        (jnp.logical_or(iy == ngy - 1, ix == 0), [cdrecv.at[2]]),
        (jnp.logical_or(iy == ngy - 1, ix == ngx - 1), [cdrecv.at[3]]),
    ):
        @pl.when(cond)
        def _(refs=refs):
            for ref in refs:
                zero(ref)
    zero(field)
    for z in range(nz):
        zero(pcb.at[z, HALO + ny:])
        zero(ty.at[z, 0:HALO])
        for k in range(3):
            zero(u.at[k, z + 1, 0:HALO])
            zero(u.at[k, z + 1, HALO + ny:])
    zero(shifted.at[:, 0:HALO])

    for i in (4, 6, 5):
        loads[i].wait()

    def coefficient(table, z, r, c):
        return table[r, facies[z], c]

    lane8 = lax.broadcasted_iota(jnp.int32, (HALO, nx), 1)
    row8 = lax.broadcasted_iota(jnp.int32, (HALO, nx), 0)
    pair8 = lax.shift_right_logical(lane8, 1)
    even8 = lax.rem(lane8, 2) == 0
    first8, last8 = lane8 == 0, lane8 == nx - 1
    nil8 = jnp.zeros((HALO, nx), f32)
    group8 = lax.shift_right_logical(lane8, 4)
    in16 = lax.rem(lane8, 2 * HALO)
    left_part = in16 < HALO

    def packed_columns(values):
        out = [nil8] * xtiles
        for z, g, x in values:
            place = (g % per) * nz + z
            out[g // per] = jnp.where(pair8 == place, pltpu.roll(x, 2 * place + 1, 1), out[g // per])
        return out

    def swapped(x):
        return jnp.where(even8, pltpu.roll(x, nx - 1, 1), pltpu.roll(x, 1, 1))

    loads[0].wait()
    values = []
    for z in range(nz):
        r = 0.5 / permb[z].astype(f32)
        u[3, z + 1, own, :] = r
        for side, at_row in ((0, 0), (1, ny - 1)):
            ysend[0, side, nz + z:nz + z + 1, :] = r[at_row:at_row + 1]
        values += [(z, g, r[g * HALO:(g + 1) * HALO]) for g in range(groups)]
    packed = packed_columns(values)
    for t in range(xtiles):
        xsend[0, 1, t] = packed[t]

    loads[1].wait()
    values = []
    for z in range(nz):
        k0 = [coefficient(ktab, z, 0, k) for k in range(3)]
        pc = k0[0] * u[0, z + 1, own, :] + k0[1] * u[1, z + 1, own, :] + k0[2] * u[2, z + 1, own, :]
        pcb[z, own, :] = pc
        for side, at_row in ((0, 0), (1, ny - 1)):
            ysend[0, side, z:z + 1, :] = pc[at_row:at_row + 1]
        values += [(z, g, pc[g * HALO:(g + 1) * HALO]) for g in range(groups)]
    packed = packed_columns(values)
    for t in range(xtiles):
        xsend[0, 0, t] = packed[t]

    beside_y = exists(-1, 0).astype(jnp.int32) + exists(1, 0).astype(jnp.int32)
    beside_x = exists(0, -1).astype(jnp.int32) + exists(0, 1).astype(jnp.int32)
    pl.semaphore_wait(barrier, beside_y + beside_x + (ngz - 1))

    def remote(src, dst, send, recv, device):
        return pltpu.make_async_remote_copy(src_ref=src, dst_ref=dst, send_sem=send, recv_sem=recv,
                                            device_id=device, device_id_type=MESH)

    def start(copies):
        for sends, copy in copies:
            @pl.when(sends)
            def _(copy=copy):
                copy.start()

    def y_copies(batch):
        s = send_y, h_recv.at[1 + batch]
        return [(exists(1, 0), remote(ysend.at[batch, 1], yrecv.at[batch, 0], *s, at(1, 0))),
                (exists(-1, 0), remote(ysend.at[batch, 0], yrecv.at[batch, 1], *s, at(-1, 0)))]

    def x_copies(batch):
        s = send_x, h_recv.at[3 + batch]
        return [(exists(0, 1), remote(xsend.at[batch], xrecv.at[batch, 0], *s, at(0, 1))),
                (exists(0, -1), remote(xsend.at[batch], xrecv.at[batch, 1], *s, at(0, -1)))]

    def z_device(d):
        return {"gx": ix, "gy": iy, "gz": iz + d}

    z_up = remote(u.at[:, nz, own], u.at[:, 0, own], send_z, h_recv.at[0], z_device(1))
    z_down = remote(u.at[:, 1, own], u.at[:, nz + 1, own], send_z, h_recv.at[0], z_device(-1))
    has_below, has_above = iz > 0, iz < ngz - 1

    start(y_copies(0))
    start(x_copies(0))
    start([(has_above, z_up), (has_below, z_down)])
    for n, dy, dx in ((1, -1, 0), (0, 1, 0), (3, 0, 1)):
        @pl.when(exists(dy, dx))
        def _(n=n, dy=dy, dx=dx):
            pl.semaphore_signal(near.at[n], inc=1, device_id=at(dy, dx), device_id_type=MESH)
    signal_peers(near.at[2])

    def counted(count, cases, descriptor, done):
        for n, ref in cases:
            @pl.when(count == n)
            def _(ref=ref):
                done(descriptor(ref))

    def wait_many(count, cases, send, recv, sent):
        counted(count, cases, lambda ref: remote(ref, ref, send, recv, z_device(0)),
                (lambda c: c.wait_send()) if sent else (lambda c: c.wait_recv()))

    def wait_y(batch):
        wait_many(beside_y, ((1, yrecv.at[batch, 0]), (2, yrecv.at[batch])), send_y, h_recv.at[1 + batch], False)

    def wait_x(batch):
        wait_many(beside_x, ((1, xrecv.at[batch, 0]), (2, xrecv.at[batch])), send_x, h_recv.at[3 + batch], False)

    beside_z = has_below.astype(jnp.int32) + has_above.astype(jnp.int32)
    z_cases = ((1, u.at[:, 1, own]), (2, u.at[:, 1:3, own]))

    for i in range(2):
        values = []
        for z in range(nz):
            c = u[1 + i, z + 1, own, :]
            for side, at_row in ((0, 0), (1, ny - 1)):
                ysend[1, side, i * nz + z:i * nz + z + 1, :] = c[at_row:at_row + 1]
            values += [(z, g, c[g * HALO:(g + 1) * HALO]) for g in range(groups)]
        packed = packed_columns(values)
        for t in range(xtiles):
            xsend[1, i, t] = packed[t]
    start(x_copies(1))
    start(y_copies(1))
    raw_group8 = group8 - raw_lane // (2 * HALO)

    def lanes_of(g):
        return (g % per) * 2 * nz

    for i in range(2):
        here, swap = nil8, nil8
        for side in range(2):
            for k in range(layers):
                rows = slice(i * nz + k * HALO, i * nz + (k + 1) * HALO)
                for other in range(2):
                    slot = (side if not other else 1 - side) * layers + k
                    moved = pltpu.roll(ysend[0, side, rows, :], (raw_lane + 2 * HALO * slot + HALO) % nx, 1)
                    if other:
                        swap = jnp.where(raw_group8 == slot, moved, swap)
                    else:
                        here = jnp.where(raw_group8 == slot, moved, here)
        rpsend[i] = here
        for side, g in ends:
            column = xsend[0, i, g // per]
            if lanes_of(g):
                column = pltpu.roll(column, nx - lanes_of(g), 1)
            dsend[side, i] = jnp.where(lane8 < 2 * nz, column, swap)

    def ways(dy, dx, copy):
        @pl.when(exists(dy, dx))
        def _():
            copy.start()

    for dx in (-1, 1):
        ways(0, dx, remote(rpsend, cxrecv.at[(1 - dx) // 2, ngz * nstrips:], send_cx, h_recv.at[5], at(0, dx)))
    for dy in (-1, 1):
        ways(dy, 0, remote(dsend.at[(1 + dy) // 2], cyrecv.at[(1 - dy) // 2, ngz * PLANES:], send_cy, h_recv.at[5], at(dy, 0)))

    def known(n, dy, dx):
        @pl.when(exists(dy, dx))
        def _():
            pl.semaphore_wait(near.at[n], 1)

    def raw_corner(dy, dx):
        ways(dy, dx, remote(dsend.at[(1 + dy) // 2], cdrecv.at[(1 - dy) + (1 - dx) // 2, ngz:], send_cd, h_recv.at[6], at(dy, dx)))


    layer_of_lane = lax.rem(lane8[0:1], 2 * nz) // 2
    lanek = [jnp.zeros((1, nx), f32) for _ in range(3)]
    for z in range(nz):
        for k in range(3):
            value = coefficient(ktab, z, 0, k)
            rowk[k, z:z + 1, :] = jnp.full((1, nx), value, f32)
            lanek[k] = jnp.where(layer_of_lane == z, value, lanek[k])
    loads[2].wait()
    loads[3].wait()

    known(0, -1, 0)
    raw_corner(-1, -1)
    raw_corner(-1, 1)
    signal_peers(far.at[0])

    def tile_of(g):
        return slice(g * HALO, (g + 1) * HALO)

    def padded(g, shift):
        return slice(HALO + g * HALO + shift, HALO + (g + 1) * HALO + shift)

    def assemble(g):
        rows, tile = padded(g, 0), tile_of(g)
        res, dia, s_y, s_x, h_x, h_y, h_z = (nil8,) * 7
        for z in range(nz):
            v = poreb[z].astype(f32)[tile]
            k00 = coefficient(ktab, z, 0, 0)
            m0 = [coefficient(mtab, z, 0, k) for k in range(3)]
            r = u[3, z + 1, rows, :]
            typ = 1.0 / (r + u[3, z + 1, padded(g, 1), :])
            if g == groups - 1:
                typ = jnp.where(row8 < HALO - 1, typ, 0.0)
            xp = jnp.where(last8, 0.0, 1.0 / (r + pltpu.roll(r, nx - 1, 1)))
            ty[z, rows, :] = typ
            txp[z, tile, :] = xp
            pc = pcb[z, rows, :]
            h_x = h_x + xp * (pc - pltpu.roll(pc, nx - 1, 1))
            h_y = h_y + typ * (pc - pcb[z, padded(g, 1), :])
            c = [u[k, z + 1, rows, :] for k in range(3)]
            res = res + (rhs[0, z, tile, :] - v * (m0[0] * c[0] + m0[1] * c[1] + m0[2] * c[2]))
            dia = dia + v * m0[0]
            s_y = s_y + k00 * typ
            s_x = s_x + k00 * xp
            if z < nz - 1:
                dk = [coefficient(ktab, z, 0, k) - coefficient(ktab, z + 1, 0, k) for k in range(3)]
                t = 1.0 / (r + u[3, z + 2, rows, :])
                tzf[z + 1, tile, :] = t
                d = [c[k] - u[k, z + 2, rows, :] for k in range(3)]
                h_z = h_z + t * (dk[0] * d[0] + dk[1] * d[1] + dk[2] * d[2])
        return res, dia, s_y, s_x, h_x, h_y, h_z

    s_res, s_dia, s_ty, s_tx, s_hx, s_hy, s_z = (list(c) for c in zip(*(assemble(g) for g in range(groups))))

    for g in range(groups):
        shifted[0, padded(g, 0), :] = s_hy[g]
        shifted[1, padded(g, 0), :] = s_ty[g]
    p_rhs, p_dia = [], []
    for g in range(groups):
        p_rhs.append(s_res[g] - s_z[g] - (s_hx[g] - pltpu.roll(s_hx[g], 1, 1)) - (s_hy[g] - shifted[0, padded(g, -1), :]))
        p_dia.append(s_dia[g] + s_ty[g] + shifted[1, padded(g, -1), :] + s_tx[g] + pltpu.roll(s_tx[g], 1, 1))

    wait_many(beside_z, z_cases, send_z, h_recv.at[0], False)
    for slot, z, inside in ((0, 0, 1), (nz + 1, nz - 1, nz)):
        k0 = [coefficient(ktab, z, 0, k) for k in range(3)]
        for g in range(groups):
            rows = padded(g, 0)
            there = u[3, slot, rows, :]
            t = jnp.where(there > 0.0, 1.0 / (u[3, inside, rows, :] + there), 0.0)
            tzf[0 if slot == 0 else nz, tile_of(g), :] = t
            d = [u[k, inside, rows, :] - u[k, slot, rows, :] for k in range(3)]
            p_rhs[g] = p_rhs[g] - t * (k0[0] * d[0] + k0[1] * d[1] + k0[2] * d[2])
    mine = [[swapped(xsend[0, i, t]) for t in range(xtiles)] for i in range(2)]

    planes = [p_rhs, p_dia, s_ty, s_tx]
    for p in range(PLANES):
        ystrips[0, p] = planes[p][0]
        ystrips[1, p] = planes[p][groups - 1]
    for i, tiles in enumerate(packing):
        strip = nil8
        for j, g in enumerate(tiles):
            for p in range(PLANES):
                slot = j * PLANES + p
                strip = jnp.where(group8 == slot, pltpu.roll(planes[p][g], (2 * HALO * slot + HALO) % nx, 1), strip)
        strips[i] = strip

    def to_all(dy, dx, src, dst, send, recv, parts=range(ngz)):
        return [(exists(dy, dx), remote(src, dst, send, c_recv.at[recv],
                                        {"gx": ix + dx, "gy": iy + dy, "gz": lax.rem(iz + d, ngz)})) for d in parts]

    def corner_strips(dy, dx, parts):
        start(to_all(dy, dx, strips.at[0 if dy < 0 else last_head], cdrecv.at[(1 - dy) + (1 - dx) // 2, iz], send_cd, 3, parts))

    pl.semaphore_wait(far.at[0], ngz - 1)
    pl.semaphore_wait(near.at[2], ngz - 1)
    corner_strips(-1, -1, range(ngz))
    corner_strips(-1, 1, range(ngz))
    known(3, 0, -1)
    raw_corner(1, -1)
    corner_strips(1, -1, range(1))
    for dx in (-1, 1):
        start(to_all(0, dx, strips, cxrecv.at[(1 - dx) // 2, pl.ds(iz * nstrips, nstrips)], send_cx, 2))
    for dy in (-1, 1):
        start(to_all(dy, 0, ystrips.at[(1 + dy) // 2], cyrecv.at[(1 - dy) // 2, pl.ds(iz * PLANES, PLANES)], send_cy, 1))

    for f in range(ktab.shape[1]):
        values = block_scalars([[mtab[r, f, c] for c in range(3)] for r in range(3)],
                               [[ktab[r, f, c] for c in range(3)] for r in range(3)])
        for i, value in enumerate(values):
            ctab[i, f] = value

    known(1, 1, 0)
    raw_corner(1, 1)
    signal_peers(far.at[1])
    corner_strips(1, 1, range(1))

    def inside(z, _):
        f = facies[z]
        kinv = [[ctab[KINV + 3 * r + c, f] for c in range(3)] for r in range(3)]
        for g in range(groups):
            rows = padded(g, 0)
            tile = tile_of(g)
            tzm, tzp = tzf[z, tile, :], tzf[z + 1, tile, :]
            typ, tym = ty[z, rows, :], ty[z, padded(g, -1), :]
            xp = txp[z, tile, :]
            xm = pltpu.roll(xp, 1, 1)
            tz = tzm + tzp
            tzs[z, tile, :] = tz
            txm[z, tile, :] = xm
            qv[0, z, tile, :] = tz + (typ + tym) + (xp + xm)
            given = [rhs[k, z, tile, :] for k in range(3)]
            for k in range(3):
                c = u[k, z + 1, rows, :]
                w[k, z, tile, :] = ((tzp * u[k, z + 2, rows, :] + tzm * u[k, z, rows, :])
                                    + (typ * u[k, z + 1, padded(g, 1), :] + tym * u[k, z + 1, padded(g, -1), :])
                                    + (xp * pltpu.roll(c, nx - 1, 1) + xm * pltpu.roll(c, 1, 1))
                                    + (kinv[k][0] * given[0] + kinv[k][1] * given[1] + kinv[k][2] * given[2]))
        return 0

    def layers_of(step, begin, end):
        for z in range(begin, end):
            step(z, 0)

    layers_of(inside, 0, nz // 2)
    pl.semaphore_wait(far.at[1], ngz - 1)
    corner_strips(1, -1, range(1, ngz))
    corner_strips(1, 1, range(1, ngz))
    layers_of(inside, nz // 2, nz)

    wait_y(0)
    top8, bottom8 = row8 == 0, row8 == HALO - 1
    lines = nil8
    y_faces = []
    for side, g, here in ((0, 0, top8), (1, groups - 1, bottom8)):
        there = yrecv[0, side, nz:, :]
        t = jnp.where(there > 0.0, 1.0 / (ysend[0, side, nz:, :] + there), 0.0)
        moved = jnp.sum(t * (ysend[0, side, :nz, :] - yrecv[0, side, :nz, :]), axis=0, keepdims=True)
        weight = jnp.sum(rowk[0] * t, axis=0, keepdims=True)
        lines = jnp.where(row8 == 2 * side, moved, jnp.where(row8 == 2 * side + 1, weight, lines))
        y_faces.append((side, g, here, t, moved, weight))
    wait_x(0)
    flux, weights, faces, outside = [], [], [], []
    for t in range(xtiles):
        there = [jnp.where(even8, xrecv[0, 0, i, t], xrecv[0, 1, i, t]) for i in range(2)]
        face = jnp.where(there[1] > 0.0, 1.0 / (mine[1][t] + there[1]), 0.0)
        flux.append(face * (mine[0][t] - there[0]))
        weights.append(face * lanek[0])
        faces.append(face)
        outside.append(there[0])

    def sums_of(flux, weights, low):
        block = jnp.logical_and(lane8 >= low, lane8 < low + 2 * nz)
        sums = []
        for values in (flux, weights):
            for parity in (even8, jnp.logical_not(even8)):
                sums.append(jnp.sum(jnp.where(jnp.logical_and(block, parity), values, 0.0), axis=1, keepdims=True))
        return sums

    def at_sides(left, right):
        return jnp.where(first8, left, jnp.where(last8, right, 0.0))

    for side, g, here, t, moved, weight in y_faces:
        for p, change in ((0, -moved), (1, weight), (2, weight))[:3 if side else 2]:
            planes[p][g] = planes[p][g] + jnp.where(here, change, 0.0)
        for z in range(nz):
            edge_row = HALO - 1 + side * ny
            ty[z, edge_row:edge_row + 1, :] = t[z:z + 1]
    zplanes[iz, PLANES * groups] = lines
    for i, tiles in enumerate(packing):
        across = nil8
        for j, g in enumerate(tiles):
            flux_l, flux_r, weight_l, weight_r = sums_of(flux[g // per], weights[g // per], lanes_of(g))
            for p, change in ((0, at_sides(-flux_l, -flux_r)), (1, at_sides(weight_l, weight_r)),
                              (3, jnp.where(last8, weight_r, 0.0))):
                planes[p][g] = planes[p][g] + change
            for p, left, right in ((0, flux_l, flux_r), (1, weight_l, weight_r), (3, weight_l, 0.0)):
                slot = (j * PLANES + p) * 2 * HALO
                across = jnp.where(lane8 == slot + HALO - 1, left, jnp.where(lane8 == slot + HALO, right, across))
        zplanes[iz, PLANES * groups + 1 + i] = across
    for p in range(PLANES):
        for g in range(groups):
            zplanes[iz, p * groups + g] = planes[p][g]
    for d in range(1, ngz):
        remote(zplanes.at[iz, 0:first_part], zplanes.at[iz, 0:first_part], send_cz, c_recv.at[0],
               {"gx": ix, "gy": iy, "gz": lax.rem(iz + d, ngz)}).start()

    wait_y(1)
    wait_x(1)
    invrow = 1.0 / rowk[0]
    for side, _, _, t, _, _ in y_faces:
        one, two_ = yrecv[1, side, :nz, :], yrecv[1, side, nz:, :]
        zero_ = (yrecv[0, side, :nz, :] - rowk[1] * one - rowk[2] * two_) * invrow
        for k, x in enumerate((zero_, one, two_)):
            yedge[side, k] = t * x
        yedge[side, 3] = t
    invlane = 1.0 / lanek[0]
    for t in range(xtiles):
        one, two_ = (jnp.where(even8, xrecv[1, 0, i, t], xrecv[1, 1, i, t]) for i in range(2))
        zero_ = (outside[t] - lanek[1] * one - lanek[2] * two_) * invlane
        for k, x in enumerate((zero_, one, two_)):
            edge[k, t] = swapped(faces[t] * x)
        edge[3, t] = swapped(faces[t])

    outer8 = jnp.logical_or(first8, last8)

    def solve(z, _):
        volume = poreb[z].astype(f32)
        f = facies[z]
        n = [[ctab[NMAT + 3 * r + c, f] for c in range(3)] for r in range(3)]
        adj = [[ctab[NADJ + 3 * r + c, f] for c in range(3)] for r in range(3)]
        dia = [ctab[NDIA + i, f] for i in range(3)]
        trace, minors, det_n = ctab[NTR, f], ctab[NC2, f], ctab[NDET, f]
        for g in range(groups):
            tile = tile_of(g)
            shift = (2 * nx - (lanes_of(g) + 1) - 2 * z) % nx
            added = [jnp.where(outer8, pltpu.roll(edge[k, g // per], shift, 1), 0.0) for k in range(4)]
            txp[z, tile, :] = txp[z, tile, :] + jnp.where(last8, added[3], 0.0)
            txm[z, tile, :] = txm[z, tile, :] + jnp.where(first8, added[3], 0.0)
            for side, head in ends:
                if g == head:
                    here = top8 if side == 0 else bottom8
                    added = [added[k] + jnp.where(here, yedge[side, k, z:z + 1, :], 0.0) for k in range(4)]
            b = [w[r, z, tile, :] + added[r] for r in range(3)]
            v = volume[tile]
            s = (qv[0, z, tile, :] + added[3]) * (1.0 / v)
            e = [[s * (s + dia[r]) + adj[r][r] if r == c else adj[r][c] - s * n[r][c] for c in range(3)] for r in range(3)]
            det = ((s + trace) * s + minors) * s + det_n
            inv = 1.0 / (v * det)
            for r in range(3):
                w[r, z, tile, :] = (e[r][0] * b[0] + e[r][1] * b[1] + e[r][2] * b[2]) * inv
                qv[r, z, tile, :] = e[r][0] * inv
        return 0

    most = nz * 5 // 8
    layers_of(solve, 0, most)

    corners = beside_y * beside_x
    wait_many(beside_y + beside_x, [(n, zplanes.at[0, 0:2 * n]) for n in range(1, 5)], send_cx, h_recv.at[5], False)
    wait_many(corners, ((1, cdrecv.at[0, ngz:]), (2, cdrecv.at[0:2, ngz:]), (4, cdrecv.at[:, ngz:])), send_cd, h_recv.at[6], False)
    from_top = raw_group8 < layers
    ours, theirs = [], []
    for i in range(2):
        ours.append(jnp.where(left_part, cxrecv[0, ngz * nstrips + i], cxrecv[1, ngz * nstrips + i]))
        theirs.append(jnp.where(from_top, jnp.where(left_part, cdrecv[0, ngz + i], cdrecv[1, ngz + i]),
                                jnp.where(left_part, cdrecv[2, ngz + i], cdrecv[3, ngz + i])))
    t = jnp.where(jnp.logical_and(raw_group8 >= 0, theirs[1] > 0.0), 1.0 / (ours[1] + theirs[1]), 0.0)
    pattern = nil8
    for k in range(layers):
        pattern = jnp.where(lax.rem(group8, layers) == (k + raw_lane // (2 * HALO)) % layers, rowk[0, k * HALO:(k + 1) * HALO, :], pattern)
    both = jnp.where(top8, jnp.sum(t * (ours[0] - theirs[0]), axis=0, keepdims=True),
                     jnp.sum(t * pattern, axis=0, keepdims=True))
    summed = both
    for k in range(1, layers):
        summed = summed + pltpu.roll(both, nx - 2 * HALO * k, 1)
    upper = pltpu.roll(summed, (2 * nx - raw_lane - HALO) % nx, 1)
    lower = pltpu.roll(summed, (2 * nx - raw_lane - 2 * HALO * layers - HALO) % nx, 1)
    zplanes[iz, first_part] = jnp.where(row8 < 2, upper, pltpu.roll(lower, 2, 0))
    for side, g in ends:
        tiles = [swapped(cyrecv[side, ngz * PLANES + i]) for i in range(2)]
        there = [jnp.where(even8, cdrecv[2 * side, ngz + i], cdrecv[2 * side + 1, ngz + i]) for i in range(2)]
        face = jnp.where(there[1] > 0.0, 1.0 / (tiles[1] + there[1]), 0.0)
        flux_l, flux_r, weight_l, weight_r = sums_of(face * (tiles[0] - there[0]), face * lanek[0], 0)
        for n, tile in enumerate((at_sides(-flux_l, -flux_r), at_sides(weight_l, weight_r),
                                  at_sides(flux_r, flux_l), at_sides(weight_r, weight_l))):
            zplanes[iz, first_part + 1 + 4 * side + n] = tile
    for d in range(1, ngz):
        remote(zplanes.at[iz, first_part:], zplanes.at[iz, first_part:], send_cz, c_recv.at[4],
               {"gx": ix, "gy": iy, "gz": lax.rem(iz + d, ngz)}).start()
    layers_of(solve, most, nz)

    if ngz > 1:
        others = zplanes.at[0:ngz - 1, 0:first_part]
        remote(others, others, send_cz, c_recv.at[0], z_device(0)).wait_recv()
    y_early, x_early = slice(0, ngz * PLANES), slice(0, ngz * nstrips)
    wait_many(beside_y, ((1, cyrecv.at[0, y_early]), (2, cyrecv.at[:, y_early])), send_cy, c_recv.at[1], False)
    wait_many(beside_x, ((1, cxrecv.at[0, x_early]), (2, cxrecv.at[:, x_early])), send_cx, c_recv.at[2], False)
    wait_many(corners, ((1, cdrecv.at[0, 0:ngz]), (2, cdrecv.at[0:2, 0:ngz]), (4, cdrecv.at[:, 0:ngz])), send_cd, c_recv.at[3], False)

    def gathered(part):
        total = part(0)
        for i in range(1, ngz):
            total = total + part(i)
        return total

    tiles_in = groups + 2
    side_tiles = [jnp.where(left_part, gathered(lambda i: cxrecv[0, i * nstrips + t]), gathered(lambda i: cxrecv[1, i * nstrips + t]))
                  + gathered(lambda i: zplanes[i, PLANES * groups + 1 + t]) for t in range(nstrips)]
    corner_tiles = [jnp.where(left_part, gathered(lambda i: cdrecv[2 * v, i]), gathered(lambda i: cdrecv[2 * v + 1, i]))
                    for v in range(2)]
    where_is = {g: (i, j) for i, tiles in enumerate(packing) for j, g in enumerate(tiles)}
    on_right, on_left = lane8 < HALO, lane8 >= nx - HALO
    strip8 = jnp.logical_or(on_right, on_left)

    def border_of(p, g):
        if 0 <= g < groups:
            i, j = where_is[g]
            tile, slot = side_tiles[i], j * PLANES + p
        else:
            tile, slot = corner_tiles[0 if g < 0 else 1], p
        return jnp.where(strip8, pltpu.roll(tile, (2 * nx - 2 * HALO * slot - HALO) % nx, 1), 0.0)

    b = [[border_of(p, g) for g in range(-1, groups + 1)] for p in range(PLANES)]
    own_lines = gathered(lambda i: zplanes[i, PLANES * groups])
    a = [[gathered(lambda i: cyrecv[0, i * PLANES + p])] + [gathered(lambda i: zplanes[i, p * groups + g]) for g in range(groups)]
         + [gathered(lambda i: cyrecv[1, i * PLANES + p])] for p in range(PLANES)]

    def beyond(grid, lines):
        for side, t, here in ((0, 0, bottom8), (1, tiles_in - 1, top8)):
            moved, weight = lines[2 * side:2 * side + 1], lines[2 * side + 1:2 * side + 2]
            for p, change in ((0, moved), (1, weight), (2, weight))[:2 if side else 3]:
                grid[p][t] = grid[p][t] + jnp.where(here, change, 0.0)

    beyond(a, own_lines)

    def east(ra, rb):
        return jnp.where(last8, rb, ra), jnp.where(last8, ra, rb)

    def west(ra, rb):
        return jnp.where(first8, rb, ra), jnp.where(first8, ra, rb)

    def fill(buffer, s, tiles):
        for t in range(tiles_in):
            field[buffer, s, (t + 1) * HALO:(t + 2) * HALO, :] = tiles[t]

    def above(buffer, s, t):
        return field[buffer, s, (t + 1) * HALO - 1:(t + 2) * HALO - 1, :]

    def below(buffer, s, t):
        return field[buffer, s, (t + 1) * HALO + 1:(t + 2) * HALO + 1, :]

    terms = [[None] * tiles_in for _ in range(2)]
    grids = (a, b)

    def prepare(s, t):
        rhs_, dia, down, right = (grids[s][p][t] for p in range(PLANES))
        there = dia > 0.0
        inv = jnp.where(there, RELAX / jnp.where(there, dia, 1.0), 0.0)
        left = west(*(pltpu.roll(grid[3][t], 1, 1) for grid in grids))[s]
        terms[s][t] = [rhs_ * inv, down * inv, above(0, s, t) * inv, right * inv, left * inv]

    fill(0, 0, a[2])
    late_b = (0, 1, groups, groups + 1)
    for t in range(1, tiles_in - 1):
        prepare(0, t)

    if ngz > 1:
        rest = zplanes.at[0:ngz - 1, first_part:]
        remote(rest, rest, send_cz, c_recv.at[4], z_device(0)).wait_recv()
    lines = jnp.where(strip8, gathered(lambda i: zplanes[i, first_part]), 0.0)
    beyond(b, lines)
    for side, t, here in ((0, 1, top8), (1, groups, bottom8)):
        moved, weight = lines[2 * side:2 * side + 1], lines[2 * side + 1:2 * side + 2]
        for p, change in ((0, -moved), (1, weight), (2, weight))[:3 if side else 2]:
            b[p][t] = b[p][t] + jnp.where(here, change, 0.0)
    fill(0, 1, b[2])
    for t in range(1, tiles_in - 1):
        prepare(1, t)
    for side, t in ((0, 0), (1, tiles_in - 1)):
        flux_, weight_, flux_past, weight_past = (
            gathered(lambda i: zplanes[i, first_part + 1 + 4 * side + n]) for n in range(4))
        for grid, change, weight in ((a, flux_, weight_), (b, flux_past, weight_past)):
            grid[0][t] = grid[0][t] + change
            grid[1][t] = grid[1][t] + weight
            grid[3][t] = grid[3][t] + jnp.where(last8, weight, 0.0)
        for s in range(2):
            prepare(s, t)

    c = [[terms[s][t][0] for t in range(tiles_in)] for s in range(2)]
    for sweep in range(1, SWEEPS):
        buffer = sweep % 2
        for s in range(2):
            fill(buffer, s, c[s])
        nxt = [[None] * tiles_in for _ in range(2)]
        for t in range(tiles_in):
            e = east(*(pltpu.roll(c[s][t], nx - 1, 1) for s in range(2)))
            ws = west(*(pltpu.roll(c[s][t], 1, 1) for s in range(2)))
            for s in range(2):
                r, tyn, tys, txe, txw = terms[s][t]
                nxt[s][t] = (((1.0 - RELAX) * c[s][t] + r) + (tyn * below(buffer, s, t) + tys * above(buffer, s, t))
                             + (txe * e[s] + txw * ws[s]))
        c = nxt
    for t in range(tiles_in):
        rows = slice(t * HALO, (t + 1) * HALO)
        final[0, rows, :] = c[0][t]
        if 0 < t < tiles_in - 1:
            final[1, rows, :] = east(*(pltpu.roll(c[s][t], nx - 1, 1) for s in range(2)))[0]
            final[2, rows, :] = west(*(pltpu.roll(c[s][t], 1, 1) for s in range(2)))[0]
    for count, cases, sem in (
        (beside_y, ((1, yrecv.at[0]), (2, yrecv)), send_y),
        (beside_x, ((1, xrecv.at[0]), (2, xrecv)), send_x),
        (beside_z, z_cases, send_z),
        (beside_y, ((1, cyrecv.at[0]), (2, cyrecv)), send_cy),
        (beside_x, ((1, cxrecv.at[0]), (2, cxrecv)), send_cx),
        (corners, ((1, cdrecv.at[0]), (2, cdrecv.at[0:2]), (4, cdrecv)), send_cd),
    ):
        wait_many(count, cases, sem, h_recv.at[0], True)
    if ngz > 1:
        others = zplanes.at[0:ngz - 1]
        remote(others, others, send_cz, c_recv.at[0], z_device(0)).wait_send()


def finish_kernel(parts, w, qv, tzs, ty, txp, txm, final, new_hbm, corr_hbm, out, out_sem):
    nz, ny, nx = tzs.shape
    own = slice(HALO, HALO + ny)
    corr = pltpu.make_async_copy(final.at[0, own], corr_hbm, out_sem.at[parts])
    corr.start()
    cc, ce, cw = (final[k, own, :] for k in range(3))
    cn, cs = final[0, HALO + 1:HALO + 1 + ny, :], final[0, HALO - 1:HALO - 1 + ny, :]

    def finish(z, _):
        g = (tzs[z] * cc + ty[z, own, :] * cn + ty[z, HALO - 1:HALO + ny - 1, :] * cs
             + txp[z] * ce + txm[z] * cw)
        for r in range(3):
            out[r, z] = w[r, z] + qv[r, z] * g
        return 0

    step = nz // parts
    outs = [corr]
    for part in range(parts):
        lax.fori_loop(part * step, (part + 1) * step, finish, 0)
        chunk = slice(part * step, (part + 1) * step)
        outs.append(pltpu.make_async_copy(out.at[:, chunk], new_hbm.at[:, chunk], out_sem.at[part]))
        outs[-1].start()
    for copy in outs:
        copy.wait()


def per_device(sizes, state, right_side, permeability, pore_volume, facies, storage_table, coupling_table):
    _, nz, ny, nx = state.shape
    sizes = sizes + (nz, ny, nx)
    f32 = jnp.float32
    ngz = sizes[2]
    cells = (nz, ny, nx)
    vmem = lambda *shape: pltpu.VMEM(shape, f32)
    hbm = pl.BlockSpec(memory_space=pltpu.HBM)
    dma = lambda n: pltpu.SemaphoreType.DMA((n,))
    ey = ny + 2 * HALO
    groups, per, xtiles = column_plan(nz, ny, nx)
    strips = len(strip_plan(ny, nx))
    facets = storage_table.shape[0]
    in_vmem = pl.BlockSpec(memory_space=pltpu.VMEM)
    handed = 4 * nx * (9 * nz * ny + nz * ey + 3 * ey)
    limit = 16384 * ((VMEM_BYTES - handed) // 16384)
    middle = pl.pallas_call(
        functools.partial(kernel, sizes),
        out_shape=(vmem(3, *cells), vmem(3, *cells), vmem(*cells), vmem(nz, ey, nx), vmem(*cells), vmem(*cells),
                   vmem(3, ey, nx)),
        in_specs=[hbm, hbm, hbm, hbm, hbm, hbm, hbm],
        out_specs=(in_vmem,) * 7,
        scratch_shapes=[
            vmem(4, nz + 2, ey, nx), vmem(nz, ey, nx), vmem(3, *cells),
            pltpu.VMEM(cells, permeability.dtype), pltpu.VMEM(cells, pore_volume.dtype),
            vmem(2, 2, 2 * nz, nx), vmem(2, 2, 2 * nz, nx),
            vmem(2, 2, xtiles, HALO, nx), vmem(2, 2, 2, xtiles, HALO, nx), vmem(4, xtiles, HALO, nx),
            vmem(3, nz, nx), vmem(nz + 1, ny, nx), vmem(2, ey, nx),
            vmem(ngz, PLANES * groups + 1 + strips + 9, HALO, nx), vmem(2, PLANES, HALO, nx), vmem(strips, HALO, nx),
            vmem(2, ngz * PLANES + 2, HALO, nx), vmem(2, ngz * strips + 2, HALO, nx), vmem(4, ngz + 2, HALO, nx),
            vmem(2, HALO, nx), vmem(2, 2, HALO, nx), vmem(2, 4, nz, nx), vmem(2, 2, ey + 2 * HALO, nx),
            pltpu.SMEM((nz,), facies.dtype), pltpu.SMEM((3, facets, 3), f32), pltpu.SMEM((3, facets, 3), f32),
            pltpu.SMEM((NCOEF, facets), f32),
            pltpu.SemaphoreType.REGULAR((4,)), pltpu.SemaphoreType.REGULAR((2,)), dma(7), dma(7), dma(5),
        ],
        compiler_params=pltpu.CompilerParams(collective_id=0, has_side_effects=True, vmem_limit_bytes=limit),
        name="cpr_apply",
    )(facies, storage_table.transpose(1, 0, 2), coupling_table.transpose(1, 0, 2),
      state, right_side, permeability, pore_volume)
    parts = 8 if nz % 8 == 0 else 1
    return tuple(pl.pallas_call(
        functools.partial(finish_kernel, parts),
        out_shape=(jax.ShapeDtypeStruct(state.shape, f32), jax.ShapeDtypeStruct((ny, nx), f32)),
        in_specs=[in_vmem] * 7,
        out_specs=(hbm, hbm),
        scratch_shapes=[vmem(3, *cells), dma(parts + 1)],
        compiler_params=pltpu.CompilerParams(vmem_limit_bytes=16 * 2**20),
        name="cpr_finish",
    )(*middle))


def solution(mesh):
    sizes = (mesh.shape["gx"], mesh.shape["gy"], mesh.shape["gz"])
    return jax.shard_map(
        functools.partial(per_device, sizes),
        mesh=mesh,
        in_specs=(
            P(None, "gz", "gy", "gx"),
            P(None, "gz", "gy", "gx"),
            P("gz", "gy", "gx"),
            P("gz", "gy", "gx"),
            P("gz"),
            P(),
            P(),
        ),
        out_specs=(P(None, "gz", "gy", "gx"), P("gy", "gx")),
        check_vma=False,
    )
```

```python
import functools
import jax
import jax.numpy as jnp
from jax import lax
from jax.experimental import pallas as pl
from jax.experimental.pallas import tpu as pltpu
from jax.sharding import PartitionSpec as P

SWEEPS = 8
RELAX = 0.8
MESH = pl.DeviceIdType.MESH
HALO = 8
VMEM_BYTES = 67043328

PLANES = 4
SIDES = [(-1, 0), (1, 0), (0, -1), (0, 1), (-1, -1), (-1, 1), (1, -1), (1, 1)]

KINV, NMAT, NADJ, NDIA, NTR, NC2, NDET, NCOEF = 0, 9, 18, 27, 30, 31, 32, 33


def cofactor(e, r, c):
    return (e[(r + 1) % 3][(c + 1) % 3] * e[(r + 2) % 3][(c + 2) % 3]
            - e[(r + 1) % 3][(c + 2) % 3] * e[(r + 2) % 3][(c + 1) % 3])


def block_scalars(m, k):
    kf = [[cofactor(k, r, c) for c in range(3)] for r in range(3)]
    inv = 1.0 / (k[0][0] * kf[0][0] + k[0][1] * kf[0][1] + k[0][2] * kf[0][2])
    kinv = [[kf[c][r] * inv for c in range(3)] for r in range(3)]
    n = [[kinv[r][0] * m[0][c] + kinv[r][1] * m[1][c] + kinv[r][2] * m[2][c] for c in range(3)] for r in range(3)]
    nf = [[cofactor(n, r, c) for c in range(3)] for r in range(3)]
    trace = n[0][0] + n[1][1] + n[2][2]
    return ([kinv[r][c] for r in range(3) for c in range(3)] + [n[r][c] for r in range(3) for c in range(3)]
            + [nf[c][r] for r in range(3) for c in range(3)] + [trace - n[i][i] for i in range(3)]
            + [trace, nf[0][0] + nf[1][1] + nf[2][2], n[0][0] * nf[0][0] + n[0][1] * nf[0][1] + n[0][2] * nf[0][2]])


def column_plan(nz, ny, nx):
    groups = ny // HALO
    per = nx // (2 * nz)
    return groups, per, -(-groups // per)


def strip_plan(ny, nx):
    groups = ny // HALO
    per = nx // (2 * HALO * PLANES)
    heads = [0] if groups == 1 else [0, groups - 1]
    others = list(range(1, groups - 1))
    packed = [[head] + [others.pop(0) for _ in range(per - 1) if others] for head in heads]
    while others:
        packed.append([others.pop(0) for _ in range(per) if others])
    return packed


def kernel(sizes, facies_hbm, mtab_hbm, ktab_hbm, state_hbm, rhs_hbm, perm_hbm, pore_hbm,
           w, qv, tzs, ty, txp, txm, final,
           u, pcb, rhs, permb, poreb, ysend, yrecv, xsend, xrecv, edge, rowk, tzf, shifted,
           zplanes, ystrips, strips, cyrecv, cxrecv, cdrecv, rpsend, dsend, swsend, yedge, field,
           facies, mtab, ktab, ctab, near, far, in_sem, h_recv, c_recv):
    ngx, ngy, ngz, nz, ny, nx = sizes
    ix, iy, iz = lax.axis_index("gx"), lax.axis_index("gy"), lax.axis_index("gz")
    own = slice(HALO, HALO + ny)
    groups, per, xtiles = column_plan(nz, ny, nx)
    packing = strip_plan(ny, nx)
    nstrips = len(packing)
    last_head = len(packing[:2]) - 1
    layers = nz // HALO
    ends = ((0, 0), (1, groups - 1))
    first_part = PLANES * groups + 1 + nstrips
    raw_lane = nx - 4 * HALO * layers
    assert nz % HALO == 0 and raw_lane >= 2 * nz
    f32 = jnp.float32
    send_y, send_x, send_z, send_cy, send_cx, send_cd, send_cz = (in_sem.at[i] for i in (0, 1, 4, 5, 6, 2, 3))

    def exists(dy, dx):
        ok = None
        for d, i, n in ((dy, iy, ngy), (dx, ix, ngx)):
            if d:
                here = (i > 0) if d < 0 else (i < n - 1)
                ok = here if ok is None else jnp.logical_and(ok, here)
        return ok

    def at(dy, dx):
        return {"gx": ix + dx, "gy": iy + dy, "gz": iz}

    barrier = pltpu.get_barrier_semaphore()
    for side in (SIDES[0], SIDES[2], SIDES[1], SIDES[3]):
        @pl.when(exists(*side))
        def _(side=side):
            pl.semaphore_signal(barrier, inc=1, device_id=at(*side), device_id_type=MESH)

    def signal_peers(sem):
        for d in range(1, ngz):
            pl.semaphore_signal(sem, inc=1, device_id={"gx": ix, "gy": iy, "gz": lax.rem(iz + d, ngz)},
                                device_id_type=MESH)

    signal_peers(barrier)

    loads = [
        pltpu.make_async_copy(perm_hbm, permb, in_sem.at[0]),
        pltpu.make_async_copy(state_hbm, u.at[0:3, 1:nz + 1, own], in_sem.at[1]),
        pltpu.make_async_copy(pore_hbm, poreb, in_sem.at[2]),
        pltpu.make_async_copy(rhs_hbm, rhs, in_sem.at[3]),
        pltpu.make_async_copy(facies_hbm, facies, in_sem.at[4]),
        pltpu.make_async_copy(mtab_hbm, mtab, in_sem.at[5]),
        pltpu.make_async_copy(ktab_hbm, ktab, in_sem.at[6]),
    ]
    for i in (4, 6, 5, 0, 1, 2, 3):
        loads[i].start()

    def zero(ref):
        ref[...] = jnp.zeros(ref.shape, ref.dtype)

    for cond, refs in (
        (iz == 0, [u.at[:, 0, own]]),
        (iz == ngz - 1, [u.at[:, nz + 1, own]]),
        (iy == 0, [yrecv.at[:, 0], cyrecv.at[0]]),
        (iy == ngy - 1, [yrecv.at[:, 1], cyrecv.at[1]]),
        (ix == 0, [xrecv.at[:, 0], cxrecv.at[0]]),
        (ix == ngx - 1, [xrecv.at[:, 1], cxrecv.at[1]]),
        (jnp.logical_or(iy == 0, ix == 0), [cdrecv.at[0]]),
        (jnp.logical_or(iy == 0, ix == ngx - 1), [cdrecv.at[1]]),
        (jnp.logical_or(iy == ngy - 1, ix == 0), [cdrecv.at[2]]),
        (jnp.logical_or(iy == ngy - 1, ix == ngx - 1), [cdrecv.at[3]]),
    ):
        @pl.when(cond)
        def _(refs=refs):
            for ref in refs:
                zero(ref)
    zero(field)
    for z in range(nz):
        zero(pcb.at[z, HALO + ny:])
        zero(ty.at[z, 0:HALO])
        for k in range(3):
            zero(u.at[k, z + 1, 0:HALO])
            zero(u.at[k, z + 1, HALO + ny:])
    zero(shifted.at[:, 0:HALO])

    for i in (4, 6, 5):
        loads[i].wait()

    def coefficient(table, z, r, c):
        return table[r, facies[z], c]

    lane8 = lax.broadcasted_iota(jnp.int32, (HALO, nx), 1)
    row8 = lax.broadcasted_iota(jnp.int32, (HALO, nx), 0)
    pair8 = lax.shift_right_logical(lane8, 1)
    even8 = lax.rem(lane8, 2) == 0
    first8, last8 = lane8 == 0, lane8 == nx - 1
    nil8 = jnp.zeros((HALO, nx), f32)
    group8 = lax.shift_right_logical(lane8, 4)
    in16 = lax.rem(lane8, 2 * HALO)
    left_part = in16 < HALO

    def packed_columns(values):
        out = [nil8] * xtiles
        for z, g, x in values:
            place = (g % per) * nz + z
            out[g // per] = jnp.where(pair8 == place, pltpu.roll(x, 2 * place + 1, 1), out[g // per])
        return out

    def swapped(x):
        return jnp.where(even8, pltpu.roll(x, nx - 1, 1), pltpu.roll(x, 1, 1))

    loads[0].wait()
    values = []
    for z in range(nz):
        r = 0.5 / permb[z].astype(f32)
        u[3, z + 1, own, :] = r
        for side, at_row in ((0, 0), (1, ny - 1)):
            ysend[0, side, nz + z:nz + z + 1, :] = r[at_row:at_row + 1]
        values += [(z, g, r[g * HALO:(g + 1) * HALO]) for g in range(groups)]
    packed = packed_columns(values)
    for t in range(xtiles):
        xsend[0, 1, t] = packed[t]

    loads[1].wait()
    values = []
    for z in range(nz):
        k0 = [coefficient(ktab, z, 0, k) for k in range(3)]
        pc = k0[0] * u[0, z + 1, own, :] + k0[1] * u[1, z + 1, own, :] + k0[2] * u[2, z + 1, own, :]
        pcb[z, own, :] = pc
        for side, at_row in ((0, 0), (1, ny - 1)):
            ysend[0, side, z:z + 1, :] = pc[at_row:at_row + 1]
        values += [(z, g, pc[g * HALO:(g + 1) * HALO]) for g in range(groups)]
    packed = packed_columns(values)
    for t in range(xtiles):
        xsend[0, 0, t] = packed[t]

    beside_y = exists(-1, 0).astype(jnp.int32) + exists(1, 0).astype(jnp.int32)
    beside_x = exists(0, -1).astype(jnp.int32) + exists(0, 1).astype(jnp.int32)
    pl.semaphore_wait(barrier, beside_y + beside_x + (ngz - 1))

    def remote(src, dst, send, recv, device):
        return pltpu.make_async_remote_copy(src_ref=src, dst_ref=dst, send_sem=send, recv_sem=recv,
                                            device_id=device, device_id_type=MESH)

    def start(copies):
        for sends, copy in copies:
            @pl.when(sends)
            def _(copy=copy):
                copy.start()

    def y_copies(batch):
        s = send_y, h_recv.at[1 + batch]
        return [(exists(1, 0), remote(ysend.at[batch, 1], yrecv.at[batch, 0], *s, at(1, 0))),
                (exists(-1, 0), remote(ysend.at[batch, 0], yrecv.at[batch, 1], *s, at(-1, 0)))]

    def x_copies(batch):
        s = send_x, h_recv.at[3 + batch]
        return [(exists(0, 1), remote(xsend.at[batch], xrecv.at[batch, 0], *s, at(0, 1))),
                (exists(0, -1), remote(xsend.at[batch], xrecv.at[batch, 1], *s, at(0, -1)))]

    def z_device(d):
        return {"gx": ix, "gy": iy, "gz": iz + d}

    z_up = remote(u.at[:, nz, own], u.at[:, 0, own], send_z, h_recv.at[0], z_device(1))
    z_down = remote(u.at[:, 1, own], u.at[:, nz + 1, own], send_z, h_recv.at[0], z_device(-1))
    has_below, has_above = iz > 0, iz < ngz - 1

    for n, dy, dx in ((1, -1, 0), (0, 1, 0), (2, 0, 1)):
        @pl.when(exists(dy, dx))
        def _(n=n, dy=dy, dx=dx):
            pl.semaphore_signal(near.at[n], inc=1, device_id=at(dy, dx), device_id_type=MESH)
    start(y_copies(0))
    start(x_copies(0))
    start([(has_above, z_up), (has_below, z_down)])

    def around(tiles, per_part):
        cases = []
        for cy in range(3):
            for cx in range(3):
                n = tiles(cy, cx)
                if n:
                    cases.append((3 * cy + cx, zplanes.at[:, 0:n] if per_part else zplanes.at[0, 0:n]))
        return cases

    def counted(count, cases, descriptor, done):
        for n, ref in cases:
            @pl.when(count == n)
            def _(ref=ref):
                done(descriptor(ref))

    def wait_many(count, cases, send, recv, sent):
        counted(count, cases, lambda ref: remote(ref, ref, send, recv, z_device(0)),
                (lambda c: c.wait_send()) if sent else (lambda c: c.wait_recv()))

    def wait_y(batch):
        wait_many(beside_y, ((1, yrecv.at[batch, 0]), (2, yrecv.at[batch])), send_y, h_recv.at[1 + batch], False)

    def wait_x(batch):
        wait_many(beside_x, ((1, xrecv.at[batch, 0]), (2, xrecv.at[batch])), send_x, h_recv.at[3 + batch], False)

    beside_z = has_below.astype(jnp.int32) + has_above.astype(jnp.int32)
    z_cases = ((1, u.at[:, 1, own]), (2, u.at[:, 1:3, own]))

    for i in range(2):
        values = []
        for z in range(nz):
            c = u[1 + i, z + 1, own, :]
            for side, at_row in ((0, 0), (1, ny - 1)):
                ysend[1, side, i * nz + z:i * nz + z + 1, :] = c[at_row:at_row + 1]
            values += [(z, g, c[g * HALO:(g + 1) * HALO]) for g in range(groups)]
        packed = packed_columns(values)
        for t in range(xtiles):
            xsend[1, i, t] = packed[t]
    start(x_copies(1))
    start(y_copies(1))
    raw_group8 = group8 - raw_lane // (2 * HALO)

    def lanes_of(g):
        return (g % per) * 2 * nz

    for i in range(2):
        here, swap = nil8, nil8
        for side in range(2):
            for k in range(layers):
                rows = slice(i * nz + k * HALO, i * nz + (k + 1) * HALO)
                for other in range(2):
                    slot = (side if not other else 1 - side) * layers + k
                    moved = pltpu.roll(ysend[0, side, rows, :], (raw_lane + 2 * HALO * slot + HALO) % nx, 1)
                    if other:
                        swap = jnp.where(raw_group8 == slot, moved, swap)
                    else:
                        here = jnp.where(raw_group8 == slot, moved, here)
        rpsend[i] = here
        for side, g in ends:
            column = xsend[0, i, g // per]
            if lanes_of(g):
                column = pltpu.roll(column, nx - lanes_of(g), 1)
            dsend[side, i] = jnp.where(lane8 < 2 * nz, column, swap)

    def ways(dy, dx, copy):
        @pl.when(exists(dy, dx))
        def _():
            copy.start()

    for dx in (-1, 1):
        ways(0, dx, remote(rpsend, cxrecv.at[(1 - dx) // 2, ngz * nstrips:], send_cx, h_recv.at[5], at(0, dx)))

    def known(n, dy, dx):
        @pl.when(exists(dy, dx))
        def _():
            pl.semaphore_wait(near.at[n], 1)

    def raw_corner(dy, dx):
        ways(dy, dx, remote(dsend.at[(1 + dy) // 2], cdrecv.at[(1 - dy) + (1 - dx) // 2, ngz:], send_cd, h_recv.at[5], at(dy, dx)))


    layer_of_lane = lax.rem(lane8[0:1], 2 * nz) // 2
    lanek = [jnp.zeros((1, nx), f32) for _ in range(3)]
    for z in range(nz):
        for k in range(3):
            value = coefficient(ktab, z, 0, k)
            rowk[k, z:z + 1, :] = jnp.full((1, nx), value, f32)
            lanek[k] = jnp.where(layer_of_lane == z, value, lanek[k])
    loads[2].wait()
    loads[3].wait()

    known(0, -1, 0)
    raw_corner(-1, -1)
    raw_corner(-1, 1)
    signal_peers(far.at[0])
    for side in range(2):
        for i in range(2):
            swsend[side, i] = swapped(dsend[side, i])
    for dy in (-1, 1):
        ways(dy, 0, remote(swsend.at[(1 + dy) // 2], cyrecv.at[(1 - dy) // 2, ngz * PLANES:], send_cy, h_recv.at[5], at(dy, 0)))

    def tile_of(g):
        return slice(g * HALO, (g + 1) * HALO)

    def padded(g, shift):
        return slice(HALO + g * HALO + shift, HALO + (g + 1) * HALO + shift)

    def assemble(g):
        rows, tile = padded(g, 0), tile_of(g)
        res, dia, s_y, s_x, h_x, h_y, h_z = (nil8,) * 7
        for z in range(nz):
            v = poreb[z].astype(f32)[tile]
            k00 = coefficient(ktab, z, 0, 0)
            m0 = [coefficient(mtab, z, 0, k) for k in range(3)]
            r = u[3, z + 1, rows, :]
            typ = 1.0 / (r + u[3, z + 1, padded(g, 1), :])
            if g == groups - 1:
                typ = jnp.where(row8 < HALO - 1, typ, 0.0)
            xp = jnp.where(last8, 0.0, 1.0 / (r + pltpu.roll(r, nx - 1, 1)))
            ty[z, rows, :] = typ
            txp[z, tile, :] = xp
            pc = pcb[z, rows, :]
            h_x = h_x + xp * (pc - pltpu.roll(pc, nx - 1, 1))
            h_y = h_y + typ * (pc - pcb[z, padded(g, 1), :])
            c = [u[k, z + 1, rows, :] for k in range(3)]
            res = res + (rhs[0, z, tile, :] - v * (m0[0] * c[0] + m0[1] * c[1] + m0[2] * c[2]))
            dia = dia + v * m0[0]
            s_y = s_y + k00 * typ
            s_x = s_x + k00 * xp
            if z < nz - 1:
                dk = [coefficient(ktab, z, 0, k) - coefficient(ktab, z + 1, 0, k) for k in range(3)]
                t = 1.0 / (r + u[3, z + 2, rows, :])
                tzf[z + 1, tile, :] = t
                d = [c[k] - u[k, z + 2, rows, :] for k in range(3)]
                h_z = h_z + t * (dk[0] * d[0] + dk[1] * d[1] + dk[2] * d[2])
        return res, dia, s_y, s_x, h_x, h_y, h_z

    s_res, s_dia, s_ty, s_tx, s_hx, s_hy, s_z = (list(c) for c in zip(*(assemble(g) for g in range(groups))))

    for g in range(groups):
        shifted[0, padded(g, 0), :] = s_hy[g]
        shifted[1, padded(g, 0), :] = s_ty[g]
    p_rhs, p_dia = [], []
    for g in range(groups):
        p_rhs.append(s_res[g] - s_z[g] - (s_hx[g] - pltpu.roll(s_hx[g], 1, 1)) - (s_hy[g] - shifted[0, padded(g, -1), :]))
        p_dia.append(s_dia[g] + s_ty[g] + shifted[1, padded(g, -1), :] + s_tx[g] + pltpu.roll(s_tx[g], 1, 1))

    wait_many(beside_z, z_cases, send_z, h_recv.at[0], False)
    for slot, z, inside in ((0, 0, 1), (nz + 1, nz - 1, nz)):
        k0 = [coefficient(ktab, z, 0, k) for k in range(3)]
        for g in range(groups):
            rows = padded(g, 0)
            there = u[3, slot, rows, :]
            t = jnp.where(there > 0.0, 1.0 / (u[3, inside, rows, :] + there), 0.0)
            tzf[0 if slot == 0 else nz, tile_of(g), :] = t
            d = [u[k, inside, rows, :] - u[k, slot, rows, :] for k in range(3)]
            p_rhs[g] = p_rhs[g] - t * (k0[0] * d[0] + k0[1] * d[1] + k0[2] * d[2])
    mine = [[swapped(xsend[0, i, t]) for t in range(xtiles)] for i in range(2)]

    planes = [p_rhs, p_dia, s_ty, s_tx]
    for p in range(PLANES):
        ystrips[0, p] = planes[p][0]
        ystrips[1, p] = planes[p][groups - 1]
    for i, tiles in enumerate(packing):
        strip = nil8
        for j, g in enumerate(tiles):
            for p in range(PLANES):
                slot = j * PLANES + p
                strip = jnp.where(group8 == slot, pltpu.roll(planes[p][g], (2 * HALO * slot + HALO) % nx, 1), strip)
        strips[i] = strip

    def to_all(dy, dx, src, dst, send, recv, parts=range(ngz)):
        return [(exists(dy, dx), remote(src, dst, send, c_recv.at[recv],
                                        {"gx": ix + dx, "gy": iy + dy, "gz": lax.rem(iz + d, ngz)})) for d in parts]

    def corner_strips(dy, dx, parts):
        start(to_all(dy, dx, strips.at[0 if dy < 0 else last_head], cdrecv.at[(1 - dy) + (1 - dx) // 2, iz], send_cd, 1, parts))

    pl.semaphore_wait(far.at[0], ngz - 1)
    corner_strips(-1, -1, range(ngz))
    corner_strips(-1, 1, range(ngz))
    known(2, 0, -1)
    raw_corner(1, -1)
    corner_strips(1, -1, range(1))
    for dx in (-1, 1):
        start(to_all(0, dx, strips, cxrecv.at[(1 - dx) // 2, pl.ds(iz * nstrips, nstrips)], send_cx, 1))
    for dy in (-1, 1):
        start(to_all(dy, 0, ystrips.at[(1 + dy) // 2], cyrecv.at[(1 - dy) // 2, pl.ds(iz * PLANES, PLANES)], send_cy, 1))

    for f in range(ktab.shape[1]):
        values = block_scalars([[mtab[r, f, c] for c in range(3)] for r in range(3)],
                               [[ktab[r, f, c] for c in range(3)] for r in range(3)])
        for i, value in enumerate(values):
            ctab[i, f] = value

    known(1, 1, 0)
    raw_corner(1, 1)
    signal_peers(far.at[1])
    corner_strips(1, 1, range(1))

    def inside(z, _):
        f = facies[z]
        kinv = [[ctab[KINV + 3 * r + c, f] for c in range(3)] for r in range(3)]
        for g in range(groups):
            rows = padded(g, 0)
            tile = tile_of(g)
            tzm, tzp = tzf[z, tile, :], tzf[z + 1, tile, :]
            typ, tym = ty[z, rows, :], ty[z, padded(g, -1), :]
            xp = txp[z, tile, :]
            xm = pltpu.roll(xp, 1, 1)
            tz = tzm + tzp
            tzs[z, tile, :] = tz
            txm[z, tile, :] = xm
            qv[0, z, tile, :] = tz + (typ + tym) + (xp + xm)
            given = [rhs[k, z, tile, :] for k in range(3)]
            for k in range(3):
                c = u[k, z + 1, rows, :]
                w[k, z, tile, :] = ((tzp * u[k, z + 2, rows, :] + tzm * u[k, z, rows, :])
                                    + (typ * u[k, z + 1, padded(g, 1), :] + tym * u[k, z + 1, padded(g, -1), :])
                                    + (xp * pltpu.roll(c, nx - 1, 1) + xm * pltpu.roll(c, 1, 1))
                                    + (kinv[k][0] * given[0] + kinv[k][1] * given[1] + kinv[k][2] * given[2]))
        return 0

    def layers_of(step, begin, end):
        for z in range(begin, end):
            step(z, 0)

    layers_of(inside, 0, nz // 2)
    pl.semaphore_wait(far.at[1], ngz - 1)
    corner_strips(1, -1, range(1, ngz))
    corner_strips(1, 1, range(1, ngz))
    layers_of(inside, nz // 2, nz)

    wait_y(0)
    top8, bottom8 = row8 == 0, row8 == HALO - 1
    lines = nil8
    y_faces = []
    for side, g, here in ((0, 0, top8), (1, groups - 1, bottom8)):
        there = yrecv[0, side, nz:, :]
        t = jnp.where(there > 0.0, 1.0 / (ysend[0, side, nz:, :] + there), 0.0)
        moved = jnp.sum(t * (ysend[0, side, :nz, :] - yrecv[0, side, :nz, :]), axis=0, keepdims=True)
        weight = jnp.sum(rowk[0] * t, axis=0, keepdims=True)
        lines = jnp.where(row8 == 2 * side, moved, jnp.where(row8 == 2 * side + 1, weight, lines))
        y_faces.append((side, g, here, t, moved, weight))
    wait_x(0)
    flux, weights, faces, outside = [], [], [], []
    for t in range(xtiles):
        there = [jnp.where(even8, xrecv[0, 0, i, t], xrecv[0, 1, i, t]) for i in range(2)]
        face = jnp.where(there[1] > 0.0, 1.0 / (mine[1][t] + there[1]), 0.0)
        flux.append(face * (mine[0][t] - there[0]))
        weights.append(face * lanek[0])
        faces.append(face)
        outside.append(there[0])

    def sums_of(flux, weights, low):
        block = jnp.logical_and(lane8 >= low, lane8 < low + 2 * nz)
        sums = []
        for values in (flux, weights):
            for parity in (even8, jnp.logical_not(even8)):
                sums.append(jnp.sum(jnp.where(jnp.logical_and(block, parity), values, 0.0), axis=1, keepdims=True))
        return sums

    def at_sides(left, right):
        return jnp.where(first8, left, jnp.where(last8, right, 0.0))

    for side, g, here, t, moved, weight in y_faces:
        for p, change in ((0, -moved), (1, weight), (2, weight))[:3 if side else 2]:
            planes[p][g] = planes[p][g] + jnp.where(here, change, 0.0)
        for z in range(nz):
            edge_row = HALO - 1 + side * ny
            ty[z, edge_row:edge_row + 1, :] = t[z:z + 1]
    zplanes[iz, PLANES * groups] = lines
    for i, tiles in enumerate(packing):
        across = nil8
        for j, g in enumerate(tiles):
            flux_l, flux_r, weight_l, weight_r = sums_of(flux[g // per], weights[g // per], lanes_of(g))
            for p, change in ((0, at_sides(-flux_l, -flux_r)), (1, at_sides(weight_l, weight_r)),
                              (3, jnp.where(last8, weight_r, 0.0))):
                planes[p][g] = planes[p][g] + change
            for p, left, right in ((0, flux_l, flux_r), (1, weight_l, weight_r), (3, weight_l, 0.0)):
                slot = (j * PLANES + p) * 2 * HALO
                across = jnp.where(lane8 == slot + HALO - 1, left, jnp.where(lane8 == slot + HALO, right, across))
        zplanes[iz, PLANES * groups + 1 + i] = across
    for p in range(PLANES):
        for g in range(groups):
            zplanes[iz, p * groups + g] = planes[p][g]
    for d in range(1, ngz):
        remote(zplanes.at[iz, 0:first_part], zplanes.at[iz, 0:first_part], send_cz, c_recv.at[0],
               {"gx": ix, "gy": iy, "gz": lax.rem(iz + d, ngz)}).start()

    wait_y(1)
    wait_x(1)
    invrow = 1.0 / rowk[0]
    for side, _, _, t, _, _ in y_faces:
        one, two_ = yrecv[1, side, :nz, :], yrecv[1, side, nz:, :]
        zero_ = (yrecv[0, side, :nz, :] - rowk[1] * one - rowk[2] * two_) * invrow
        for k, x in enumerate((zero_, one, two_)):
            yedge[side, k] = t * x
        yedge[side, 3] = t
    invlane = 1.0 / lanek[0]
    for t in range(xtiles):
        one, two_ = (jnp.where(even8, xrecv[1, 0, i, t], xrecv[1, 1, i, t]) for i in range(2))
        zero_ = (outside[t] - lanek[1] * one - lanek[2] * two_) * invlane
        for k, x in enumerate((zero_, one, two_)):
            edge[k, t] = swapped(faces[t] * x)
        edge[3, t] = swapped(faces[t])

    outer8 = jnp.logical_or(first8, last8)

    def solve(z, _):
        volume = poreb[z].astype(f32)
        f = facies[z]
        n = [[ctab[NMAT + 3 * r + c, f] for c in range(3)] for r in range(3)]
        adj = [[ctab[NADJ + 3 * r + c, f] for c in range(3)] for r in range(3)]
        dia = [ctab[NDIA + i, f] for i in range(3)]
        trace, minors, det_n = ctab[NTR, f], ctab[NC2, f], ctab[NDET, f]
        for g in range(groups):
            tile = tile_of(g)
            shift = (2 * nx - (lanes_of(g) + 1) - 2 * z) % nx
            added = [jnp.where(outer8, pltpu.roll(edge[k, g // per], shift, 1), 0.0) for k in range(4)]
            txp[z, tile, :] = txp[z, tile, :] + jnp.where(last8, added[3], 0.0)
            txm[z, tile, :] = txm[z, tile, :] + jnp.where(first8, added[3], 0.0)
            for side, head in ends:
                if g == head:
                    here = top8 if side == 0 else bottom8
                    added = [added[k] + jnp.where(here, yedge[side, k, z:z + 1, :], 0.0) for k in range(4)]
            b = [w[r, z, tile, :] + added[r] for r in range(3)]
            v = volume[tile]
            s = (qv[0, z, tile, :] + added[3]) * (1.0 / v)
            e = [[s * (s + dia[r]) + adj[r][r] if r == c else adj[r][c] - s * n[r][c] for c in range(3)] for r in range(3)]
            det = ((s + trace) * s + minors) * s + det_n
            inv = 1.0 / (v * det)
            for r in range(3):
                w[r, z, tile, :] = (e[r][0] * b[0] + e[r][1] * b[1] + e[r][2] * b[2]) * inv
                qv[r, z, tile, :] = e[r][0] * inv
        return 0

    most = nz * 5 // 8
    layers_of(solve, 0, most)

    corners = beside_y * beside_x
    place = 3 * beside_y + beside_x
    wait_many(place, around(lambda cy, cx: 2 * (cy + cx + cy * cx), False), send_cx, h_recv.at[5], False)
    from_top = raw_group8 < layers
    ours, theirs = [], []
    for i in range(2):
        ours.append(jnp.where(left_part, cxrecv[0, ngz * nstrips + i], cxrecv[1, ngz * nstrips + i]))
        theirs.append(jnp.where(from_top, jnp.where(left_part, cdrecv[0, ngz + i], cdrecv[1, ngz + i]),
                                jnp.where(left_part, cdrecv[2, ngz + i], cdrecv[3, ngz + i])))
    t = jnp.where(jnp.logical_and(raw_group8 >= 0, theirs[1] > 0.0), 1.0 / (ours[1] + theirs[1]), 0.0)
    pattern = nil8
    for k in range(layers):
        pattern = jnp.where(lax.rem(group8, layers) == (k + raw_lane // (2 * HALO)) % layers, rowk[0, k * HALO:(k + 1) * HALO, :], pattern)
    both = jnp.where(lax.rem(row8, 2) == 0, jnp.sum(t * (ours[0] - theirs[0]), axis=0, keepdims=True),
                     jnp.sum(t * pattern, axis=0, keepdims=True))

    def unpacked(side):
        total = None
        for k in range(layers):
            moved = pltpu.roll(both, (2 * nx - raw_lane - 2 * HALO * (side * layers + k) - HALO) % nx, 1)
            total = moved if total is None else total + moved
        return total

    zplanes[iz, first_part] = jnp.where(row8 < 2, unpacked(0), unpacked(1))
    for side, g in ends:
        tiles = [cyrecv[side, ngz * PLANES + i] for i in range(2)]
        there = [jnp.where(even8, cdrecv[2 * side, ngz + i], cdrecv[2 * side + 1, ngz + i]) for i in range(2)]
        face = jnp.where(there[1] > 0.0, 1.0 / (tiles[1] + there[1]), 0.0)
        flux_l, flux_r, weight_l, weight_r = sums_of(face * (tiles[0] - there[0]), face * lanek[0], 0)
        for n, tile in enumerate((at_sides(-flux_l, -flux_r), at_sides(weight_l, weight_r),
                                  at_sides(flux_r, flux_l), at_sides(weight_r, weight_l))):
            zplanes[iz, first_part + 1 + 4 * side + n] = tile
    for d in range(1, ngz):
        remote(zplanes.at[iz, first_part:], zplanes.at[iz, first_part:], send_cz, c_recv.at[2],
               {"gx": ix, "gy": iy, "gz": lax.rem(iz + d, ngz)}).start()
    layers_of(solve, most, nz)

    if ngz > 1:
        others = zplanes.at[0:ngz - 1, 0:first_part]
        remote(others, others, send_cz, c_recv.at[0], z_device(0)).wait_recv()
    wait_many(place, around(lambda cy, cx: PLANES * cy + nstrips * cx + cy * cx, True), send_cx, c_recv.at[1], False)

    def gathered(part):
        total = part(0)
        for i in range(1, ngz):
            total = total + part(i)
        return total

    tiles_in = groups + 2
    side_tiles = [jnp.where(left_part, gathered(lambda i: cxrecv[0, i * nstrips + t]), gathered(lambda i: cxrecv[1, i * nstrips + t]))
                  + gathered(lambda i: zplanes[i, PLANES * groups + 1 + t]) for t in range(nstrips)]
    corner_tiles = [jnp.where(left_part, gathered(lambda i: cdrecv[2 * v, i]), gathered(lambda i: cdrecv[2 * v + 1, i]))
                    for v in range(2)]
    where_is = {g: (i, j) for i, tiles in enumerate(packing) for j, g in enumerate(tiles)}
    on_right, on_left = lane8 < HALO, lane8 >= nx - HALO
    strip8 = jnp.logical_or(on_right, on_left)

    def border_of(p, g):
        if 0 <= g < groups:
            i, j = where_is[g]
            tile, slot = side_tiles[i], j * PLANES + p
        else:
            tile, slot = corner_tiles[0 if g < 0 else 1], p
        return jnp.where(strip8, pltpu.roll(tile, (2 * nx - 2 * HALO * slot - HALO) % nx, 1), 0.0)

    b = [[border_of(p, g) for g in range(-1, groups + 1)] for p in range(PLANES)]
    own_lines = gathered(lambda i: zplanes[i, PLANES * groups])
    a = [[gathered(lambda i: cyrecv[0, i * PLANES + p])] + [gathered(lambda i: zplanes[i, p * groups + g]) for g in range(groups)]
         + [gathered(lambda i: cyrecv[1, i * PLANES + p])] for p in range(PLANES)]

    def beyond(grid, lines):
        for side, t, here in ((0, 0, bottom8), (1, tiles_in - 1, top8)):
            moved, weight = lines[2 * side:2 * side + 1], lines[2 * side + 1:2 * side + 2]
            for p, change in ((0, moved), (1, weight), (2, weight))[:2 if side else 3]:
                grid[p][t] = grid[p][t] + jnp.where(here, change, 0.0)

    beyond(a, own_lines)

    def east(ra, rb):
        return jnp.where(last8, rb, ra), jnp.where(last8, ra, rb)

    def west(ra, rb):
        return jnp.where(first8, rb, ra), jnp.where(first8, ra, rb)

    def fill(buffer, s, tiles):
        for t in range(tiles_in):
            field[buffer, s, (t + 1) * HALO:(t + 2) * HALO, :] = tiles[t]

    def above(buffer, s, t):
        return field[buffer, s, (t + 1) * HALO - 1:(t + 2) * HALO - 1, :]

    def below(buffer, s, t):
        return field[buffer, s, (t + 1) * HALO + 1:(t + 2) * HALO + 1, :]

    terms = [[None] * tiles_in for _ in range(2)]
    grids = (a, b)

    def prepare(s, t):
        rhs_, dia, down, right = (grids[s][p][t] for p in range(PLANES))
        there = dia > 0.0
        inv = jnp.where(there, RELAX / jnp.where(there, dia, 1.0), 0.0)
        left = west(*(pltpu.roll(grid[3][t], 1, 1) for grid in grids))[s]
        terms[s][t] = [rhs_ * inv, down * inv, above(0, s, t) * inv, right * inv, left * inv]

    fill(0, 0, a[2])
    late_b = (0, 1, groups, groups + 1)
    for t in range(1, tiles_in - 1):
        prepare(0, t)

    if ngz > 1:
        rest = zplanes.at[0:ngz - 1, first_part:]
        remote(rest, rest, send_cz, c_recv.at[2], z_device(0)).wait_recv()
    lines = jnp.where(strip8, gathered(lambda i: zplanes[i, first_part]), 0.0)
    beyond(b, lines)
    for side, t, here in ((0, 1, top8), (1, groups, bottom8)):
        moved, weight = lines[2 * side:2 * side + 1], lines[2 * side + 1:2 * side + 2]
        for p, change in ((0, -moved), (1, weight), (2, weight))[:3 if side else 2]:
            b[p][t] = b[p][t] + jnp.where(here, change, 0.0)
    fill(0, 1, b[2])
    for t in range(1, tiles_in - 1):
        prepare(1, t)
    for side, t in ((0, 0), (1, tiles_in - 1)):
        flux_, weight_, flux_past, weight_past = (
            gathered(lambda i: zplanes[i, first_part + 1 + 4 * side + n]) for n in range(4))
        for grid, change, weight in ((a, flux_, weight_), (b, flux_past, weight_past)):
            grid[0][t] = grid[0][t] + change
            grid[1][t] = grid[1][t] + weight
            grid[3][t] = grid[3][t] + jnp.where(last8, weight, 0.0)
        for s in range(2):
            prepare(s, t)

    c = [[terms[s][t][0] for t in range(tiles_in)] for s in range(2)]
    for sweep in range(1, SWEEPS):
        buffer = sweep % 2
        for s in range(2):
            fill(buffer, s, c[s])
        nxt = [[None] * tiles_in for _ in range(2)]
        for t in range(tiles_in):
            e = east(*(pltpu.roll(c[s][t], nx - 1, 1) for s in range(2)))
            ws = west(*(pltpu.roll(c[s][t], 1, 1) for s in range(2)))
            for s in range(2):
                r, tyn, tys, txe, txw = terms[s][t]
                nxt[s][t] = (((1.0 - RELAX) * c[s][t] + r) + (tyn * below(buffer, s, t) + tys * above(buffer, s, t))
                             + (txe * e[s] + txw * ws[s]))
        c = nxt
    for t in range(tiles_in):
        rows = slice(t * HALO, (t + 1) * HALO)
        final[0, rows, :] = c[0][t]
        if 0 < t < tiles_in - 1:
            final[1, rows, :] = east(*(pltpu.roll(c[s][t], nx - 1, 1) for s in range(2)))[0]
            final[2, rows, :] = west(*(pltpu.roll(c[s][t], 1, 1) for s in range(2)))[0]
    for count, cases, sem in (
        (beside_y, ((1, yrecv.at[0]), (2, yrecv)), send_y),
        (beside_x, ((1, xrecv.at[0]), (2, xrecv)), send_x),
        (beside_z, z_cases, send_z),
        (beside_y, ((1, cyrecv.at[0]), (2, cyrecv)), send_cy),
        (beside_x, ((1, cxrecv.at[0]), (2, cxrecv)), send_cx),
        (corners, ((1, cdrecv.at[0]), (2, cdrecv.at[0:2]), (4, cdrecv)), send_cd),
    ):
        wait_many(count, cases, sem, h_recv.at[0], True)
    if ngz > 1:
        others = zplanes.at[0:ngz - 1]
        remote(others, others, send_cz, c_recv.at[0], z_device(0)).wait_send()


def finish_kernel(parts, w, qv, tzs, ty, txp, txm, final, new_hbm, corr_hbm, out, out_sem):
    nz, ny, nx = tzs.shape
    own = slice(HALO, HALO + ny)
    corr = pltpu.make_async_copy(final.at[0, own], corr_hbm, out_sem.at[parts])
    corr.start()
    cc, ce, cw = (final[k, own, :] for k in range(3))
    cn, cs = final[0, HALO + 1:HALO + 1 + ny, :], final[0, HALO - 1:HALO - 1 + ny, :]

    def finish(z, _):
        g = (tzs[z] * cc + ty[z, own, :] * cn + ty[z, HALO - 1:HALO + ny - 1, :] * cs
             + txp[z] * ce + txm[z] * cw)
        for r in range(3):
            out[r, z] = w[r, z] + qv[r, z] * g
        return 0

    step = nz // parts
    outs = [corr]
    for part in range(parts):
        lax.fori_loop(part * step, (part + 1) * step, finish, 0)
        chunk = slice(part * step, (part + 1) * step)
        outs.append(pltpu.make_async_copy(out.at[:, chunk], new_hbm.at[:, chunk], out_sem.at[part]))
        outs[-1].start()
    for copy in outs:
        copy.wait()


def per_device(sizes, state, right_side, permeability, pore_volume, facies, storage_table, coupling_table):
    _, nz, ny, nx = state.shape
    sizes = sizes + (nz, ny, nx)
    f32 = jnp.float32
    ngz = sizes[2]
    cells = (nz, ny, nx)
    vmem = lambda *shape: pltpu.VMEM(shape, f32)
    hbm = pl.BlockSpec(memory_space=pltpu.HBM)
    dma = lambda n: pltpu.SemaphoreType.DMA((n,))
    ey = ny + 2 * HALO
    groups, per, xtiles = column_plan(nz, ny, nx)
    strips = len(strip_plan(ny, nx))
    facets = storage_table.shape[0]
    in_vmem = pl.BlockSpec(memory_space=pltpu.VMEM)
    handed = 4 * nx * (9 * nz * ny + nz * ey + 3 * ey)
    limit = 16384 * ((VMEM_BYTES - handed) // 16384)
    middle = pl.pallas_call(
        functools.partial(kernel, sizes),
        out_shape=(vmem(3, *cells), vmem(3, *cells), vmem(*cells), vmem(nz, ey, nx), vmem(*cells), vmem(*cells),
                   vmem(3, ey, nx)),
        in_specs=[hbm, hbm, hbm, hbm, hbm, hbm, hbm],
        out_specs=(in_vmem,) * 7,
        scratch_shapes=[
            vmem(4, nz + 2, ey, nx), vmem(nz, ey, nx), vmem(3, *cells),
            pltpu.VMEM(cells, permeability.dtype), pltpu.VMEM(cells, pore_volume.dtype),
            vmem(2, 2, 2 * nz, nx), vmem(2, 2, 2 * nz, nx),
            vmem(2, 2, xtiles, HALO, nx), vmem(2, 2, 2, xtiles, HALO, nx), vmem(4, xtiles, HALO, nx),
            vmem(3, nz, nx), vmem(nz + 1, ny, nx), vmem(2, ey, nx),
            vmem(ngz, PLANES * groups + 1 + strips + 9, HALO, nx), vmem(2, PLANES, HALO, nx), vmem(strips, HALO, nx),
            vmem(2, ngz * PLANES + 2, HALO, nx), vmem(2, ngz * strips + 2, HALO, nx), vmem(4, ngz + 2, HALO, nx),
            vmem(2, HALO, nx), vmem(2, 2, HALO, nx), vmem(2, 2, HALO, nx), vmem(2, 4, nz, nx), vmem(2, 2, ey + 2 * HALO, nx),
            pltpu.SMEM((nz,), facies.dtype), pltpu.SMEM((3, facets, 3), f32), pltpu.SMEM((3, facets, 3), f32),
            pltpu.SMEM((NCOEF, facets), f32),
            pltpu.SemaphoreType.REGULAR((3,)), pltpu.SemaphoreType.REGULAR((2,)), dma(7), dma(6), dma(3),
        ],
        compiler_params=pltpu.CompilerParams(collective_id=0, has_side_effects=True, vmem_limit_bytes=limit),
        name="cpr_apply",
    )(facies, storage_table.transpose(1, 0, 2), coupling_table.transpose(1, 0, 2),
      state, right_side, permeability, pore_volume)
    parts = 8 if nz % 8 == 0 else 1
    return tuple(pl.pallas_call(
        functools.partial(finish_kernel, parts),
        out_shape=(jax.ShapeDtypeStruct(state.shape, f32), jax.ShapeDtypeStruct((ny, nx), f32)),
        in_specs=[in_vmem] * 7,
        out_specs=(hbm, hbm),
        scratch_shapes=[vmem(3, *cells), dma(parts + 1)],
        compiler_params=pltpu.CompilerParams(vmem_limit_bytes=16 * 2**20),
        name="cpr_finish",
    )(*middle))


def solution(mesh):
    sizes = (mesh.shape["gx"], mesh.shape["gy"], mesh.shape["gz"])
    return jax.shard_map(
        functools.partial(per_device, sizes),
        mesh=mesh,
        in_specs=(
            P(None, "gz", "gy", "gx"),
            P(None, "gz", "gy", "gx"),
            P("gz", "gy", "gx"),
            P("gz", "gy", "gx"),
            P("gz"),
            P(),
            P(),
        ),
        out_specs=(P(None, "gz", "gy", "gx"), P("gy", "gx")),
        check_vma=False,
    )
```

```python
import functools
import jax
import jax.numpy as jnp
from jax import lax
from jax.experimental import pallas as pl
from jax.experimental.pallas import tpu as pltpu
from jax.sharding import PartitionSpec as P

SWEEPS = 8
RELAX = 0.8
MESH = pl.DeviceIdType.MESH
HALO = 8
VMEM_BYTES = 67043328

PLANES = 4
SIDES = [(-1, 0), (1, 0), (0, -1), (0, 1), (-1, -1), (-1, 1), (1, -1), (1, 1)]

KINV, NMAT, NADJ, NDIA, NTR, NC2, NDET, NCOEF = 0, 9, 18, 27, 30, 31, 32, 33


def cofactor(e, r, c):
    return (e[(r + 1) % 3][(c + 1) % 3] * e[(r + 2) % 3][(c + 2) % 3]
            - e[(r + 1) % 3][(c + 2) % 3] * e[(r + 2) % 3][(c + 1) % 3])


def block_scalars(m, k):
    kf = [[cofactor(k, r, c) for c in range(3)] for r in range(3)]
    inv = 1.0 / (k[0][0] * kf[0][0] + k[0][1] * kf[0][1] + k[0][2] * kf[0][2])
    kinv = [[kf[c][r] * inv for c in range(3)] for r in range(3)]
    n = [[kinv[r][0] * m[0][c] + kinv[r][1] * m[1][c] + kinv[r][2] * m[2][c] for c in range(3)] for r in range(3)]
    nf = [[cofactor(n, r, c) for c in range(3)] for r in range(3)]
    trace = n[0][0] + n[1][1] + n[2][2]
    return ([kinv[r][c] for r in range(3) for c in range(3)] + [n[r][c] for r in range(3) for c in range(3)]
            + [nf[c][r] for r in range(3) for c in range(3)] + [trace - n[i][i] for i in range(3)]
            + [trace, nf[0][0] + nf[1][1] + nf[2][2], n[0][0] * nf[0][0] + n[0][1] * nf[0][1] + n[0][2] * nf[0][2]])


def column_plan(nz, ny, nx):
    groups = ny // HALO
    per = nx // (2 * nz)
    return groups, per, -(-groups // per)


def strip_plan(ny, nx):
    groups = ny // HALO
    per = nx // (2 * HALO * PLANES)
    heads = [0] if groups == 1 else [0, groups - 1]
    others = list(range(1, groups - 1))
    packed = [[head] + [others.pop(0) for _ in range(per - 1) if others] for head in heads]
    while others:
        packed.append([others.pop(0) for _ in range(per) if others])
    return packed


def kernel(sizes, facies_hbm, mtab_hbm, ktab_hbm, state_hbm, rhs_hbm, perm_hbm, pore_hbm,
           w, qv, tzs, ty, txp, txm, final,
           u, pcb, rhs, permb, poreb, ysend, yrecv, xsend, xrecv, edge, rowk, tzf, shifted,
           zplanes, ystrips, strips, cyrecv, cxrecv, cdrecv, rpsend, dsend, swsend, yedge, field,
           facies, mtab, ktab, ctab, near, far, in_sem, h_recv, c_recv):
    ngx, ngy, ngz, nz, ny, nx = sizes
    ix, iy, iz = lax.axis_index("gx"), lax.axis_index("gy"), lax.axis_index("gz")
    own = slice(HALO, HALO + ny)
    groups, per, xtiles = column_plan(nz, ny, nx)
    packing = strip_plan(ny, nx)
    nstrips = len(packing)
    last_head = len(packing[:2]) - 1
    layers = nz // HALO
    ends = ((0, 0), (1, groups - 1))
    first_part = PLANES * groups + 1 + nstrips
    raw_lane = nx - 4 * HALO * layers
    assert nz % HALO == 0 and raw_lane >= 2 * nz
    f32 = jnp.float32
    send_y, send_x, send_z, send_cy, send_cx, send_cd, send_cz = (in_sem.at[i] for i in (0, 1, 4, 5, 6, 2, 3))

    def exists(dy, dx):
        ok = None
        for d, i, n in ((dy, iy, ngy), (dx, ix, ngx)):
            if d:
                here = (i > 0) if d < 0 else (i < n - 1)
                ok = here if ok is None else jnp.logical_and(ok, here)
        return ok

    def at(dy, dx):
        return {"gx": ix + dx, "gy": iy + dy, "gz": iz}

    barrier = pltpu.get_barrier_semaphore()
    for side in (SIDES[0], SIDES[2], SIDES[1], SIDES[3]):
        @pl.when(exists(*side))
        def _(side=side):
            pl.semaphore_signal(barrier, inc=1, device_id=at(*side), device_id_type=MESH)

    def signal_peers(sem):
        for d in range(1, ngz):
            pl.semaphore_signal(sem, inc=1, device_id={"gx": ix, "gy": iy, "gz": lax.rem(iz + d, ngz)},
                                device_id_type=MESH)

    signal_peers(barrier)

    loads = [
        pltpu.make_async_copy(perm_hbm, permb, in_sem.at[0]),
        pltpu.make_async_copy(state_hbm, u.at[0:3, 1:nz + 1, own], in_sem.at[1]),
        pltpu.make_async_copy(pore_hbm, poreb, in_sem.at[2]),
        pltpu.make_async_copy(rhs_hbm, rhs, in_sem.at[3]),
        pltpu.make_async_copy(facies_hbm, facies, in_sem.at[4]),
        pltpu.make_async_copy(mtab_hbm, mtab, in_sem.at[5]),
        pltpu.make_async_copy(ktab_hbm, ktab, in_sem.at[6]),
    ]
    for i in (4, 6, 5, 0, 1, 2, 3):
        loads[i].start()

    def zero(ref):
        ref[...] = jnp.zeros(ref.shape, ref.dtype)

    for cond, refs in (
        (iz == 0, [u.at[:, 0, own]]),
        (iz == ngz - 1, [u.at[:, nz + 1, own]]),
        (iy == 0, [yrecv.at[:, 0], cyrecv.at[0]]),
        (iy == ngy - 1, [yrecv.at[:, 1], cyrecv.at[1]]),
        (ix == 0, [xrecv.at[:, 0], cxrecv.at[0]]),
        (ix == ngx - 1, [xrecv.at[:, 1], cxrecv.at[1]]),
        (jnp.logical_or(iy == 0, ix == 0), [cdrecv.at[0]]),
        (jnp.logical_or(iy == 0, ix == ngx - 1), [cdrecv.at[1]]),
        (jnp.logical_or(iy == ngy - 1, ix == 0), [cdrecv.at[2]]),
        (jnp.logical_or(iy == ngy - 1, ix == ngx - 1), [cdrecv.at[3]]),
    ):
        @pl.when(cond)
        def _(refs=refs):
            for ref in refs:
                zero(ref)
    zero(field)
    for z in range(nz):
        zero(pcb.at[z, HALO + ny:])
        zero(ty.at[z, 0:HALO])
        for k in range(3):
            zero(u.at[k, z + 1, 0:HALO])
            zero(u.at[k, z + 1, HALO + ny:])
    zero(shifted.at[:, 0:HALO])

    for i in (4, 6, 5):
        loads[i].wait()

    def coefficient(table, z, r, c):
        return table[r, facies[z], c]

    lane8 = lax.broadcasted_iota(jnp.int32, (HALO, nx), 1)
    row8 = lax.broadcasted_iota(jnp.int32, (HALO, nx), 0)
    pair8 = lax.shift_right_logical(lane8, 1)
    even8 = lax.rem(lane8, 2) == 0
    first8, last8 = lane8 == 0, lane8 == nx - 1
    nil8 = jnp.zeros((HALO, nx), f32)
    group8 = lax.shift_right_logical(lane8, 4)
    in16 = lax.rem(lane8, 2 * HALO)
    left_part = in16 < HALO

    def packed_columns(values):
        out = [nil8] * xtiles
        for z, g, x in values:
            place = (g % per) * nz + z
            out[g // per] = jnp.where(pair8 == place, pltpu.roll(x, 2 * place + 1, 1), out[g // per])
        return out

    def swapped(x):
        return jnp.where(even8, pltpu.roll(x, nx - 1, 1), pltpu.roll(x, 1, 1))

    loads[0].wait()
    values = []
    for z in range(nz):
        r = 0.5 / permb[z].astype(f32)
        u[3, z + 1, own, :] = r
        for side, at_row in ((0, 0), (1, ny - 1)):
            ysend[0, side, nz + z:nz + z + 1, :] = r[at_row:at_row + 1]
        values += [(z, g, r[g * HALO:(g + 1) * HALO]) for g in range(groups)]
    packed = packed_columns(values)
    for t in range(xtiles):
        xsend[0, 1, t] = packed[t]

    loads[1].wait()
    values = []
    for z in range(nz):
        k0 = [coefficient(ktab, z, 0, k) for k in range(3)]
        pc = k0[0] * u[0, z + 1, own, :] + k0[1] * u[1, z + 1, own, :] + k0[2] * u[2, z + 1, own, :]
        pcb[z, own, :] = pc
        for side, at_row in ((0, 0), (1, ny - 1)):
            ysend[0, side, z:z + 1, :] = pc[at_row:at_row + 1]
        values += [(z, g, pc[g * HALO:(g + 1) * HALO]) for g in range(groups)]
    packed = packed_columns(values)
    for t in range(xtiles):
        xsend[0, 0, t] = packed[t]

    beside_y = exists(-1, 0).astype(jnp.int32) + exists(1, 0).astype(jnp.int32)
    beside_x = exists(0, -1).astype(jnp.int32) + exists(0, 1).astype(jnp.int32)
    pl.semaphore_wait(barrier, beside_y + beside_x + (ngz - 1))

    def remote(src, dst, send, recv, device):
        return pltpu.make_async_remote_copy(src_ref=src, dst_ref=dst, send_sem=send, recv_sem=recv,
                                            device_id=device, device_id_type=MESH)

    def start(copies):
        for sends, copy in copies:
            @pl.when(sends)
            def _(copy=copy):
                copy.start()

    def y_copies(batch):
        s = send_y, h_recv.at[1 + batch]
        return [(exists(1, 0), remote(ysend.at[batch, 1], yrecv.at[batch, 0], *s, at(1, 0))),
                (exists(-1, 0), remote(ysend.at[batch, 0], yrecv.at[batch, 1], *s, at(-1, 0)))]

    def x_copies(batch):
        s = send_x, h_recv.at[3 + batch]
        return [(exists(0, 1), remote(xsend.at[batch], xrecv.at[batch, 0], *s, at(0, 1))),
                (exists(0, -1), remote(xsend.at[batch], xrecv.at[batch, 1], *s, at(0, -1)))]

    def z_device(d):
        return {"gx": ix, "gy": iy, "gz": iz + d}

    z_up = remote(u.at[:, nz, own], u.at[:, 0, own], send_z, h_recv.at[0], z_device(1))
    z_down = remote(u.at[:, 1, own], u.at[:, nz + 1, own], send_z, h_recv.at[0], z_device(-1))
    has_below, has_above = iz > 0, iz < ngz - 1

    for n, dy, dx in ((1, -1, 0), (0, 1, 0), (2, 0, 1)):
        @pl.when(exists(dy, dx))
        def _(n=n, dy=dy, dx=dx):
            pl.semaphore_signal(near.at[n], inc=1, device_id=at(dy, dx), device_id_type=MESH)
    start(y_copies(0))
    start(x_copies(0))
    start([(has_above, z_up), (has_below, z_down)])

    def around(tiles, per_part):
        cases = []
        for cy in range(3):
            for cx in range(3):
                n = tiles(cy, cx)
                if n:
                    cases.append((3 * cy + cx, zplanes.at[:, 0:n] if per_part else zplanes.at[0, 0:n]))
        return cases

    def counted(count, cases, descriptor, done):
        for n, ref in cases:
            @pl.when(count == n)
            def _(ref=ref):
                done(descriptor(ref))

    def wait_many(count, cases, send, recv, sent):
        counted(count, cases, lambda ref: remote(ref, ref, send, recv, z_device(0)),
                (lambda c: c.wait_send()) if sent else (lambda c: c.wait_recv()))

    def wait_y(batch):
        wait_many(beside_y, ((1, yrecv.at[batch, 0]), (2, yrecv.at[batch])), send_y, h_recv.at[1 + batch], False)

    def wait_x(batch):
        wait_many(beside_x, ((1, xrecv.at[batch, 0]), (2, xrecv.at[batch])), send_x, h_recv.at[3 + batch], False)

    beside_z = has_below.astype(jnp.int32) + has_above.astype(jnp.int32)
    z_cases = ((1, u.at[:, 1, own]), (2, u.at[:, 1:3, own]))

    for i in range(2):
        values = []
        for z in range(nz):
            c = u[1 + i, z + 1, own, :]
            for side, at_row in ((0, 0), (1, ny - 1)):
                ysend[1, side, i * nz + z:i * nz + z + 1, :] = c[at_row:at_row + 1]
            values += [(z, g, c[g * HALO:(g + 1) * HALO]) for g in range(groups)]
        packed = packed_columns(values)
        for t in range(xtiles):
            xsend[1, i, t] = packed[t]
    start(x_copies(1))
    start(y_copies(1))
    raw_group8 = group8 - raw_lane // (2 * HALO)

    def lanes_of(g):
        return (g % per) * 2 * nz

    for i in range(2):
        here, swap = nil8, nil8
        for side in range(2):
            for k in range(layers):
                rows = slice(i * nz + k * HALO, i * nz + (k + 1) * HALO)
                for other in range(2):
                    slot = (side if not other else 1 - side) * layers + k
                    moved = pltpu.roll(ysend[0, side, rows, :], (raw_lane + 2 * HALO * slot + HALO) % nx, 1)
                    if other:
                        swap = jnp.where(raw_group8 == slot, moved, swap)
                    else:
                        here = jnp.where(raw_group8 == slot, moved, here)
        rpsend[i] = here
        for side, g in ends:
            column = xsend[0, i, g // per]
            if lanes_of(g):
                column = pltpu.roll(column, nx - lanes_of(g), 1)
            dsend[side, i] = jnp.where(lane8 < 2 * nz, column, swap)

    def ways(dy, dx, copy):
        @pl.when(exists(dy, dx))
        def _():
            copy.start()

    for dx in (-1, 1):
        ways(0, dx, remote(rpsend, cxrecv.at[(1 - dx) // 2, ngz * nstrips:], send_cx, h_recv.at[5], at(0, dx)))

    def known(n, dy, dx):
        @pl.when(exists(dy, dx))
        def _():
            pl.semaphore_wait(near.at[n], 1)

    def raw_corner(dy, dx):
        ways(dy, dx, remote(dsend.at[(1 + dy) // 2], cdrecv.at[(1 - dy) + (1 - dx) // 2, ngz:], send_cd, h_recv.at[5], at(dy, dx)))


    layer_of_lane = lax.rem(lane8[0:1], 2 * nz) // 2
    lanek = [jnp.zeros((1, nx), f32) for _ in range(3)]
    for z in range(nz):
        for k in range(3):
            value = coefficient(ktab, z, 0, k)
            rowk[k, z:z + 1, :] = jnp.full((1, nx), value, f32)
            lanek[k] = jnp.where(layer_of_lane == z, value, lanek[k])
    loads[2].wait()
    loads[3].wait()

    for side in range(2):
        for i in range(2):
            swsend[side, i] = swapped(dsend[side, i])
    for dy in (-1, 1):
        ways(dy, 0, remote(swsend.at[(1 + dy) // 2], cyrecv.at[(1 - dy) // 2, ngz * PLANES:], send_cy, h_recv.at[5], at(dy, 0)))
    known(0, -1, 0)
    raw_corner(-1, -1)
    raw_corner(-1, 1)
    signal_peers(far.at[0])

    def tile_of(g):
        return slice(g * HALO, (g + 1) * HALO)

    def padded(g, shift):
        return slice(HALO + g * HALO + shift, HALO + (g + 1) * HALO + shift)

    def assemble(g):
        rows, tile = padded(g, 0), tile_of(g)
        res, dia, s_y, s_x, h_x, h_y, h_z = (nil8,) * 7
        for z in range(nz):
            v = poreb[z].astype(f32)[tile]
            k00 = coefficient(ktab, z, 0, 0)
            m0 = [coefficient(mtab, z, 0, k) for k in range(3)]
            r = u[3, z + 1, rows, :]
            typ = 1.0 / (r + u[3, z + 1, padded(g, 1), :])
            if g == groups - 1:
                typ = jnp.where(row8 < HALO - 1, typ, 0.0)
            xp = jnp.where(last8, 0.0, 1.0 / (r + pltpu.roll(r, nx - 1, 1)))
            ty[z, rows, :] = typ
            txp[z, tile, :] = xp
            pc = pcb[z, rows, :]
            h_x = h_x + xp * (pc - pltpu.roll(pc, nx - 1, 1))
            h_y = h_y + typ * (pc - pcb[z, padded(g, 1), :])
            c = [u[k, z + 1, rows, :] for k in range(3)]
            res = res + (rhs[0, z, tile, :] - v * (m0[0] * c[0] + m0[1] * c[1] + m0[2] * c[2]))
            dia = dia + v * m0[0]
            s_y = s_y + k00 * typ
            s_x = s_x + k00 * xp
            if z < nz - 1:
                dk = [coefficient(ktab, z, 0, k) - coefficient(ktab, z + 1, 0, k) for k in range(3)]
                t = 1.0 / (r + u[3, z + 2, rows, :])
                tzf[z + 1, tile, :] = t
                d = [c[k] - u[k, z + 2, rows, :] for k in range(3)]
                h_z = h_z + t * (dk[0] * d[0] + dk[1] * d[1] + dk[2] * d[2])
        return res, dia, s_y, s_x, h_x, h_y, h_z

    s_res, s_dia, s_ty, s_tx, s_hx, s_hy, s_z = (list(c) for c in zip(*(assemble(g) for g in range(groups))))

    for g in range(groups):
        shifted[0, padded(g, 0), :] = s_hy[g]
        shifted[1, padded(g, 0), :] = s_ty[g]
    p_rhs, p_dia = [], []
    for g in range(groups):
        p_rhs.append(s_res[g] - s_z[g] - (s_hx[g] - pltpu.roll(s_hx[g], 1, 1)) - (s_hy[g] - shifted[0, padded(g, -1), :]))
        p_dia.append(s_dia[g] + s_ty[g] + shifted[1, padded(g, -1), :] + s_tx[g] + pltpu.roll(s_tx[g], 1, 1))

    wait_many(beside_z, z_cases, send_z, h_recv.at[0], False)
    for slot, z, inside in ((0, 0, 1), (nz + 1, nz - 1, nz)):
        k0 = [coefficient(ktab, z, 0, k) for k in range(3)]
        for g in range(groups):
            rows = padded(g, 0)
            there = u[3, slot, rows, :]
            t = jnp.where(there > 0.0, 1.0 / (u[3, inside, rows, :] + there), 0.0)
            tzf[0 if slot == 0 else nz, tile_of(g), :] = t
            d = [u[k, inside, rows, :] - u[k, slot, rows, :] for k in range(3)]
            p_rhs[g] = p_rhs[g] - t * (k0[0] * d[0] + k0[1] * d[1] + k0[2] * d[2])
    mine = [[swapped(xsend[0, i, t]) for t in range(xtiles)] for i in range(2)]

    planes = [p_rhs, p_dia, s_ty, s_tx]
    for p in range(PLANES):
        ystrips[0, p] = planes[p][0]
        ystrips[1, p] = planes[p][groups - 1]
    for i, tiles in enumerate(packing):
        strip = nil8
        for j, g in enumerate(tiles):
            for p in range(PLANES):
                slot = j * PLANES + p
                strip = jnp.where(group8 == slot, pltpu.roll(planes[p][g], (2 * HALO * slot + HALO) % nx, 1), strip)
        strips[i] = strip

    def to_all(dy, dx, src, dst, send, recv, parts=range(ngz)):
        return [(exists(dy, dx), remote(src, dst, send, c_recv.at[recv],
                                        {"gx": ix + dx, "gy": iy + dy, "gz": lax.rem(iz + d, ngz)})) for d in parts]

    def corner_strips(dy, dx, parts):
        start(to_all(dy, dx, strips.at[0 if dy < 0 else last_head], cdrecv.at[(1 - dy) + (1 - dx) // 2, iz], send_cd, 1, parts))

    pl.semaphore_wait(far.at[0], ngz - 1)
    corner_strips(-1, -1, range(ngz))
    corner_strips(-1, 1, range(ngz))
    known(2, 0, -1)
    raw_corner(1, -1)
    corner_strips(1, -1, range(1))
    for dx in (-1, 1):
        start(to_all(0, dx, strips, cxrecv.at[(1 - dx) // 2, pl.ds(iz * nstrips, nstrips)], send_cx, 1))
    for dy in (-1, 1):
        start(to_all(dy, 0, ystrips.at[(1 + dy) // 2], cyrecv.at[(1 - dy) // 2, pl.ds(iz * PLANES, PLANES)], send_cy, 1))

    for f in range(ktab.shape[1]):
        values = block_scalars([[mtab[r, f, c] for c in range(3)] for r in range(3)],
                               [[ktab[r, f, c] for c in range(3)] for r in range(3)])
        for i, value in enumerate(values):
            ctab[i, f] = value

    known(1, 1, 0)
    raw_corner(1, 1)
    signal_peers(far.at[1])
    corner_strips(1, 1, range(1))

    def inside(z, _):
        f = facies[z]
        kinv = [[ctab[KINV + 3 * r + c, f] for c in range(3)] for r in range(3)]
        for g in range(groups):
            rows = padded(g, 0)
            tile = tile_of(g)
            tzm, tzp = tzf[z, tile, :], tzf[z + 1, tile, :]
            typ, tym = ty[z, rows, :], ty[z, padded(g, -1), :]
            xp = txp[z, tile, :]
            xm = pltpu.roll(xp, 1, 1)
            tz = tzm + tzp
            tzs[z, tile, :] = tz
            txm[z, tile, :] = xm
            qv[0, z, tile, :] = tz + (typ + tym) + (xp + xm)
            given = [rhs[k, z, tile, :] for k in range(3)]
            for k in range(3):
                c = u[k, z + 1, rows, :]
                w[k, z, tile, :] = ((tzp * u[k, z + 2, rows, :] + tzm * u[k, z, rows, :])
                                    + (typ * u[k, z + 1, padded(g, 1), :] + tym * u[k, z + 1, padded(g, -1), :])
                                    + (xp * pltpu.roll(c, nx - 1, 1) + xm * pltpu.roll(c, 1, 1))
                                    + (kinv[k][0] * given[0] + kinv[k][1] * given[1] + kinv[k][2] * given[2]))
        return 0

    def layers_of(step, begin, end):
        for z in range(begin, end):
            step(z, 0)

    layers_of(inside, 0, nz // 2)
    pl.semaphore_wait(far.at[1], ngz - 1)
    corner_strips(1, -1, range(1, ngz))
    corner_strips(1, 1, range(1, ngz))
    layers_of(inside, nz // 2, nz)

    wait_y(0)
    top8, bottom8 = row8 == 0, row8 == HALO - 1
    lines = nil8
    y_faces = []
    for side, g, here in ((0, 0, top8), (1, groups - 1, bottom8)):
        there = yrecv[0, side, nz:, :]
        t = jnp.where(there > 0.0, 1.0 / (ysend[0, side, nz:, :] + there), 0.0)
        moved = jnp.sum(t * (ysend[0, side, :nz, :] - yrecv[0, side, :nz, :]), axis=0, keepdims=True)
        weight = jnp.sum(rowk[0] * t, axis=0, keepdims=True)
        lines = jnp.where(row8 == 2 * side, moved, jnp.where(row8 == 2 * side + 1, weight, lines))
        y_faces.append((side, g, here, t, moved, weight))
    wait_x(0)
    flux, weights, faces, outside = [], [], [], []
    for t in range(xtiles):
        there = [jnp.where(even8, xrecv[0, 0, i, t], xrecv[0, 1, i, t]) for i in range(2)]
        face = jnp.where(there[1] > 0.0, 1.0 / (mine[1][t] + there[1]), 0.0)
        flux.append(face * (mine[0][t] - there[0]))
        weights.append(face * lanek[0])
        faces.append(face)
        outside.append(there[0])

    def sums_of(flux, weights, low):
        block = jnp.logical_and(lane8 >= low, lane8 < low + 2 * nz)
        sums = []
        for values in (flux, weights):
            for parity in (even8, jnp.logical_not(even8)):
                sums.append(jnp.sum(jnp.where(jnp.logical_and(block, parity), values, 0.0), axis=1, keepdims=True))
        return sums

    def at_sides(left, right):
        return jnp.where(first8, left, jnp.where(last8, right, 0.0))

    for side, g, here, t, moved, weight in y_faces:
        for p, change in ((0, -moved), (1, weight), (2, weight))[:3 if side else 2]:
            planes[p][g] = planes[p][g] + jnp.where(here, change, 0.0)
        for z in range(nz):
            edge_row = HALO - 1 + side * ny
            ty[z, edge_row:edge_row + 1, :] = t[z:z + 1]
    zplanes[iz, PLANES * groups] = lines
    for i, tiles in enumerate(packing):
        across = nil8
        for j, g in enumerate(tiles):
            flux_l, flux_r, weight_l, weight_r = sums_of(flux[g // per], weights[g // per], lanes_of(g))
            for p, change in ((0, at_sides(-flux_l, -flux_r)), (1, at_sides(weight_l, weight_r)),
                              (3, jnp.where(last8, weight_r, 0.0))):
                planes[p][g] = planes[p][g] + change
            for p, left, right in ((0, flux_l, flux_r), (1, weight_l, weight_r), (3, weight_l, 0.0)):
                slot = (j * PLANES + p) * 2 * HALO
                across = jnp.where(lane8 == slot + HALO - 1, left, jnp.where(lane8 == slot + HALO, right, across))
        zplanes[iz, PLANES * groups + 1 + i] = across
    for p in range(PLANES):
        for g in range(groups):
            zplanes[iz, p * groups + g] = planes[p][g]
    for d in range(1, ngz):
        remote(zplanes.at[iz, 0:first_part], zplanes.at[iz, 0:first_part], send_cz, c_recv.at[0],
               {"gx": ix, "gy": iy, "gz": lax.rem(iz + d, ngz)}).start()

    wait_y(1)
    wait_x(1)
    invrow = 1.0 / rowk[0]
    for side, _, _, t, _, _ in y_faces:
        one, two_ = yrecv[1, side, :nz, :], yrecv[1, side, nz:, :]
        zero_ = (yrecv[0, side, :nz, :] - rowk[1] * one - rowk[2] * two_) * invrow
        for k, x in enumerate((zero_, one, two_)):
            yedge[side, k] = t * x
        yedge[side, 3] = t
    invlane = 1.0 / lanek[0]
    for t in range(xtiles):
        one, two_ = (jnp.where(even8, xrecv[1, 0, i, t], xrecv[1, 1, i, t]) for i in range(2))
        zero_ = (outside[t] - lanek[1] * one - lanek[2] * two_) * invlane
        for k, x in enumerate((zero_, one, two_)):
            edge[k, t] = swapped(faces[t] * x)
        edge[3, t] = swapped(faces[t])

    outer8 = jnp.logical_or(first8, last8)

    def solve(z, _):
        volume = poreb[z].astype(f32)
        f = facies[z]
        n = [[ctab[NMAT + 3 * r + c, f] for c in range(3)] for r in range(3)]
        adj = [[ctab[NADJ + 3 * r + c, f] for c in range(3)] for r in range(3)]
        dia = [ctab[NDIA + i, f] for i in range(3)]
        trace, minors, det_n = ctab[NTR, f], ctab[NC2, f], ctab[NDET, f]
        for g in range(groups):
            tile = tile_of(g)
            shift = (2 * nx - (lanes_of(g) + 1) - 2 * z) % nx
            added = [jnp.where(outer8, pltpu.roll(edge[k, g // per], shift, 1), 0.0) for k in range(4)]
            txp[z, tile, :] = txp[z, tile, :] + jnp.where(last8, added[3], 0.0)
            txm[z, tile, :] = txm[z, tile, :] + jnp.where(first8, added[3], 0.0)
            for side, head in ends:
                if g == head:
                    here = top8 if side == 0 else bottom8
                    added = [added[k] + jnp.where(here, yedge[side, k, z:z + 1, :], 0.0) for k in range(4)]
            b = [w[r, z, tile, :] + added[r] for r in range(3)]
            v = volume[tile]
            s = (qv[0, z, tile, :] + added[3]) * (1.0 / v)
            e = [[s * (s + dia[r]) + adj[r][r] if r == c else adj[r][c] - s * n[r][c] for c in range(3)] for r in range(3)]
            det = ((s + trace) * s + minors) * s + det_n
            inv = 1.0 / (v * det)
            for r in range(3):
                w[r, z, tile, :] = (e[r][0] * b[0] + e[r][1] * b[1] + e[r][2] * b[2]) * inv
                qv[r, z, tile, :] = e[r][0] * inv
        return 0

    most = nz * 5 // 8
    layers_of(solve, 0, most)

    corners = beside_y * beside_x
    place = 3 * beside_y + beside_x
    wait_many(place, around(lambda cy, cx: 2 * (cy + cx + cy * cx), False), send_cx, h_recv.at[5], False)
    from_top = raw_group8 < layers
    ours, theirs = [], []
    for i in range(2):
        ours.append(jnp.where(left_part, cxrecv[0, ngz * nstrips + i], cxrecv[1, ngz * nstrips + i]))
        theirs.append(jnp.where(from_top, jnp.where(left_part, cdrecv[0, ngz + i], cdrecv[1, ngz + i]),
                                jnp.where(left_part, cdrecv[2, ngz + i], cdrecv[3, ngz + i])))
    t = jnp.where(jnp.logical_and(raw_group8 >= 0, theirs[1] > 0.0), 1.0 / (ours[1] + theirs[1]), 0.0)
    pattern = nil8
    for k in range(layers):
        pattern = jnp.where(lax.rem(group8, layers) == (k + raw_lane // (2 * HALO)) % layers, rowk[0, k * HALO:(k + 1) * HALO, :], pattern)
    both = jnp.where(lax.rem(row8, 2) == 0, jnp.sum(t * (ours[0] - theirs[0]), axis=0, keepdims=True),
                     jnp.sum(t * pattern, axis=0, keepdims=True))

    def unpacked(side):
        total = None
        for k in range(layers):
            moved = pltpu.roll(both, (2 * nx - raw_lane - 2 * HALO * (side * layers + k) - HALO) % nx, 1)
            total = moved if total is None else total + moved
        return total

    zplanes[iz, first_part] = jnp.where(row8 < 2, unpacked(0), unpacked(1))
    for side, g in ends:
        tiles = [cyrecv[side, ngz * PLANES + i] for i in range(2)]
        there = [jnp.where(even8, cdrecv[2 * side, ngz + i], cdrecv[2 * side + 1, ngz + i]) for i in range(2)]
        face = jnp.where(there[1] > 0.0, 1.0 / (tiles[1] + there[1]), 0.0)
        flux_l, flux_r, weight_l, weight_r = sums_of(face * (tiles[0] - there[0]), face * lanek[0], 0)
        for n, tile in enumerate((at_sides(-flux_l, -flux_r), at_sides(weight_l, weight_r),
                                  at_sides(flux_r, flux_l), at_sides(weight_r, weight_l))):
            zplanes[iz, first_part + 1 + 4 * side + n] = tile
    for d in range(1, ngz):
        remote(zplanes.at[iz, first_part:], zplanes.at[iz, first_part:], send_cz, c_recv.at[2],
               {"gx": ix, "gy": iy, "gz": lax.rem(iz + d, ngz)}).start()
    layers_of(solve, most, nz)

    if ngz > 1:
        others = zplanes.at[0:ngz - 1, 0:first_part]
        remote(others, others, send_cz, c_recv.at[0], z_device(0)).wait_recv()
    wait_many(place, around(lambda cy, cx: PLANES * cy + nstrips * cx + cy * cx, True), send_cx, c_recv.at[1], False)

    def gathered(part):
        total = part(0)
        for i in range(1, ngz):
            total = total + part(i)
        return total

    tiles_in = groups + 2
    side_tiles = [jnp.where(left_part, gathered(lambda i: cxrecv[0, i * nstrips + t]), gathered(lambda i: cxrecv[1, i * nstrips + t]))
                  + gathered(lambda i: zplanes[i, PLANES * groups + 1 + t]) for t in range(nstrips)]
    corner_tiles = [jnp.where(left_part, gathered(lambda i: cdrecv[2 * v, i]), gathered(lambda i: cdrecv[2 * v + 1, i]))
                    for v in range(2)]
    where_is = {g: (i, j) for i, tiles in enumerate(packing) for j, g in enumerate(tiles)}
    on_right, on_left = lane8 < HALO, lane8 >= nx - HALO
    strip8 = jnp.logical_or(on_right, on_left)

    def border_of(p, g):
        if 0 <= g < groups:
            i, j = where_is[g]
            tile, slot = side_tiles[i], j * PLANES + p
        else:
            tile, slot = corner_tiles[0 if g < 0 else 1], p
        return jnp.where(strip8, pltpu.roll(tile, (2 * nx - 2 * HALO * slot - HALO) % nx, 1), 0.0)

    b = [[border_of(p, g) for g in range(-1, groups + 1)] for p in range(PLANES)]
    own_lines = gathered(lambda i: zplanes[i, PLANES * groups])
    a = [[gathered(lambda i: cyrecv[0, i * PLANES + p])] + [gathered(lambda i: zplanes[i, p * groups + g]) for g in range(groups)]
         + [gathered(lambda i: cyrecv[1, i * PLANES + p])] for p in range(PLANES)]

    def beyond(grid, lines):
        for side, t, here in ((0, 0, bottom8), (1, tiles_in - 1, top8)):
            moved, weight = lines[2 * side:2 * side + 1], lines[2 * side + 1:2 * side + 2]
            for p, change in ((0, moved), (1, weight), (2, weight))[:2 if side else 3]:
                grid[p][t] = grid[p][t] + jnp.where(here, change, 0.0)

    beyond(a, own_lines)

    def east(ra, rb):
        return jnp.where(last8, rb, ra), jnp.where(last8, ra, rb)

    def west(ra, rb):
        return jnp.where(first8, rb, ra), jnp.where(first8, ra, rb)

    def fill(buffer, s, tiles):
        for t in range(tiles_in):
            field[buffer, s, (t + 1) * HALO:(t + 2) * HALO, :] = tiles[t]

    def above(buffer, s, t):
        return field[buffer, s, (t + 1) * HALO - 1:(t + 2) * HALO - 1, :]

    def below(buffer, s, t):
        return field[buffer, s, (t + 1) * HALO + 1:(t + 2) * HALO + 1, :]

    terms = [[None] * tiles_in for _ in range(2)]
    grids = (a, b)

    def prepare(s, t):
        rhs_, dia, down, right = (grids[s][p][t] for p in range(PLANES))
        there = dia > 0.0
        inv = jnp.where(there, RELAX / jnp.where(there, dia, 1.0), 0.0)
        left = west(*(pltpu.roll(grid[3][t], 1, 1) for grid in grids))[s]
        terms[s][t] = [rhs_ * inv, down * inv, above(0, s, t) * inv, right * inv, left * inv]

    fill(0, 0, a[2])
    late_b = (0, 1, groups, groups + 1)
    for t in range(1, tiles_in - 1):
        prepare(0, t)

    if ngz > 1:
        rest = zplanes.at[0:ngz - 1, first_part:]
        remote(rest, rest, send_cz, c_recv.at[2], z_device(0)).wait_recv()
    lines = jnp.where(strip8, gathered(lambda i: zplanes[i, first_part]), 0.0)
    beyond(b, lines)
    for side, t, here in ((0, 1, top8), (1, groups, bottom8)):
        moved, weight = lines[2 * side:2 * side + 1], lines[2 * side + 1:2 * side + 2]
        for p, change in ((0, -moved), (1, weight), (2, weight))[:3 if side else 2]:
            b[p][t] = b[p][t] + jnp.where(here, change, 0.0)
    fill(0, 1, b[2])
    for t in range(1, tiles_in - 1):
        prepare(1, t)
    for side, t in ((0, 0), (1, tiles_in - 1)):
        flux_, weight_, flux_past, weight_past = (
            gathered(lambda i: zplanes[i, first_part + 1 + 4 * side + n]) for n in range(4))
        for grid, change, weight in ((a, flux_, weight_), (b, flux_past, weight_past)):
            grid[0][t] = grid[0][t] + change
            grid[1][t] = grid[1][t] + weight
            grid[3][t] = grid[3][t] + jnp.where(last8, weight, 0.0)
        for s in range(2):
            prepare(s, t)

    c = [[terms[s][t][0] for t in range(tiles_in)] for s in range(2)]
    for sweep in range(1, SWEEPS):
        buffer = sweep % 2
        for s in range(2):
            fill(buffer, s, c[s])
        nxt = [[None] * tiles_in for _ in range(2)]
        for t in range(tiles_in):
            e = east(*(pltpu.roll(c[s][t], nx - 1, 1) for s in range(2)))
            ws = west(*(pltpu.roll(c[s][t], 1, 1) for s in range(2)))
            for s in range(2):
                r, tyn, tys, txe, txw = terms[s][t]
                nxt[s][t] = (((1.0 - RELAX) * c[s][t] + r) + (tyn * below(buffer, s, t) + tys * above(buffer, s, t))
                             + (txe * e[s] + txw * ws[s]))
        c = nxt
    for t in range(tiles_in):
        rows = slice(t * HALO, (t + 1) * HALO)
        final[0, rows, :] = c[0][t]
        if 0 < t < tiles_in - 1:
            final[1, rows, :] = east(*(pltpu.roll(c[s][t], nx - 1, 1) for s in range(2)))[0]
            final[2, rows, :] = west(*(pltpu.roll(c[s][t], 1, 1) for s in range(2)))[0]
    for count, cases, sem in (
        (beside_y, ((1, yrecv.at[0]), (2, yrecv)), send_y),
        (beside_x, ((1, xrecv.at[0]), (2, xrecv)), send_x),
        (beside_z, z_cases, send_z),
        (beside_y, ((1, cyrecv.at[0]), (2, cyrecv)), send_cy),
        (beside_x, ((1, cxrecv.at[0]), (2, cxrecv)), send_cx),
        (corners, ((1, cdrecv.at[0]), (2, cdrecv.at[0:2]), (4, cdrecv)), send_cd),
    ):
        wait_many(count, cases, sem, h_recv.at[0], True)
    if ngz > 1:
        others = zplanes.at[0:ngz - 1]
        remote(others, others, send_cz, c_recv.at[0], z_device(0)).wait_send()


def finish_kernel(parts, w, qv, tzs, ty, txp, txm, final, new_hbm, corr_hbm, out, out_sem):
    nz, ny, nx = tzs.shape
    own = slice(HALO, HALO + ny)
    corr = pltpu.make_async_copy(final.at[0, own], corr_hbm, out_sem.at[parts])
    corr.start()
    cc, ce, cw = (final[k, own, :] for k in range(3))
    cn, cs = final[0, HALO + 1:HALO + 1 + ny, :], final[0, HALO - 1:HALO - 1 + ny, :]

    def finish(z, _):
        g = (tzs[z] * cc + ty[z, own, :] * cn + ty[z, HALO - 1:HALO + ny - 1, :] * cs
             + txp[z] * ce + txm[z] * cw)
        for r in range(3):
            out[r, z] = w[r, z] + qv[r, z] * g
        return 0

    step = nz // parts
    outs = [corr]
    for part in range(parts):
        lax.fori_loop(part * step, (part + 1) * step, finish, 0)
        chunk = slice(part * step, (part + 1) * step)
        outs.append(pltpu.make_async_copy(out.at[:, chunk], new_hbm.at[:, chunk], out_sem.at[part]))
        outs[-1].start()
    for copy in outs:
        copy.wait()


def per_device(sizes, state, right_side, permeability, pore_volume, facies, storage_table, coupling_table):
    _, nz, ny, nx = state.shape
    sizes = sizes + (nz, ny, nx)
    f32 = jnp.float32
    ngz = sizes[2]
    cells = (nz, ny, nx)
    vmem = lambda *shape: pltpu.VMEM(shape, f32)
    hbm = pl.BlockSpec(memory_space=pltpu.HBM)
    dma = lambda n: pltpu.SemaphoreType.DMA((n,))
    ey = ny + 2 * HALO
    groups, per, xtiles = column_plan(nz, ny, nx)
    strips = len(strip_plan(ny, nx))
    facets = storage_table.shape[0]
    in_vmem = pl.BlockSpec(memory_space=pltpu.VMEM)
    handed = 4 * nx * (9 * nz * ny + nz * ey + 3 * ey)
    limit = 16384 * ((VMEM_BYTES - handed) // 16384)
    middle = pl.pallas_call(
        functools.partial(kernel, sizes),
        out_shape=(vmem(3, *cells), vmem(3, *cells), vmem(*cells), vmem(nz, ey, nx), vmem(*cells), vmem(*cells),
                   vmem(3, ey, nx)),
        in_specs=[hbm, hbm, hbm, hbm, hbm, hbm, hbm],
        out_specs=(in_vmem,) * 7,
        scratch_shapes=[
            vmem(4, nz + 2, ey, nx), vmem(nz, ey, nx), vmem(3, *cells),
            pltpu.VMEM(cells, permeability.dtype), pltpu.VMEM(cells, pore_volume.dtype),
            vmem(2, 2, 2 * nz, nx), vmem(2, 2, 2 * nz, nx),
            vmem(2, 2, xtiles, HALO, nx), vmem(2, 2, 2, xtiles, HALO, nx), vmem(4, xtiles, HALO, nx),
            vmem(3, nz, nx), vmem(nz + 1, ny, nx), vmem(2, ey, nx),
            vmem(ngz, PLANES * groups + 1 + strips + 9, HALO, nx), vmem(2, PLANES, HALO, nx), vmem(strips, HALO, nx),
            vmem(2, ngz * PLANES + 2, HALO, nx), vmem(2, ngz * strips + 2, HALO, nx), vmem(4, ngz + 2, HALO, nx),
            vmem(2, HALO, nx), vmem(2, 2, HALO, nx), vmem(2, 2, HALO, nx), vmem(2, 4, nz, nx), vmem(2, 2, ey + 2 * HALO, nx),
            pltpu.SMEM((nz,), facies.dtype), pltpu.SMEM((3, facets, 3), f32), pltpu.SMEM((3, facets, 3), f32),
            pltpu.SMEM((NCOEF, facets), f32),
            pltpu.SemaphoreType.REGULAR((3,)), pltpu.SemaphoreType.REGULAR((2,)), dma(7), dma(6), dma(3),
        ],
        compiler_params=pltpu.CompilerParams(collective_id=0, has_side_effects=True, vmem_limit_bytes=limit),
        name="cpr_apply",
    )(facies, storage_table.transpose(1, 0, 2), coupling_table.transpose(1, 0, 2),
      state, right_side, permeability, pore_volume)
    parts = 8 if nz % 8 == 0 else 1
    return tuple(pl.pallas_call(
        functools.partial(finish_kernel, parts),
        out_shape=(jax.ShapeDtypeStruct(state.shape, f32), jax.ShapeDtypeStruct((ny, nx), f32)),
        in_specs=[in_vmem] * 7,
        out_specs=(hbm, hbm),
        scratch_shapes=[vmem(3, *cells), dma(parts + 1)],
        compiler_params=pltpu.CompilerParams(vmem_limit_bytes=16 * 2**20),
        name="cpr_finish",
    )(*middle))


def solution(mesh):
    sizes = (mesh.shape["gx"], mesh.shape["gy"], mesh.shape["gz"])
    return jax.shard_map(
        functools.partial(per_device, sizes),
        mesh=mesh,
        in_specs=(
            P(None, "gz", "gy", "gx"),
            P(None, "gz", "gy", "gx"),
            P("gz", "gy", "gx"),
            P("gz", "gy", "gx"),
            P("gz"),
            P(),
            P(),
        ),
        out_specs=(P(None, "gz", "gy", "gx"), P("gy", "gx")),
        check_vma=False,
    )
```
